256 devices in a mesh: blk: 64 (over z, x, core), ch: 4 (over y).
Axes of the slice: x: 4, y: 4, z: 8, core: 2. Of those that a mesh axis runs over, the one named last changes fastest.
Arguments:
- features: bfloat16 [128, 65536], P('ch', 'blk'), may hold values from -6 to 6
- weight: bfloat16 [27, 128, 128], P(None, 'ch'), may hold values from -0.1875 to 0.1875
- grad_out: bfloat16 [128, 65536], P('ch', 'blk'), may hold values from -6 to 6
- rulebook: int32 [27, 65536], P(None, 'blk'), may hold values from 0 to 1280, as said below
Outputs:
- output: bfloat16 [128, 65536], P('ch', 'blk')
- grad_features: bfloat16 [128, 65536], P('ch', 'blk')
- weight_grad: float32 [27, 128, 128], P(None, 'ch')
The draws below stay inside these ranges and needn't reach their ends.
Inputs may be any that keep to these rules, and one draw needn't show every extreme that they name: `rulebook`: slots 0 to 127 of every block hold active voxels of its lowest layer, slots 128 to 255 active voxels of its highest layer, then come active inner voxels, then empty slots; at least 640 slots of a block are active and some block has all 1024. Offset k = 9 (dx + 1) + 3 (dy + 1) + (dz + 1), dz along the block order. An entry names the table column of the active neighbour at that offset, and the zero column 1280 for an inactive neighbour, one outside the image, and for every entry of an empty slot. If entry k of slot i names slot j, entry 26 - k of j names i.
All inputs are finite; a program needn't handle non-finite values.
Results may differ from the reference program's by a relative error of at most 0.001.
Values may be sent and summed in bfloat16 or wider, within the bound.
No kernel may reach another device: no remote copies, remote signals or barrier semaphores. Data moves between devices by JAX's collectives and lax.ppermute only.
A program may use at most 64 MiB of HBM per device.

```python
import math
import jax
import jax.numpy as jnp
from jax import lax

C = 128
VOX = 1024
FACE = 128
BLK_DEV = 1
NBLK = 64
SLOTS = 65536
N_BLK = 64


def block_layout(key):
    key_low, key_high, key_inner = jax.random.split(key, 3)
    lowest = jax.random.permutation(key_low, 256)[:FACE]
    highest = 3840 + jax.random.permutation(key_high, 256)[:FACE]
    interior = 256 + jax.random.permutation(key_inner, 3584)[:VOX - 2 * FACE]
    return jnp.concatenate([lowest, highest, interior]).astype(jnp.int32)


def draw_rulebook(key, part):
    nblocks = NBLK
    devices = NBLK // BLK_DEV
    block_keys = jax.random.split(jax.random.fold_in(key, 7), nblocks)
    positions = jax.vmap(block_layout)(block_keys)
    count_key, pick_key = jax.random.split(jax.random.fold_in(key, 11))
    counts = jax.random.randint(count_key, (nblocks,), 2 * FACE + (VOX - 2 * FACE) // 2, VOX + 1)
    full_block = jax.random.randint(pick_key, (), 0, nblocks)
    block_ids = jnp.arange(nblocks, dtype=jnp.int32)
    counts = jnp.where(block_ids == full_block, VOX, counts)
    slot_ids = jnp.arange(VOX, dtype=jnp.int32)
    active = slot_ids[None, :] < counts[:, None]
    lookup = jnp.full((nblocks, 4096), -1, jnp.int32)
    lookup = lookup.at[block_ids[:, None], positions].set(jnp.where(active, slot_ids[None, :], -1))
    cell_z = positions // 256
    cell_x = positions // 16 % 16
    cell_y = positions % 16
    local_rows = BLK_DEV * VOX
    zero_col = local_rows + 2 * BLK_DEV * FACE
    slot_place = (block_ids // devices)[:, None]
    lower_block = jnp.clip(block_ids - 1, 0, nblocks - 1)[:, None]
    upper_block = jnp.clip(block_ids + 1, 0, nblocks - 1)[:, None]
    entries = []
    for step_x in (-1, 0, 1):
        for step_y in (-1, 0, 1):
            for step_z in (-1, 0, 1):
                next_x = cell_x + step_x
                next_y = cell_y + step_y
                next_z = cell_z + step_z
                inside = (next_x >= 0) & (next_x < 16) & (next_y >= 0) & (next_y < 16)
                flat_cell = jnp.clip(next_x, 0, 15) * 16 + jnp.clip(next_y, 0, 15)
                same_slot = lookup[block_ids[:, None], jnp.clip(next_z, 0, 15) * 256 + flat_cell]
                lower_slot = lookup[lower_block, 3840 + flat_cell]
                upper_slot = lookup[upper_block, flat_cell]
                same_index = jnp.where(same_slot >= 0, slot_place * VOX + same_slot, zero_col)
                lower_index = jnp.where((lower_slot >= 0) & (block_ids[:, None] > 0), local_rows + slot_place * FACE + lower_slot - FACE, zero_col)
                upper_index = jnp.where((upper_slot >= 0) & (block_ids[:, None] < nblocks - 1), local_rows + BLK_DEV * FACE + slot_place * FACE + upper_slot, zero_col)
                chosen = jnp.where(next_z < 0, lower_index, jnp.where(next_z > 15, upper_index, same_index))
                entries.append(jnp.where(inside & active, chosen, zero_col))
    rulebook = jnp.stack(entries)
    rulebook = rulebook.reshape(27, BLK_DEV, devices, VOX).transpose(0, 2, 1, 3).reshape(27, nblocks * VOX)
    return rulebook.astype(jnp.int32)


def steps_of(own_key, extent, cuts, low, top_value):
    level, own = 1.0, jax.random.fold_in(own_key, 6)
    for dim, shards_of in cuts:
        steps = jnp.exp(jax.random.uniform(jax.random.fold_in(own, dim), (shards_of,), jnp.float32, low / len(cuts), top_value / len(cuts)))
        level = level * jnp.repeat(steps, extent[dim] // shards_of).reshape([-1 if axis == dim else 1 for axis in range(len(extent))])
    return level


def scatter_about(key, shape, spread, bound, pieces=(), held_as=jnp.bfloat16):
    array = jax.random.normal(key, shape, jnp.float32) * spread
    if len(pieces) > 0:
        array = steps_of(key, shape, pieces, -0.22, 0.18) * array
    return jnp.clip(array, min=-bound, max=bound).astype(held_as)


def setup_inputs(seed: int = 0) -> dict:
    streams_of = jax.random.split(jax.random.key(seed), 5)
    return {
        "features": scatter_about(streams_of[0], (C, SLOTS), 1.0, 6.0, ((0, 4), (1, 64))),
        "weight": scatter_about(streams_of[1], (27, C, C), (9 * C) ** -0.5, 0.1875, ((1, 4),)),
        "grad_out": scatter_about(streams_of[2], (C, SLOTS), 1.0, 6.0, ((0, 4), (1, 64))),
        "rulebook": draw_rulebook(jax.random.fold_in(streams_of[4], 71), 0),
    }


def by_block(source, devices):
    chan_count = source.shape[0]
    shaped = source.reshape(chan_count, devices, BLK_DEV, VOX).transpose(0, 2, 1, 3)
    return shaped.reshape(chan_count, devices * BLK_DEV, VOX)

def by_device(blocks, devices):
    chan_count, block_count, face_depth = blocks.shape
    shaped = blocks.reshape(chan_count, BLK_DEV, devices, face_depth).transpose(2, 0, 1, 3)
    return shaped.reshape(devices, chan_count, BLK_DEV * face_depth)

def tables(field):
    devices = N_BLK
    chan_count = field.shape[0]
    blocks = by_block(field, devices)
    highest = blocks[:, :, FACE:2 * FACE]
    lowest = blocks[:, :, :FACE]
    zeros = jnp.zeros_like(highest[:, :1])
    from_lower = jnp.concatenate([zeros, highest[:, :-1]], axis=1)
    from_upper = jnp.concatenate([lowest[:, 1:], zeros], axis=1)
    own_rows = field.reshape(chan_count, devices, BLK_DEV * VOX).transpose(1, 0, 2)
    zero_column = jnp.zeros((devices, chan_count, 1), field.dtype)
    return jnp.concatenate([own_rows, by_device(from_lower, devices), by_device(from_upper, devices), zero_column], axis=2)

def convolve(inputs, weights, rulebook):
    extended = tables(inputs)
    picks_all = rulebook.reshape(27, N_BLK, BLK_DEV * VOX).transpose(1, 0, 2)

    def one_device(device_pair):
        source, indices = device_pair
        running = jnp.zeros((weights.shape[2], indices.shape[1]), inputs.dtype)
        for offset in range(27):
            running = running + jnp.dot(weights[offset].T, source[:, indices[offset]], precision=lax.Precision.HIGHEST, preferred_element_type=jnp.float32)
        return running
    result = lax.map(one_device, (extended, picks_all))
    return result.transpose(1, 0, 2).reshape(weights.shape[2], -1)

def reference(features, weight, grad_out, rulebook):
    inputs32 = features.astype(jnp.float32)
    weights32 = weight.astype(jnp.float32)
    cotangent = grad_out.astype(jnp.float32)

    def forward(inputs, weights):
        return convolve(inputs, weights, rulebook)
    output, pullback = jax.vjp(forward, inputs32, weights32)
    grad_inputs, grad_weights = pullback(cotangent)
    norm_scale = 1.0 / math.sqrt(NBLK * VOX)
    return (output.astype(jnp.bfloat16), grad_inputs.astype(jnp.bfloat16), (grad_weights * norm_scale).astype(jnp.float32))
```

```python
import jax
import jax.numpy as jnp
from jax import lax
from jax.experimental import pallas as pl
from jax.experimental.pallas import tpu as pltpu
from jax.sharding import PartitionSpec as P

VOX = 1024
FACE = 128
LANES = 128
PART = 112
INNER = tuple(range(2, 8))
VMEM = pl.BlockSpec(memory_space=pltpu.VMEM)


def source_tiles(group, dz):
    if group == 0:
        return {-1: (8,), 0: (0,), 1: INNER}[dz]
    if group == 1:
        return {-1: INNER, 0: (1,), 1: (9,)}[dz]
    return {-1: (0,) + INNER, 0: INNER, 1: (1,) + INNER}[dz]


def picked(row, group, tiles, load):
    span = row[:, LANES * group : LANES * (group + 1)]
    index = jnp.broadcast_to(span, (32, LANES))
    lane = index & (LANES - 1)
    tile = index >> 7
    total = jnp.zeros((32, LANES), jnp.float32)
    for t in tiles:
        values = jnp.take_along_axis(load(t), lane, axis=1, mode="promise_in_bounds")
        total = jnp.where(tile == t, values, total)
    return total


def tile_span(t):
    return slice(LANES * t, LANES * (t + 1))


def gather_kernel(x_ref, rule_ref, dense_ref, table):
    table[...] = x_ref[...].astype(jnp.float32)

    def step(j, carry):
        for d in range(3):
            k = 3 * j + d
            row = rule_ref[pl.ds(k, 1), :]
            for group in range(8):
                tiles = source_tiles(group, d - 1)
                if tiles[0] >= 8:
                    continue
                got = picked(row, group, tiles, lambda t: table[:, tile_span(t)])
                rows = pl.ds(pl.multiple_of(32 * k, 32), 32)
                dense_ref[rows, tile_span(group)] = got.astype(jnp.bfloat16)
        return carry

    lax.fori_loop(0, 9, step, 0)


def weight_kernel(
    dense_in, rule_ref, lower_ref, upper_ref, g0, g1, g2, g3,
    dense_ref, grad_ref, low_ref, high_ref, keep_ref, send_ref, faces, terms,
):
    chan = lax.axis_index("ch")
    place = lax.axis_index("blk")
    for m, part in enumerate((g0, g1, g2, g3)):
        rows = pl.ds(pl.multiple_of(32 * (chan ^ m), 32), 32)
        grad_ref[rows, :] = part[...]
        low_ref[rows, :] = part[:, :FACE]
        high_ref[rows, :] = part[:, FACE : 2 * FACE]
    faces[:, :FACE] = lower_ref[...].astype(jnp.float32)
    faces[:, FACE:] = upper_ref[...].astype(jnp.float32)

    def step(j, carry):
        for group, d in ((0, 0), (1, 2)):
            k = 3 * j + d
            row = rule_ref[pl.ds(k, 1), :]
            got = picked(row, group, (8 + group,), lambda t: faces[:, tile_span(t - 8)])
            rows = pl.ds(pl.multiple_of(32 * k, 32), 32)
            dense_ref[rows, tile_span(group)] = got.astype(jnp.bfloat16)
        return carry

    lax.fori_loop(0, 9, step, 0)
    terms[:864, :] = lax.dot_general(
        dense_ref[...], grad_ref[...], (((1,), (1,)), ((), ())),
        preferred_element_type=jnp.float32,
    ) * (1.0 / 256.0)
    terms[864:, :] = jnp.zeros((32, LANES), jnp.float32)
    near = place & 7
    for q in range(4):
        for odd, target in ((0, keep_ref), (1, send_ref)):
            start = pl.multiple_of(PART * (near ^ (2 * q + odd)), 8)
            target[PART * q : PART * (q + 1), :] = terms[pl.ds(start, PART), :]


def forward_kernel(dense_ref, weight_ref, out_ref):
    out_ref[...] = lax.dot_general(
        weight_ref[...], dense_ref[...], (((0,), (0,)), ((), ())),
        preferred_element_type=jnp.float32,
    )


def back_kernel(grad_ref, lower_ref, upper_ref, weight_ref, rule_ref, out_ref, terms, total):
    weights = weight_ref[...]
    terms[:, :VOX] = jnp.dot(weights, grad_ref[...], preferred_element_type=jnp.float32)
    terms[:, VOX : VOX + FACE] = jnp.dot(
        weights, lower_ref[...], preferred_element_type=jnp.float32
    )
    terms[:, VOX + FACE :] = jnp.dot(
        weights, upper_ref[...], preferred_element_type=jnp.float32
    )
    total[...] = jnp.zeros_like(total)

    def step(j, carry):
        rules = [rule_ref[pl.ds(3 * j + d, 1), :] for d in range(3)]
        for group in range(8):
            running = total[:, tile_span(group)]
            for d in range(3):
                rows = pl.ds(pl.multiple_of(32 * (26 - 3 * j - d), 32), 32)
                running = running + picked(
                    rules[d], group, source_tiles(group, d - 1),
                    lambda t: terms[rows, tile_span(t)],
                )
            total[:, tile_span(group)] = running
        return carry

    lax.fori_loop(0, 9, step, 0)
    out_ref[...] = total[...].astype(jnp.bfloat16)


def split_sum_kernel(keep_ref, came_ref, *outs):
    for q, out in enumerate(outs):
        rows = slice(PART * q, PART * (q + 1))
        out[...] = keep_ref[rows, :] + came_ref[rows, :]


def sum_kernel(*refs):
    total = refs[0][...]
    for ref in refs[1:-1]:
        total = total + ref[...]
    refs[-1][...] = total


def join_kernel(*refs):
    for q, ref in enumerate(refs[:-1]):
        refs[-1][PART * q : PART * (q + 1), :] = ref[...]


def place_kernel(even_ref, odd_ref, out_ref, held):
    near = lax.axis_index("blk") & 7
    for q in range(4):
        rows = slice(PART * q, PART * (q + 1))
        held[2 * PART * q : 2 * PART * q + PART, :] = even_ref[rows, :]
        held[2 * PART * q + PART : 2 * PART * (q + 1), :] = odd_ref[rows, :]
    for p in range(8):
        count = min(PART, 864 - PART * p)
        start = pl.multiple_of(PART * (near ^ p), 8)
        out_ref[PART * p : PART * p + count, :] = held[pl.ds(start, count), :]


def call(kernel, outs, args, scratch=(), aliases=None, flops=0, name=None):
    moved = sum(a.size * a.dtype.itemsize for a in list(args) + jax.tree.leaves(outs))
    return pl.pallas_call(
        kernel,
        out_shape=outs,
        in_specs=[VMEM] * len(args),
        out_specs=jax.tree.map(lambda _: VMEM, outs),
        scratch_shapes=list(scratch),
        input_output_aliases=aliases or {},
        compiler_params=pltpu.CompilerParams(vmem_limit_bytes=40 << 20),
        cost_estimate=pl.CostEstimate(flops=flops, bytes_accessed=moved, transcendentals=0),
        name=name,
    )(*args)


def f32(*shape):
    return jax.ShapeDtypeStruct(shape, jnp.float32)


def bf16(*shape):
    return jax.ShapeDtypeStruct(shape, jnp.bfloat16)


def swap(value, mask):
    count = lax.axis_size("blk")
    return lax.ppermute(value, "blk", [(i, i ^ mask) for i in range(count)])


def shifted(value, steps):
    count = lax.axis_size("blk")
    return lax.ppermute(value, "blk", [(i, (i + steps) % count) for i in range(count)])


def per_device(features, weight, grad_out, rulebook):
    weights = weight.reshape(864, 128)
    from_lower = shifted(features[:, FACE : 2 * FACE], 1)
    from_upper = shifted(features[:, :FACE], -1)
    parts = [
        lax.ppermute(grad_out, "ch", [(i, i ^ m) for i in range(4)]) for m in (1, 2, 3)
    ]
    dense = call(
        gather_kernel, bf16(864, VOX), (features, rulebook),
        [pltpu.VMEM((32, VOX), jnp.float32)], flops=3 << 30, name="gather",
    )
    dense, grads, low, high, keep, send = call(
        weight_kernel,
        (bf16(864, VOX), bf16(128, VOX), bf16(128, FACE), bf16(128, FACE),
         f32(4 * PART, 128), f32(4 * PART, 128)),
        (dense, rulebook, from_lower, from_upper, grad_out, *parts),
        [pltpu.VMEM((32, 2 * FACE), jnp.float32), pltpu.VMEM((8 * PART, 128), jnp.float32)],
        aliases={0: 0}, flops=1 << 30, name="weight_terms",
    )
    came = swap(send, 1)
    partial = call(
        forward_kernel, f32(128, VOX), (dense, weights), flops=1 << 30, name="forward"
    )
    output = lax.psum_scatter(partial, "ch", scatter_dimension=0, tiled=True)
    pieces = call(split_sum_kernel, (f32(PART, 128),) * 4, (keep, came), name="sum_pair")
    others = [swap(pieces[q], 2 * q) for q in (1, 2, 3)]
    total = call(sum_kernel, f32(PART, 128), (pieces[0], *others), name="sum_four")
    for mask in (8, 16, 32):
        total = call(sum_kernel, f32(PART, 128), (total, swap(total, mask)), name="sum_two")
    even = call(
        join_kernel, f32(4 * PART, 128),
        (total, *[swap(total, 2 * q) for q in (1, 2, 3)]), name="join",
    )
    odd = swap(even, 1)
    weight_grad = call(
        place_kernel, f32(864, 128), (even, odd),
        [pltpu.VMEM((8 * PART, 128), jnp.float32)], name="place",
    )
    lower_grads = shifted(high, 1)
    upper_grads = shifted(low, -1)
    grad_features = call(
        back_kernel, bf16(32, VOX), (grads, lower_grads, upper_grads, weights, rulebook),
        [pltpu.VMEM((864, VOX + 2 * FACE), jnp.float32), pltpu.VMEM((32, VOX), jnp.float32)],
        flops=5 << 30, name="back",
    )
    return (
        output.astype(jnp.bfloat16),
        grad_features,
        weight_grad.reshape(27, 32, 128),
    )


def solution(mesh):
    placed = (P("ch", "blk"), P(None, "ch", None), P("ch", "blk"), P(None, "blk"))
    return jax.shard_map(
        per_device,
        mesh=mesh,
        in_specs=placed,
        out_specs=(P("ch", "blk"), P("ch", "blk"), P(None, "ch", None)),
        check_vma=False,
    )
```

```python
import functools

import jax
import jax.numpy as jnp
from jax import lax
from jax.experimental import pallas as pl
from jax.experimental.pallas import tpu as pltpu
from jax.sharding import PartitionSpec as P

VOX = 1024
FACE = 128
LANES = 128
PART = 112
INNER = tuple(range(2, 8))
VMEM = pl.BlockSpec(memory_space=pltpu.VMEM)


def source_tiles(group, dz):
    if group == 0:
        return {-1: (8,), 0: (0,), 1: INNER}[dz]
    if group == 1:
        return {-1: INNER, 0: (1,), 1: (9,)}[dz]
    return {-1: (0,) + INNER, 0: INNER, 1: (1,) + INNER}[dz]


def picked(row, group, tiles, load):
    span = row[:, LANES * group : LANES * (group + 1)]
    index = jnp.broadcast_to(span, (32, LANES))
    lane = index & (LANES - 1)
    tile = index >> 7
    total = jnp.zeros((32, LANES), jnp.float32)
    for t in tiles:
        values = jnp.take_along_axis(load(t), lane, axis=1, mode="promise_in_bounds")
        total = jnp.where(tile == t, values, total)
    return total


def tile_span(t):
    return slice(LANES * t, LANES * (t + 1))


def gather_kernel(x_ref, rule_ref, dense_ref, table):
    table[...] = x_ref[...].astype(jnp.float32)

    def step(j, carry):
        for d in range(3):
            k = 3 * j + d
            row = rule_ref[pl.ds(k, 1), :]
            for group in range(8):
                tiles = source_tiles(group, d - 1)
                if tiles[0] >= 8:
                    continue
                got = picked(row, group, tiles, lambda t: table[:, tile_span(t)])
                rows = pl.ds(pl.multiple_of(32 * k, 32), 32)
                dense_ref[rows, tile_span(group)] = got.astype(jnp.bfloat16)
        return carry

    lax.fori_loop(0, 9, step, 0)


def weight_kernel(
    dense_in, rule_ref, lower_ref, upper_ref, g0, g1, g2, g3,
    dense_ref, grad_ref, keep_ref, send_ref, faces, terms,
):
    chan = lax.axis_index("ch")
    near = lax.axis_index("blk") & 7
    for m, part in enumerate((g0, g1, g2, g3)):
        grad_ref[pl.ds(pl.multiple_of(32 * (chan ^ m), 32), 32), :] = part[...]
    faces[:, :FACE] = lower_ref[:32, :].astype(jnp.float32)
    faces[:, FACE:] = upper_ref[:32, :].astype(jnp.float32)

    def step(j, carry):
        for group, d in ((0, 0), (1, 2)):
            k = 3 * j + d
            row = rule_ref[pl.ds(k, 1), :]
            got = picked(row, group, (8 + group,), lambda t: faces[:, tile_span(t - 8)])
            rows = pl.ds(pl.multiple_of(32 * k, 32), 32)
            dense_ref[rows, tile_span(group)] = got.astype(jnp.bfloat16)
        return carry

    lax.fori_loop(0, 9, step, 0)
    terms[:864, :] = lax.dot_general(
        dense_ref[...], grad_ref[...], (((1,), (1,)), ((), ())),
        preferred_element_type=jnp.float32,
    ) * (1.0 / 256.0)
    terms[864:, :] = jnp.zeros((32, LANES), jnp.float32)
    for q in range(4):
        for odd, target in ((0, keep_ref), (1, send_ref)):
            start = pl.multiple_of(PART * (near ^ (2 * q + odd)), 8)
            target[PART * q : PART * (q + 1), :] = terms[pl.ds(start, PART), :]


def forward_kernel(dense_ref, weight_ref, lower_ref, upper_ref, own, s1, s2, s3, sums):
    chan = lax.axis_index("ch")
    sums[...] = lax.dot_general(
        weight_ref[...], dense_ref[...], (((0,), (0,)), ((), ())),
        preferred_element_type=jnp.float32,
    )
    for m, target in enumerate((own, s1, s2, s3)):
        rows = pl.ds(pl.multiple_of(32 * (chan ^ m), 32), 32)
        target[:, :VOX] = sums[rows, :]
        if m:
            target[:, VOX : VOX + FACE] = lower_ref[32:, :].astype(jnp.float32)
            target[:, VOX + FACE :] = upper_ref[32:, :].astype(jnp.float32)


def back_terms_kernel(weight_ref, grad_ref, terms_ref):
    terms_ref[...] = jnp.dot(
        weight_ref[...], grad_ref[...], preferred_element_type=jnp.float32
    )


def back_inner_kernel(groups, fresh, *refs):
    terms, rule_ref = refs[0], refs[1]
    out_ref = refs[-1]
    for group in groups:
        out_ref[:, tile_span(group)] = jnp.zeros((32, LANES), jnp.float32)

    def step(j, carry):
        rules = [rule_ref[pl.ds(3 * j + d, 1), :] for d in range(3)]
        for group in groups:
            running = out_ref[:, tile_span(group)]
            for d in range(3):
                rows = pl.ds(pl.multiple_of(32 * (26 - 3 * j - d), 32), 32)
                running = running + picked(
                    rules[d], group, source_tiles(group, d - 1),
                    lambda t: terms[rows, tile_span(t)],
                )
            out_ref[:, tile_span(group)] = running
        return carry

    lax.fori_loop(0, 9, step, 0)


def edge_kernel(
    terms, rule_ref, weight_ref, lower_ref, upper_ref, inner, own, r1, r2, r3,
    out_ref, grad_ref, faces, products, total,
):
    chan = lax.axis_index("ch")
    summed = (own[...] + r1[:, :VOX]) + (r2[:, :VOX] + r3[:, :VOX])
    out_ref[...] = summed.astype(jnp.bfloat16)
    rows = pl.ds(pl.multiple_of(32 * chan, 32), 32)
    faces[rows, :FACE] = lower_ref[32:, :]
    faces[rows, FACE:] = upper_ref[32:, :]
    for m, part in enumerate((r1, r2, r3)):
        rows = pl.ds(pl.multiple_of(32 * (chan ^ (m + 1)), 32), 32)
        faces[rows, :] = part[:, VOX:].astype(jnp.bfloat16)
    products[...] = jnp.dot(
        weight_ref[...], faces[...], preferred_element_type=jnp.float32
    )
    total[...] = jnp.zeros_like(total)

    def step(j, carry):
        rules = [rule_ref[pl.ds(3 * j + d, 1), :] for d in range(3)]
        for group in range(2):
            running = total[:, tile_span(group)]
            for d in range(3):
                rows = pl.ds(pl.multiple_of(32 * (26 - 3 * j - d), 32), 32)
                running = running + picked(
                    rules[d], group, source_tiles(group, d - 1),
                    lambda t: products[rows, tile_span(t - 8)] if t >= 8
                    else terms[rows, tile_span(t)],
                )
            total[:, tile_span(group)] = running
        return carry

    lax.fori_loop(0, 9, step, 0)
    grad_ref[:, : 2 * LANES] = total[...].astype(jnp.bfloat16)
    grad_ref[:, 2 * LANES :] = inner[:, 2 * LANES :].astype(jnp.bfloat16)


def split_sum_kernel(keep_ref, came_ref, *outs):
    for q, out in enumerate(outs):
        rows = slice(PART * q, PART * (q + 1))
        out[...] = keep_ref[rows, :] + came_ref[rows, :]


def sum_kernel(*refs):
    values = [ref[...] for ref in refs[:-1]]
    while len(values) > 1:
        values = [values[i] + values[i + 1] for i in range(0, len(values), 2)]
    refs[-1][...] = values[0]


def join_kernel(*refs):
    for q, ref in enumerate(refs[:-1]):
        refs[-1][PART * q : PART * (q + 1), :] = ref[...]


def place_kernel(even_ref, odd_ref, out_ref, held):
    near = lax.axis_index("blk") & 7
    for q in range(4):
        rows = slice(PART * q, PART * (q + 1))
        held[2 * PART * q : 2 * PART * q + PART, :] = even_ref[rows, :]
        held[2 * PART * q + PART : 2 * PART * (q + 1), :] = odd_ref[rows, :]
    for p in range(8):
        count = min(PART, 864 - PART * p)
        start = pl.multiple_of(PART * (near ^ p), 8)
        out_ref[PART * p : PART * p + count, :] = held[pl.ds(start, count), :]


def call(kernel, outs, args, scratch=(), aliases=None, flops=0, name=None):
    moved = sum(a.size * a.dtype.itemsize for a in list(args) + jax.tree.leaves(outs))
    return pl.pallas_call(
        kernel,
        out_shape=outs,
        in_specs=[VMEM] * len(args),
        out_specs=jax.tree.map(lambda _: VMEM, outs),
        scratch_shapes=list(scratch),
        input_output_aliases=aliases or {},
        compiler_params=pltpu.CompilerParams(vmem_limit_bytes=40 << 20),
        cost_estimate=pl.CostEstimate(flops=flops, bytes_accessed=moved, transcendentals=0),
        name=name,
    )(*args)


def f32(*shape):
    return jax.ShapeDtypeStruct(shape, jnp.float32)


def bf16(*shape):
    return jax.ShapeDtypeStruct(shape, jnp.bfloat16)


def swap(value, mask):
    count = lax.axis_size("blk")
    return lax.ppermute(value, "blk", [(i, i ^ mask) for i in range(count)])


def shifted(value, steps):
    count = lax.axis_size("blk")
    return lax.ppermute(value, "blk", [(i, (i + steps) % count) for i in range(count)])


def per_device(features, weight, grad_out, rulebook):
    weights = weight.reshape(864, 128)

    def over_ch(value, mask):
        return lax.ppermute(value, "ch", [(i, i ^ mask) for i in range(4)])

    lowest = jnp.concatenate([features[:, :FACE], grad_out[:, :FACE]])
    highest = jnp.concatenate([features[:, FACE : 2 * FACE], grad_out[:, FACE : 2 * FACE]])
    parts = [over_ch(grad_out, m) for m in (1, 2, 3)]
    from_lower = shifted(highest, 1)
    from_upper = shifted(lowest, -1)
    dense = call(
        gather_kernel, bf16(864, VOX), (features, rulebook),
        [pltpu.VMEM((32, VOX), jnp.float32)], flops=3 << 30, name="gather",
    )
    dense, grads, keep, send = call(
        weight_kernel,
        (bf16(864, VOX), bf16(128, VOX), f32(4 * PART, 128), f32(4 * PART, 128)),
        (dense, rulebook, from_lower, from_upper, grad_out, *parts),
        [pltpu.VMEM((32, 2 * FACE), jnp.float32), pltpu.VMEM((8 * PART, 128), jnp.float32)],
        aliases={0: 0}, flops=1 << 30, name="weight_terms",
    )
    came = swap(send, 1)
    own, *sends = call(
        forward_kernel, (f32(32, VOX),) + (f32(32, VOX + 2 * FACE),) * 3,
        (dense, weights, from_lower, from_upper),
        [pltpu.VMEM((128, VOX), jnp.float32)], flops=1 << 30, name="forward",
    )
    pieces = call(split_sum_kernel, (f32(PART, 128),) * 4, (keep, came), name="sum_pair")
    others = [swap(pieces[q], 2 * q) for q in (1, 2, 3)]
    back = call(
        back_terms_kernel, f32(864, VOX), (weights, grads), flops=1 << 30, name="back_terms"
    )
    total = call(sum_kernel, f32(PART, 128), (pieces[0], *others), name="sum_four")
    shares = [over_ch(sends[m - 1], m) for m in (1, 2, 3)]
    total = call(sum_kernel, f32(PART, 128), (total, swap(total, 8)), name="sum_two")
    inner = call(
        functools.partial(back_inner_kernel, (2, 3, 4), True), f32(32, VOX),
        (back, rulebook), flops=3 << 30, name="back_inner",
    )
    total = call(
        sum_kernel, f32(PART, 128), (total, *[swap(total, m) for m in (16, 32, 48)]),
        name="sum_four",
    )
    inner = call(
        functools.partial(back_inner_kernel, (5, 6, 7), False), f32(32, VOX),
        (back, rulebook, inner), aliases={2: 0}, flops=3 << 30, name="back_inner",
    )
    even = call(
        join_kernel, f32(4 * PART, 128),
        (total, *[swap(total, 2 * q) for q in (1, 2, 3)]), name="join",
    )
    output, grad_features = call(
        edge_kernel, (bf16(32, VOX), bf16(32, VOX)),
        (back, rulebook, weights, from_lower, from_upper, inner, own, *shares),
        [pltpu.VMEM((128, 2 * FACE), jnp.bfloat16), pltpu.VMEM((864, 2 * FACE), jnp.float32),
         pltpu.VMEM((32, 2 * LANES), jnp.float32)],
        flops=2 << 30, name="edge",
    )
    odd = swap(even, 1)
    weight_grad = call(
        place_kernel, f32(864, 128), (even, odd),
        [pltpu.VMEM((8 * PART, 128), jnp.float32)], name="place",
    )
    return output, grad_features, weight_grad.reshape(27, 32, 128)


def solution(mesh):
    placed = (P("ch", "blk"), P(None, "ch", None), P("ch", "blk"), P(None, "blk"))
    return jax.shard_map(
        per_device,
        mesh=mesh,
        in_specs=placed,
        out_specs=(P("ch", "blk"), P("ch", "blk"), P(None, "ch", None)),
        check_vma=False,
    )
```

```python
import functools

import jax
import jax.numpy as jnp
from jax import lax
from jax.experimental import pallas as pl
from jax.experimental.pallas import tpu as pltpu
from jax.sharding import PartitionSpec as P

VOX = 1024
FACE = 128
LANES = 128
PART = 112
INNER = tuple(range(2, 8))
EDGE = (0, 1, 7)
VMEM = pl.BlockSpec(memory_space=pltpu.VMEM)


def source_tiles(group, dz):
    if group == 0:
        return {-1: (8,), 0: (0,), 1: INNER}[dz]
    if group == 1:
        return {-1: INNER, 0: (1,), 1: (9,)}[dz]
    return {-1: (0,) + INNER, 0: INNER, 1: (1,) + INNER}[dz]


def picked(row, group, tiles, load):
    span = row[:, LANES * group : LANES * (group + 1)]
    index = jnp.broadcast_to(span, (32, LANES))
    lane = index & (LANES - 1)
    tile = index >> 7
    total = jnp.zeros((32, LANES), jnp.float32)
    for t in tiles:
        values = jnp.take_along_axis(load(t), lane, axis=1, mode="promise_in_bounds")
        total = jnp.where(tile == t, values, total)
    return total


def tile_span(t):
    return slice(LANES * t, LANES * (t + 1))


def faces_kernel(x_ref, g_ref, near_ref, far_ref):
    odd = (lax.axis_index("blk") & 1) == 1
    for rows, ref in ((slice(0, 32), x_ref), (slice(32, 64), g_ref)):
        lowest = ref[:, :FACE].astype(jnp.float32)
        highest = ref[:, FACE : 2 * FACE].astype(jnp.float32)
        near_ref[rows, :] = jnp.where(odd, lowest, highest).astype(jnp.bfloat16)
        far_ref[rows, :] = jnp.where(odd, highest, lowest).astype(jnp.bfloat16)


def by_side(near, far):
    odd = (lax.axis_index("blk") & 1) == 1
    near = near.astype(jnp.float32)
    far = far.astype(jnp.float32)
    return jnp.where(odd, near, far), jnp.where(odd, far, near)


def gather_kernel(x_ref, rule_ref, dense_ref, table):
    table[...] = x_ref[...].astype(jnp.float32)

    def step(j, carry):
        for d in range(3):
            k = 3 * j + d
            row = rule_ref[pl.ds(k, 1), :]
            for group in range(8):
                tiles = source_tiles(group, d - 1)
                if tiles[0] >= 8:
                    continue
                got = picked(row, group, tiles, lambda t: table[:, tile_span(t)])
                rows = pl.ds(pl.multiple_of(32 * k, 32), 32)
                dense_ref[rows, tile_span(group)] = got.astype(jnp.bfloat16)
        return carry

    lax.fori_loop(0, 9, step, 0)


def weight_kernel(
    dense_in, rule_ref, near_ref, far_ref, g0, g1, g2, g3,
    dense_ref, grad_ref, keep_ref, send_ref, faces, terms,
):
    chan = lax.axis_index("ch")
    spot = lax.axis_index("blk") & 7
    for m, part in enumerate((g0, g1, g2, g3)):
        grad_ref[pl.ds(pl.multiple_of(32 * (chan ^ m), 32), 32), :] = part[...]
    faces[:, :FACE], faces[:, FACE:] = by_side(near_ref[:32, :], far_ref[:32, :])

    def step(j, carry):
        for group, d in ((0, 0), (1, 2)):
            k = 3 * j + d
            row = rule_ref[pl.ds(k, 1), :]
            got = picked(row, group, (8 + group,), lambda t: faces[:, tile_span(t - 8)])
            rows = pl.ds(pl.multiple_of(32 * k, 32), 32)
            dense_ref[rows, tile_span(group)] = got.astype(jnp.bfloat16)
        return carry

    lax.fori_loop(0, 9, step, 0)
    terms[:864, :] = lax.dot_general(
        dense_ref[...], grad_ref[...], (((1,), (1,)), ((), ())),
        preferred_element_type=jnp.float32,
    ) * (1.0 / 256.0)
    terms[864:, :] = jnp.zeros((32, LANES), jnp.float32)
    for q in range(4):
        for odd, target in ((0, keep_ref), (1, send_ref)):
            start = pl.multiple_of(PART * (spot ^ (2 * q + odd)), 8)
            target[PART * q : PART * (q + 1), :] = terms[pl.ds(start, PART), :]


def forward_kernel(dense_ref, weight_ref, near_ref, far_ref, own, s1, s2, s3, sums):
    chan = lax.axis_index("ch")
    sums[...] = lax.dot_general(
        weight_ref[...], dense_ref[...], (((0,), (0,)), ((), ())),
        preferred_element_type=jnp.float32,
    )
    lower, upper = by_side(near_ref[32:, :], far_ref[32:, :])
    for m, target in enumerate((own, s1, s2, s3)):
        rows = pl.ds(pl.multiple_of(32 * (chan ^ m), 32), 32)
        target[:, :VOX] = sums[rows, :]
        if m:
            target[:, VOX : VOX + FACE] = lower
            target[:, VOX + FACE :] = upper


def back_terms_kernel(weight_ref, grad_ref, terms_ref):
    terms_ref[...] = jnp.dot(
        weight_ref[...], grad_ref[...], preferred_element_type=jnp.float32
    )


def back_inner_kernel(groups, *refs):
    terms, rule_ref = refs[0], refs[1]
    out_ref = refs[-1]
    for group in groups:
        out_ref[:, tile_span(group)] = jnp.zeros((32, LANES), jnp.float32)

    def step(j, carry):
        rules = [rule_ref[pl.ds(3 * j + d, 1), :] for d in range(3)]
        for group in groups:
            running = out_ref[:, tile_span(group)]
            for d in range(3):
                rows = pl.ds(pl.multiple_of(32 * (26 - 3 * j - d), 32), 32)
                running = running + picked(
                    rules[d], group, source_tiles(group, d - 1),
                    lambda t: terms[rows, tile_span(t)],
                )
            out_ref[:, tile_span(group)] = running
        return carry

    lax.fori_loop(0, 9, step, 0)


def edge_kernel(
    terms, rule_ref, weight_ref, near_ref, far_ref, inner, own, r1, r2, r3,
    out_ref, grad_ref, faces, products, total,
):
    chan = lax.axis_index("ch")
    summed = (own[...] + r1[:, :VOX]) + (r2[:, :VOX] + r3[:, :VOX])
    out_ref[...] = summed.astype(jnp.bfloat16)
    rows = pl.ds(pl.multiple_of(32 * chan, 32), 32)
    lower, upper = by_side(near_ref[32:, :], far_ref[32:, :])
    faces[rows, :FACE] = lower.astype(jnp.bfloat16)
    faces[rows, FACE:] = upper.astype(jnp.bfloat16)
    for m, part in enumerate((r1, r2, r3)):
        rows = pl.ds(pl.multiple_of(32 * (chan ^ (m + 1)), 32), 32)
        faces[rows, :] = part[:, VOX:].astype(jnp.bfloat16)
    products[...] = jnp.dot(
        weight_ref[...], faces[...], preferred_element_type=jnp.float32
    )
    total[...] = jnp.zeros_like(total)

    def step(j, carry):
        rules = [rule_ref[pl.ds(3 * j + d, 1), :] for d in range(3)]
        for group in EDGE:
            running = total[:, tile_span(group)]
            for d in range(3):
                rows = pl.ds(pl.multiple_of(32 * (26 - 3 * j - d), 32), 32)
                running = running + picked(
                    rules[d], group, source_tiles(group, d - 1),
                    lambda t: products[rows, tile_span(t - 8)] if t >= 8
                    else terms[rows, tile_span(t)],
                )
            total[:, tile_span(group)] = running
        return carry

    lax.fori_loop(0, 9, step, 0)
    for group in range(8):
        source = total if group in EDGE else inner
        grad_ref[:, tile_span(group)] = source[:, tile_span(group)].astype(jnp.bfloat16)


def split_sum_kernel(keep_ref, came_ref, *outs):
    for q, out in enumerate(outs):
        rows = slice(PART * q, PART * (q + 1))
        out[...] = keep_ref[rows, :] + came_ref[rows, :]


def sum_kernel(*refs):
    values = [ref[...] for ref in refs[:-1]]
    while len(values) > 1:
        values = [values[i] + values[i + 1] for i in range(0, len(values), 2)]
    refs[-1][...] = values[0]


def join_kernel(*refs):
    for q, ref in enumerate(refs[:-1]):
        refs[-1][PART * q : PART * (q + 1), :] = ref[...]


def place_kernel(even_ref, odd_ref, out_ref, held):
    spot = lax.axis_index("blk") & 7
    for q in range(4):
        rows = slice(PART * q, PART * (q + 1))
        held[2 * PART * q : 2 * PART * q + PART, :] = even_ref[rows, :]
        held[2 * PART * q + PART : 2 * PART * (q + 1), :] = odd_ref[rows, :]
    for p in range(8):
        count = min(PART, 864 - PART * p)
        start = pl.multiple_of(PART * (spot ^ p), 8)
        out_ref[PART * p : PART * p + count, :] = held[pl.ds(start, count), :]


def call(kernel, outs, args, scratch=(), aliases=None, flops=0, name=None):
    moved = sum(a.size * a.dtype.itemsize for a in list(args) + jax.tree.leaves(outs))
    return pl.pallas_call(
        kernel,
        out_shape=outs,
        in_specs=[VMEM] * len(args),
        out_specs=jax.tree.map(lambda _: VMEM, outs),
        scratch_shapes=list(scratch),
        input_output_aliases=aliases or {},
        compiler_params=pltpu.CompilerParams(vmem_limit_bytes=40 << 20),
        cost_estimate=pl.CostEstimate(flops=flops, bytes_accessed=moved, transcendentals=0),
        name=name,
    )(*args)


def f32(*shape):
    return jax.ShapeDtypeStruct(shape, jnp.float32)


def bf16(*shape):
    return jax.ShapeDtypeStruct(shape, jnp.bfloat16)


def swap(value, mask):
    count = lax.axis_size("blk")
    return lax.ppermute(value, "blk", [(i, i ^ mask) for i in range(count)])


def swap_far(value):
    count = lax.axis_size("blk")
    pairs = [(i, (i + 1 if i % 2 else i - 1) % count) for i in range(count)]
    return lax.ppermute(value, "blk", pairs)


def after(values, *others):
    return lax.optimization_barrier((*values, *others))[: len(values)]


def per_device(features, weight, grad_out, rulebook):
    weights = weight.reshape(864, 128)

    def over_ch(value, mask):
        return lax.ppermute(value, "ch", [(i, i ^ mask) for i in range(4)])

    x, g, rules = features, grad_out, rulebook
    near, far = call(faces_kernel, (bf16(64, FACE),) * 2, (x, g), name="faces")
    near = swap(near, 1)
    far = swap_far(far)
    parts = [over_ch(g, m) for m in (1, 2, 3)]
    dense = call(
        gather_kernel, bf16(864, VOX), (x, rules),
        [pltpu.VMEM((32, VOX), jnp.float32)], flops=3 << 30, name="gather",
    )
    dense, grads, keep, send = call(
        weight_kernel,
        (bf16(864, VOX), bf16(128, VOX), f32(4 * PART, 128), f32(4 * PART, 128)),
        (dense, rules, near, far, g, *parts),
        [pltpu.VMEM((32, 2 * FACE), jnp.float32), pltpu.VMEM((8 * PART, 128), jnp.float32)],
        aliases={0: 0}, flops=1 << 30, name="weight_terms",
    )
    came = swap(send, 1)
    own, *sends = call(
        forward_kernel, (f32(32, VOX),) + (f32(32, VOX + 2 * FACE),) * 3,
        (dense, weights, near, far),
        [pltpu.VMEM((128, VOX), jnp.float32)], flops=1 << 30, name="forward",
    )
    back = call(
        back_terms_kernel, f32(864, VOX), (weights, grads), flops=1 << 30, name="back_terms"
    )
    came, = after((came,), own, back)
    pieces = call(split_sum_kernel, (f32(PART, 128),) * 4, (keep, came), name="sum_pair")
    others = [swap(pieces[q], 2 * q) for q in (1, 2, 3)]
    shares = [over_ch(send, m) for m, send in zip((1, 2, 3), after(sends, *pieces))]
    others = after(others, *shares)
    total = call(sum_kernel, f32(PART, 128), (pieces[0], *others), name="sum_four")
    pair = swap(total, 8)
    inner = call(
        functools.partial(back_inner_kernel, (2, 3)), f32(32, VOX),
        (back, rules), flops=2 << 30, name="back_inner",
    )
    pair, = after((pair,), inner)
    total = call(sum_kernel, f32(PART, 128), (total, pair), name="sum_two")
    others = [swap(total, m) for m in (16, 32, 48)]
    inner = call(
        functools.partial(back_inner_kernel, (4, 5, 6)), f32(32, VOX),
        (back, rules, inner), aliases={2: 0}, flops=3 << 30, name="back_inner",
    )
    others = after(others, inner)
    total = call(sum_kernel, f32(PART, 128), (total, *others), name="sum_four")
    others = [swap(total, 2 * q) for q in (1, 2, 3)]
    output, grad_features = call(
        edge_kernel, (bf16(32, VOX), bf16(32, VOX)),
        (back, rules, weights, near, far, inner, own, *shares),
        [pltpu.VMEM((128, 2 * FACE), jnp.bfloat16), pltpu.VMEM((864, 2 * FACE), jnp.float32),
         pltpu.VMEM((32, VOX), jnp.float32)],
        flops=2 << 30, name="edge",
    )
    others = after(others, output)
    even = call(join_kernel, f32(4 * PART, 128), (total, *others), name="join")
    odd = swap(even, 1)
    weight_grad = call(
        place_kernel, f32(864, 128), (even, odd),
        [pltpu.VMEM((8 * PART, 128), jnp.float32)], name="place",
    )
    return output, grad_features, weight_grad.reshape(27, 32, 128)


def solution(mesh):
    placed = (P("ch", "blk"), P(None, "ch", None), P("ch", "blk"), P(None, "blk"))
    return jax.shard_map(
        per_device,
        mesh=mesh,
        in_specs=placed,
        out_specs=(P("ch", "blk"), P("ch", "blk"), P(None, "ch", None)),
        check_vma=False,
    )
```

```python
import functools

import jax
import jax.numpy as jnp
from jax import lax
from jax.experimental import pallas as pl
from jax.experimental.pallas import tpu as pltpu
from jax.sharding import PartitionSpec as P

VOX = 1024
FACE = 128
LANES = 128
PART = 112
INNER = tuple(range(2, 8))
EDGE = (0, 1)
VMEM = pl.BlockSpec(memory_space=pltpu.VMEM)


def source_tiles(group, dz):
    if group == 0:
        return {-1: (8,), 0: (0,), 1: INNER}[dz]
    if group == 1:
        return {-1: INNER, 0: (1,), 1: (9,)}[dz]
    return {-1: (0,) + INNER, 0: INNER, 1: (1,) + INNER}[dz]


def picked(row, group, tiles, load):
    span = row[:, LANES * group : LANES * (group + 1)]
    index = jnp.broadcast_to(span, (32, LANES))
    lane = index & (LANES - 1)
    tile = index >> 7
    total = jnp.zeros((32, LANES), jnp.float32)
    for t in tiles:
        values = jnp.take_along_axis(load(t), lane, axis=1, mode="promise_in_bounds")
        total = jnp.where(tile == t, values, total)
    return total


def tile_span(t):
    return slice(LANES * t, LANES * (t + 1))


def faces_kernel(x_ref, g_ref, near_ref, far_ref):
    odd = (lax.axis_index("blk") & 1) == 1
    for rows, ref in ((slice(0, 32), x_ref), (slice(32, 64), g_ref)):
        lowest = ref[:, :FACE].astype(jnp.float32)
        highest = ref[:, FACE : 2 * FACE].astype(jnp.float32)
        near_ref[rows, :] = jnp.where(odd, lowest, highest).astype(jnp.bfloat16)
        far_ref[rows, :] = jnp.where(odd, highest, lowest).astype(jnp.bfloat16)


def by_side(near, far):
    odd = (lax.axis_index("blk") & 1) == 1
    near = near.astype(jnp.float32)
    far = far.astype(jnp.float32)
    return jnp.where(odd, near, far), jnp.where(odd, far, near)


def gather_kernel(x_ref, rule_ref, dense_ref, table):
    table[...] = x_ref[...].astype(jnp.float32)

    def step(j, carry):
        for d in range(3):
            k = 3 * j + d
            row = rule_ref[pl.ds(k, 1), :]
            for group in range(8):
                tiles = source_tiles(group, d - 1)
                if tiles[0] >= 8:
                    continue
                got = picked(row, group, tiles, lambda t: table[:, tile_span(t)])
                rows = pl.ds(pl.multiple_of(32 * k, 32), 32)
                dense_ref[rows, tile_span(group)] = got.astype(jnp.bfloat16)
        return carry

    lax.fori_loop(0, 9, step, 0)


def weight_kernel(
    dense_in, rule_ref, near_ref, far_ref, pair_ref, other_ref,
    dense_ref, grad_ref, keep_ref, send_ref, faces, terms,
):
    chan = lax.axis_index("ch")
    spot = lax.axis_index("blk") & 7
    for m in range(4):
        part = (pair_ref if m < 2 else other_ref)[32 * (m % 2) : 32 * (m % 2) + 32, :]
        grad_ref[pl.ds(pl.multiple_of(32 * (chan ^ m), 32), 32), :] = part
    faces[:, :FACE], faces[:, FACE:] = by_side(near_ref[:32, :], far_ref[:32, :])

    def step(j, carry):
        for group, d in ((0, 0), (1, 2)):
            k = 3 * j + d
            row = rule_ref[pl.ds(k, 1), :]
            got = picked(row, group, (8 + group,), lambda t: faces[:, tile_span(t - 8)])
            rows = pl.ds(pl.multiple_of(32 * k, 32), 32)
            dense_ref[rows, tile_span(group)] = got.astype(jnp.bfloat16)
        return carry

    lax.fori_loop(0, 9, step, 0)
    terms[:864, :] = lax.dot_general(
        dense_ref[...], grad_ref[...], (((1,), (1,)), ((), ())),
        preferred_element_type=jnp.float32,
    ) * (1.0 / 256.0)
    terms[864:, :] = jnp.zeros((32, LANES), jnp.float32)
    for i, q in enumerate((0, 2, 1, 3)):
        for odd, target in ((0, keep_ref), (1, send_ref)):
            start = pl.multiple_of(PART * (spot ^ (2 * q + odd)), 8)
            target[PART * i : PART * (i + 1), :] = terms[pl.ds(start, PART), :]


def forward_kernel(dense_ref, weight_ref, near_ref, far_ref, keep_ref, send_ref, sums):
    chan = lax.axis_index("ch")
    sums[...] = lax.dot_general(
        weight_ref[...], dense_ref[...], (((0,), (0,)), ((), ())),
        preferred_element_type=jnp.float32,
    )
    for m in range(4):
        target = send_ref if m % 2 else keep_ref
        rows = pl.ds(pl.multiple_of(32 * (chan ^ m), 32), 32)
        target[32 * (m // 2) : 32 * (m // 2) + 32, :VOX] = sums[rows, :]
    lower, upper = by_side(near_ref[32:, :], far_ref[32:, :])
    send_ref[:32, VOX:] = lower
    send_ref[32:, VOX:] = upper


def middle_kernel(keep_ref, came_ref, near_ref, far_ref, own_ref, send_ref):
    own_ref[...] = keep_ref[:32, :] + came_ref[:32, :VOX]
    send_ref[:, :VOX] = keep_ref[32:, :] + came_ref[32:, :VOX]
    lower, upper = by_side(near_ref[32:, :], far_ref[32:, :])
    send_ref[:, VOX : VOX + FACE] = lower
    send_ref[:, VOX + FACE : VOX + 2 * FACE] = upper
    send_ref[:, VOX + 2 * FACE : VOX + 3 * FACE] = came_ref[:32, VOX:]
    send_ref[:, VOX + 3 * FACE :] = came_ref[32:, VOX:]


def back_terms_kernel(weight_ref, grad_ref, terms_ref):
    terms_ref[...] = jnp.dot(
        weight_ref[...], grad_ref[...], preferred_element_type=jnp.float32
    )


def back_inner_kernel(groups, terms, rule_ref, *refs):
    out_ref = refs[-1]
    for group in groups:
        out_ref[:, tile_span(group)] = jnp.zeros((32, LANES), jnp.float32)

    def step(j, carry):
        rules = [rule_ref[pl.ds(3 * j + d, 1), :] for d in range(3)]
        for group in groups:
            running = out_ref[:, tile_span(group)]
            for d in range(3):
                rows = pl.ds(pl.multiple_of(32 * (26 - 3 * j - d), 32), 32)
                running = running + picked(
                    rules[d], group, source_tiles(group, d - 1),
                    lambda t: terms[rows, tile_span(t)],
                )
            out_ref[:, tile_span(group)] = running
        return carry

    lax.fori_loop(0, 9, step, 0)


def edge_kernel(
    terms, rule_ref, weight_ref, near_ref, far_ref, inner, own_ref, first_ref, second_ref,
    out_ref, grad_ref, faces, products, total,
):
    chan = lax.axis_index("ch")
    out_ref[...] = (own_ref[...] + second_ref[:, :VOX]).astype(jnp.bfloat16)
    lower, upper = by_side(near_ref[32:, :], far_ref[32:, :])
    pairs = (
        (lower, upper),
        (first_ref[:32, VOX:], first_ref[32:, VOX:]),
        (second_ref[:, VOX : VOX + FACE], second_ref[:, VOX + FACE : VOX + 2 * FACE]),
        (second_ref[:, VOX + 2 * FACE : VOX + 3 * FACE], second_ref[:, VOX + 3 * FACE :]),
    )
    for m, (lower, upper) in enumerate(pairs):
        rows = pl.ds(pl.multiple_of(32 * (chan ^ m), 32), 32)
        faces[rows, :FACE] = lower.astype(jnp.bfloat16)
        faces[rows, FACE:] = upper.astype(jnp.bfloat16)
    products[...] = jnp.dot(
        weight_ref[...], faces[...], preferred_element_type=jnp.float32
    )
    total[...] = jnp.zeros_like(total)

    def step(j, carry):
        rules = [rule_ref[pl.ds(3 * j + d, 1), :] for d in range(3)]
        for group in EDGE:
            running = total[:, tile_span(group)]
            for d in range(3):
                rows = pl.ds(pl.multiple_of(32 * (26 - 3 * j - d), 32), 32)
                running = running + picked(
                    rules[d], group, source_tiles(group, d - 1),
                    lambda t: products[rows, tile_span(t - 8)] if t >= 8
                    else terms[rows, tile_span(t)],
                )
            total[:, tile_span(group)] = running
        return carry

    lax.fori_loop(0, 9, step, 0)
    for group in range(8):
        source = total if group in EDGE else inner
        grad_ref[:, tile_span(group)] = source[:, tile_span(group)].astype(jnp.bfloat16)


def split_sum_kernel(keep_ref, came_ref, low_ref, high_ref):
    half = low_ref.shape[0]
    low_ref[...] = keep_ref[:half, :] + came_ref[:half, :]
    high_ref[...] = keep_ref[half:, :] + came_ref[half:, :]


def sum_kernel(a_ref, b_ref, out_ref):
    out_ref[...] = a_ref[...] + b_ref[...]


def join_kernel(a_ref, b_ref, out_ref):
    half = a_ref.shape[0]
    out_ref[:half, :] = a_ref[...]
    out_ref[half:, :] = b_ref[...]


def place_kernel(even_ref, odd_ref, out_ref, held):
    spot = lax.axis_index("blk") & 7
    for i, q in enumerate((0, 2, 1, 3)):
        rows = slice(PART * i, PART * (i + 1))
        held[2 * PART * q : 2 * PART * q + PART, :] = even_ref[rows, :]
        held[2 * PART * q + PART : 2 * PART * (q + 1), :] = odd_ref[rows, :]
    for p in range(8):
        count = min(PART, 864 - PART * p)
        start = pl.multiple_of(PART * (spot ^ p), 8)
        out_ref[PART * p : PART * p + count, :] = held[pl.ds(start, count), :]


def call(kernel, outs, args, scratch=(), aliases=None, flops=0, name=None):
    moved = sum(a.size * a.dtype.itemsize for a in list(args) + jax.tree.leaves(outs))
    return pl.pallas_call(
        kernel,
        out_shape=outs,
        in_specs=[VMEM] * len(args),
        out_specs=jax.tree.map(lambda _: VMEM, outs),
        scratch_shapes=list(scratch),
        input_output_aliases=aliases or {},
        compiler_params=pltpu.CompilerParams(vmem_limit_bytes=40 << 20),
        cost_estimate=pl.CostEstimate(flops=flops, bytes_accessed=moved, transcendentals=0),
        name=name,
    )(*args)


def f32(*shape):
    return jax.ShapeDtypeStruct(shape, jnp.float32)


def bf16(*shape):
    return jax.ShapeDtypeStruct(shape, jnp.bfloat16)


def swap(value, mask):
    count = lax.axis_size("blk")
    return lax.ppermute(value, "blk", [(i, i ^ mask) for i in range(count)])


def swap_far(value):
    count = lax.axis_size("blk")
    pairs = [(i, (i + 1 if i % 2 else i - 1) % count) for i in range(count)]
    return lax.ppermute(value, "blk", pairs)


def after(values, *others):
    return lax.optimization_barrier((*values, *others))[: len(values)]


def per_device(features, weight, grad_out, rulebook):
    weights = weight.reshape(864, 128)

    def over_ch(value, mask):
        return lax.ppermute(value, "ch", [(i, i ^ mask) for i in range(4)])

    x, g, rules = features, grad_out, rulebook
    near, far = call(
        faces_kernel, (bf16(64, FACE),) * 2, (x, g), flops=1 << 30, name="faces"
    )
    pair = call(join_kernel, bf16(64, VOX), (g, over_ch(g, 1)), name="join")
    near = swap(near, 1)
    far = swap_far(far)
    other = over_ch(pair, 2)
    dense = call(
        gather_kernel, bf16(864, VOX), (x, rules),
        [pltpu.VMEM((32, VOX), jnp.float32)], flops=3 << 30, name="gather",
    )
    dense, grads, keep, send = call(
        weight_kernel,
        (bf16(864, VOX), bf16(128, VOX), f32(4 * PART, 128), f32(4 * PART, 128)),
        (dense, rules, near, far, pair, other),
        [pltpu.VMEM((32, 2 * FACE), jnp.float32), pltpu.VMEM((8 * PART, 128), jnp.float32)],
        aliases={0: 0}, flops=1 << 30, name="weight_terms",
    )

    def inner_part(groups, inner=None):
        args = (back, rules) if inner is None else (back, rules, inner)
        return call(
            functools.partial(back_inner_kernel, groups), f32(32, VOX), args,
            aliases=None if inner is None else {2: 0}, flops=len(groups) << 30,
            name="back_inner",
        )

    came = swap(send, 1)
    ours, first = call(
        forward_kernel, (f32(64, VOX), f32(64, VOX + FACE)), (dense, weights, near, far),
        [pltpu.VMEM((128, VOX), jnp.float32)], flops=1 << 30, name="forward",
    )
    back = call(
        back_terms_kernel, f32(864, VOX), (weights, grads), flops=1 << 30, name="back_terms"
    )
    came, = after((came,), ours, back)
    kept, sent = call(split_sum_kernel, (f32(2 * PART, 128),) * 2, (keep, came), name="halve")
    came = swap(sent, 2)
    first, = after((first,), kept)
    first = over_ch(first, 1)
    inner = inner_part((2,))
    came, = after((came,), inner)
    kept, sent = call(split_sum_kernel, (f32(PART, 128),) * 2, (kept, came), name="halve")
    came = swap(sent, 4)
    own, second = call(
        middle_kernel, (f32(32, VOX), f32(32, VOX + 4 * FACE)), (ours, first, near, far),
        name="middle",
    )
    came, = after((came,), own)
    total = call(sum_kernel, f32(PART, 128), (kept, came), name="add")
    second, = after((second,), total)
    second = over_ch(second, 2)
    for mask, groups in ((8, (3,)), (16, (4, 5)), (32, (6,))):
        came = swap(total, mask)
        inner = inner_part(groups, inner)
        came, = after((came,), inner)
        total = call(sum_kernel, f32(PART, 128), (total, came), name="add")
    came = swap(total, 4)
    inner = inner_part((7,), inner)
    came, = after((came,), inner)
    total = call(join_kernel, f32(2 * PART, 128), (total, came), name="join")
    came = swap(total, 2)
    output, grad_features = call(
        edge_kernel, (bf16(32, VOX), bf16(32, VOX)),
        (back, rules, weights, near, far, inner, own, first, second),
        [pltpu.VMEM((128, 2 * FACE), jnp.bfloat16), pltpu.VMEM((864, 2 * FACE), jnp.float32),
         pltpu.VMEM((32, VOX), jnp.float32)],
        flops=2 << 30, name="edge",
    )
    came, = after((came,), output)
    even = call(join_kernel, f32(4 * PART, 128), (total, came), name="join")
    odd = swap(even, 1)
    weight_grad = call(
        place_kernel, f32(864, 128), (even, odd),
        [pltpu.VMEM((8 * PART, 128), jnp.float32)], name="place",
    )
    return output, grad_features, weight_grad.reshape(27, 32, 128)


def solution(mesh):
    placed = (P("ch", "blk"), P(None, "ch", None), P("ch", "blk"), P(None, "blk"))
    return jax.shard_map(
        per_device,
        mesh=mesh,
        in_specs=placed,
        out_specs=(P("ch", "blk"), P("ch", "blk"), P(None, "ch", None)),
        check_vma=False,
    )
```

```python
import functools

import jax
import jax.numpy as jnp
from jax import lax
from jax.experimental import pallas as pl
from jax.experimental.pallas import tpu as pltpu
from jax.sharding import PartitionSpec as P

VOX = 1024
FACE = 128
LANES = 128
PART = 112
INNER = tuple(range(2, 8))
EDGE = (0, 1)
VMEM = pl.BlockSpec(memory_space=pltpu.VMEM)


def source_tiles(group, dz):
    if group == 0:
        return {-1: (8,), 0: (0,), 1: INNER}[dz]
    if group == 1:
        return {-1: INNER, 0: (1,), 1: (9,)}[dz]
    return {-1: (0,) + INNER, 0: INNER, 1: (1,) + INNER}[dz]


def picked(row, group, tiles, load):
    span = row[:, LANES * group : LANES * (group + 1)]
    index = jnp.broadcast_to(span, (32, LANES))
    lane = index & (LANES - 1)
    tile = index >> 7
    total = jnp.zeros((32, LANES), jnp.float32)
    for t in tiles:
        values = jnp.take_along_axis(load(t), lane, axis=1, mode="promise_in_bounds")
        total = jnp.where(tile == t, values, total)
    return total


def tile_span(t):
    return slice(LANES * t, LANES * (t + 1))


def faces_kernel(x_ref, g_ref, near_ref, far_ref):
    odd = (lax.axis_index("blk") & 1) == 1
    for rows, ref in ((slice(0, 32), x_ref), (slice(32, 64), g_ref)):
        lowest = ref[:, :FACE].astype(jnp.float32)
        highest = ref[:, FACE : 2 * FACE].astype(jnp.float32)
        near_ref[rows, :] = jnp.where(odd, lowest, highest).astype(jnp.bfloat16)
        far_ref[rows, :] = jnp.where(odd, highest, lowest).astype(jnp.bfloat16)


def by_side(near, far):
    odd = (lax.axis_index("blk") & 1) == 1
    near = near.astype(jnp.float32)
    far = far.astype(jnp.float32)
    return jnp.where(odd, near, far), jnp.where(odd, far, near)


def gather_kernel(x_ref, rule_ref, dense_ref, table):
    table[...] = x_ref[...].astype(jnp.float32)

    def step(j, carry):
        for d in range(3):
            k = 3 * j + d
            row = rule_ref[pl.ds(k, 1), :]
            for group in range(8):
                tiles = source_tiles(group, d - 1)
                if tiles[0] >= 8:
                    continue
                got = picked(row, group, tiles, lambda t: table[:, tile_span(t)])
                rows = pl.ds(pl.multiple_of(32 * k, 32), 32)
                dense_ref[rows, tile_span(group)] = got.astype(jnp.bfloat16)
        return carry

    lax.fori_loop(0, 9, step, 0)


def weight_kernel(
    dense_in, rule_ref, near_ref, far_ref, pair_ref, other_ref,
    dense_ref, grad_ref, keep_ref, send_ref, faces, terms,
):
    chan = lax.axis_index("ch")
    spot = lax.axis_index("blk") & 7
    for m in range(4):
        part = (pair_ref if m < 2 else other_ref)[32 * (m % 2) : 32 * (m % 2) + 32, :]
        grad_ref[pl.ds(pl.multiple_of(32 * (chan ^ m), 32), 32), :] = part
    faces[:, :FACE], faces[:, FACE:] = by_side(near_ref[:32, :], far_ref[:32, :])

    def step(j, carry):
        for group, d in ((0, 0), (1, 2)):
            k = 3 * j + d
            row = rule_ref[pl.ds(k, 1), :]
            got = picked(row, group, (8 + group,), lambda t: faces[:, tile_span(t - 8)])
            rows = pl.ds(pl.multiple_of(32 * k, 32), 32)
            dense_ref[rows, tile_span(group)] = got.astype(jnp.bfloat16)
        return carry

    lax.fori_loop(0, 9, step, 0)
    terms[:864, :] = lax.dot_general(
        dense_ref[...], grad_ref[...], (((1,), (1,)), ((), ())),
        preferred_element_type=jnp.float32,
    ) * (1.0 / 256.0)
    terms[864:, :] = jnp.zeros((32, LANES), jnp.float32)
    for q in range(4):
        for odd, target in ((0, keep_ref), (1, send_ref)):
            start = pl.multiple_of(PART * (spot ^ (2 * q + odd)), 8)
            target[PART * q : PART * (q + 1), :] = terms[pl.ds(start, PART), :]


def forward_kernel(dense_ref, weight_ref, near_ref, far_ref, keep_ref, send_ref, sums):
    chan = lax.axis_index("ch")
    sums[...] = lax.dot_general(
        weight_ref[...], dense_ref[...], (((0,), (0,)), ((), ())),
        preferred_element_type=jnp.float32,
    )
    for m in range(4):
        target = send_ref if m % 2 else keep_ref
        rows = pl.ds(pl.multiple_of(32 * (chan ^ m), 32), 32)
        target[32 * (m // 2) : 32 * (m // 2) + 32, :VOX] = sums[rows, :]
    lower, upper = by_side(near_ref[32:, :], far_ref[32:, :])
    send_ref[:32, VOX:] = lower
    send_ref[32:, VOX:] = upper


def middle_kernel(keep_ref, came_ref, near_ref, far_ref, own_ref, send_ref):
    own_ref[...] = keep_ref[:32, :] + came_ref[:32, :VOX]
    send_ref[:, :VOX] = keep_ref[32:, :] + came_ref[32:, :VOX]
    lower, upper = by_side(near_ref[32:, :], far_ref[32:, :])
    send_ref[:, VOX : VOX + FACE] = lower
    send_ref[:, VOX + FACE : VOX + 2 * FACE] = upper
    send_ref[:, VOX + 2 * FACE : VOX + 3 * FACE] = came_ref[:32, VOX:]
    send_ref[:, VOX + 3 * FACE :] = came_ref[32:, VOX:]


def back_terms_kernel(weight_ref, grad_ref, terms_ref):
    terms_ref[...] = jnp.dot(
        weight_ref[...], grad_ref[...], preferred_element_type=jnp.float32
    )


def back_inner_kernel(groups, terms, rule_ref, *refs):
    out_ref = refs[-1]
    for group in groups:
        out_ref[:, tile_span(group)] = jnp.zeros((32, LANES), jnp.float32)

    def step(j, carry):
        rules = [rule_ref[pl.ds(3 * j + d, 1), :] for d in range(3)]
        for group in groups:
            running = out_ref[:, tile_span(group)]
            for d in range(3):
                rows = pl.ds(pl.multiple_of(32 * (26 - 3 * j - d), 32), 32)
                running = running + picked(
                    rules[d], group, source_tiles(group, d - 1),
                    lambda t: terms[rows, tile_span(t)],
                )
            out_ref[:, tile_span(group)] = running
        return carry

    lax.fori_loop(0, 9, step, 0)


def edge_kernel(
    terms, rule_ref, weight_ref, near_ref, far_ref, inner, own_ref, first_ref, second_ref,
    out_ref, grad_ref, faces, products, total,
):
    chan = lax.axis_index("ch")
    out_ref[...] = (own_ref[...] + second_ref[:, :VOX]).astype(jnp.bfloat16)
    lower, upper = by_side(near_ref[32:, :], far_ref[32:, :])
    pairs = (
        (lower, upper),
        (first_ref[:32, VOX:], first_ref[32:, VOX:]),
        (second_ref[:, VOX : VOX + FACE], second_ref[:, VOX + FACE : VOX + 2 * FACE]),
        (second_ref[:, VOX + 2 * FACE : VOX + 3 * FACE], second_ref[:, VOX + 3 * FACE :]),
    )
    for m, (lower, upper) in enumerate(pairs):
        rows = pl.ds(pl.multiple_of(32 * (chan ^ m), 32), 32)
        faces[rows, :FACE] = lower.astype(jnp.bfloat16)
        faces[rows, FACE:] = upper.astype(jnp.bfloat16)
    products[...] = jnp.dot(
        weight_ref[...], faces[...], preferred_element_type=jnp.float32
    )
    total[...] = jnp.zeros_like(total)

    def step(j, carry):
        rules = [rule_ref[pl.ds(3 * j + d, 1), :] for d in range(3)]
        for group in EDGE:
            running = total[:, tile_span(group)]
            for d in range(3):
                rows = pl.ds(pl.multiple_of(32 * (26 - 3 * j - d), 32), 32)
                running = running + picked(
                    rules[d], group, source_tiles(group, d - 1),
                    lambda t: products[rows, tile_span(t - 8)] if t >= 8
                    else terms[rows, tile_span(t)],
                )
            total[:, tile_span(group)] = running
        return carry

    lax.fori_loop(0, 9, step, 0)
    for group in range(8):
        source = total if group in EDGE else inner
        grad_ref[:, tile_span(group)] = source[:, tile_span(group)].astype(jnp.bfloat16)


def split_sum_kernel(keep_ref, came_ref, *outs):
    for q, out in enumerate(outs):
        rows = slice(PART * q, PART * (q + 1))
        out[...] = keep_ref[rows, :] + came_ref[rows, :]


def sum_kernel(*refs):
    values = [ref[...] for ref in refs[:-1]]
    while len(values) > 1:
        values = [values[i] + values[i + 1] for i in range(0, len(values), 2)]
    refs[-1][...] = values[0]


def join_kernel(*refs):
    size = refs[0].shape[0]
    for q, ref in enumerate(refs[:-1]):
        refs[-1][size * q : size * (q + 1), :] = ref[...]


def place_kernel(even_ref, odd_ref, out_ref, held):
    spot = lax.axis_index("blk") & 7
    for q in range(4):
        rows = slice(PART * q, PART * (q + 1))
        held[2 * PART * q : 2 * PART * q + PART, :] = even_ref[rows, :]
        held[2 * PART * q + PART : 2 * PART * (q + 1), :] = odd_ref[rows, :]
    for p in range(8):
        count = min(PART, 864 - PART * p)
        start = pl.multiple_of(PART * (spot ^ p), 8)
        out_ref[PART * p : PART * p + count, :] = held[pl.ds(start, count), :]


def call(kernel, outs, args, scratch=(), aliases=None, flops=0, name=None):
    moved = sum(a.size * a.dtype.itemsize for a in list(args) + jax.tree.leaves(outs))
    return pl.pallas_call(
        kernel,
        out_shape=outs,
        in_specs=[VMEM] * len(args),
        out_specs=jax.tree.map(lambda _: VMEM, outs),
        scratch_shapes=list(scratch),
        input_output_aliases=aliases or {},
        compiler_params=pltpu.CompilerParams(vmem_limit_bytes=40 << 20),
        cost_estimate=pl.CostEstimate(flops=flops, bytes_accessed=moved, transcendentals=0),
        name=name,
    )(*args)


def f32(*shape):
    return jax.ShapeDtypeStruct(shape, jnp.float32)


def bf16(*shape):
    return jax.ShapeDtypeStruct(shape, jnp.bfloat16)


def swap(value, mask):
    count = lax.axis_size("blk")
    return lax.ppermute(value, "blk", [(i, i ^ mask) for i in range(count)])


def swap_far(value):
    count = lax.axis_size("blk")
    pairs = [(i, (i + 1 if i % 2 else i - 1) % count) for i in range(count)]
    return lax.ppermute(value, "blk", pairs)


def after(values, *others):
    return lax.optimization_barrier((*values, *others))[: len(values)]


def per_device(features, weight, grad_out, rulebook):
    weights = weight.reshape(864, 128)

    def over_ch(value, mask):
        return lax.ppermute(value, "ch", [(i, i ^ mask) for i in range(4)])

    x, g, rules = features, grad_out, rulebook
    near, far = call(
        faces_kernel, (bf16(64, FACE),) * 2, (x, g), flops=1 << 30, name="faces"
    )
    pair = call(join_kernel, bf16(64, VOX), (g, over_ch(g, 1)), name="join")
    near = swap(near, 1)
    far = swap_far(far)
    other = over_ch(pair, 2)
    dense = call(
        gather_kernel, bf16(864, VOX), (x, rules),
        [pltpu.VMEM((32, VOX), jnp.float32)], flops=3 << 30, name="gather",
    )
    dense, grads, keep, send = call(
        weight_kernel,
        (bf16(864, VOX), bf16(128, VOX), f32(4 * PART, 128), f32(4 * PART, 128)),
        (dense, rules, near, far, pair, other),
        [pltpu.VMEM((32, 2 * FACE), jnp.float32), pltpu.VMEM((8 * PART, 128), jnp.float32)],
        aliases={0: 0}, flops=1 << 30, name="weight_terms",
    )

    def inner_part(groups, inner=None):
        args = (back, rules) if inner is None else (back, rules, inner)
        return call(
            functools.partial(back_inner_kernel, groups), f32(32, VOX), args,
            aliases=None if inner is None else {2: 0}, flops=len(groups) << 30,
            name="back_inner",
        )

    came = swap(send, 1)
    ours, first = call(
        forward_kernel, (f32(64, VOX), f32(64, VOX + FACE)), (dense, weights, near, far),
        [pltpu.VMEM((128, VOX), jnp.float32)], flops=1 << 30, name="forward",
    )
    back = call(
        back_terms_kernel, f32(864, VOX), (weights, grads), flops=1 << 30, name="back_terms"
    )
    came, = after((came,), ours, back)
    pieces = call(split_sum_kernel, (f32(PART, 128),) * 4, (keep, came), name="sum_pair")
    others = [swap(pieces[q], 2 * q) for q in (1, 2, 3)]
    first, = after((first,), *pieces)
    first = over_ch(first, 1)
    inner = inner_part((2, 3))
    others = after(others, inner)
    total = call(sum_kernel, f32(PART, 128), (pieces[0], *others), name="sum_four")
    came = swap(total, 8)
    ours, first = after((ours, first), total)
    own, second = call(
        middle_kernel, (f32(32, VOX), f32(32, VOX + 4 * FACE)), (ours, first, near, far),
        name="middle",
    )
    inner = inner_part((4,), inner)
    came, = after((came,), inner, own)
    total = call(sum_kernel, f32(PART, 128), (total, came), name="sum_two")
    second = over_ch(second, 2)
    others = [swap(total, m) for m in (16, 32, 48)]
    inner = inner_part((5, 6, 7), inner)
    others = after(others, inner)
    total = call(sum_kernel, f32(PART, 128), (total, *others), name="sum_four")
    others = [swap(total, 2 * q) for q in (1, 2, 3)]
    output, grad_features = call(
        edge_kernel, (bf16(32, VOX), bf16(32, VOX)),
        (back, rules, weights, near, far, inner, own, first, second),
        [pltpu.VMEM((128, 2 * FACE), jnp.bfloat16), pltpu.VMEM((864, 2 * FACE), jnp.float32),
         pltpu.VMEM((32, VOX), jnp.float32)],
        flops=2 << 30, name="edge",
    )
    others = after(others, output)
    even = call(join_kernel, f32(4 * PART, 128), (total, *others), name="join")
    odd = swap(even, 1)
    weight_grad = call(
        place_kernel, f32(864, 128), (even, odd),
        [pltpu.VMEM((8 * PART, 128), jnp.float32)], name="place",
    )
    return output, grad_features, weight_grad.reshape(27, 32, 128)


def solution(mesh):
    placed = (P("ch", "blk"), P(None, "ch", None), P("ch", "blk"), P(None, "blk"))
    return jax.shard_map(
        per_device,
        mesh=mesh,
        in_specs=placed,
        out_specs=(P("ch", "blk"), P("ch", "blk"), P(None, "ch", None)),
        check_vma=False,
    )
```

```python
import functools

import jax
import jax.numpy as jnp
from jax import lax
from jax.experimental import pallas as pl
from jax.experimental.pallas import tpu as pltpu
from jax.sharding import PartitionSpec as P

VOX = 1024
FACE = 128
LANES = 128
PART = 112
INNER = tuple(range(2, 8))
EDGE = (0, 1)
VMEM = pl.BlockSpec(memory_space=pltpu.VMEM)


def source_tiles(group, dz):
    if group == 0:
        return {-1: (8,), 0: (0,), 1: INNER}[dz]
    if group == 1:
        return {-1: INNER, 0: (1,), 1: (9,)}[dz]
    return {-1: (0,) + INNER, 0: INNER, 1: (1,) + INNER}[dz]


def picked(row, group, tiles, load):
    span = row[:, LANES * group : LANES * (group + 1)]
    index = jnp.broadcast_to(span, (32, LANES))
    lane = index & (LANES - 1)
    tile = index >> 7
    total = jnp.zeros((32, LANES), jnp.float32)
    for t in tiles:
        values = jnp.take_along_axis(load(t), lane, axis=1, mode="promise_in_bounds")
        total = jnp.where(tile == t, values, total)
    return total


def tile_span(t):
    return slice(LANES * t, LANES * (t + 1))


def faces_kernel(x_ref, g_ref, near_ref, far_ref):
    odd = (lax.axis_index("blk") & 1) == 1
    for rows, ref in ((slice(0, 32), x_ref), (slice(32, 64), g_ref)):
        lowest = ref[:, :FACE].astype(jnp.float32)
        highest = ref[:, FACE : 2 * FACE].astype(jnp.float32)
        near_ref[rows, :] = jnp.where(odd, lowest, highest).astype(jnp.bfloat16)
        far_ref[rows, :] = jnp.where(odd, highest, lowest).astype(jnp.bfloat16)


def by_side(near, far):
    odd = (lax.axis_index("blk") & 1) == 1
    near = near.astype(jnp.float32)
    far = far.astype(jnp.float32)
    return jnp.where(odd, near, far), jnp.where(odd, far, near)


def gather_kernel(x_ref, rule_ref, dense_ref, table):
    table[...] = x_ref[...].astype(jnp.float32)
    for k in range(27):
        row = rule_ref[k : k + 1, :]
        for group in range(8):
            tiles = source_tiles(group, k % 3 - 1)
            if tiles[0] >= 8:
                continue
            got = picked(row, group, tiles, lambda t: table[:, tile_span(t)])
            dense_ref[32 * k : 32 * k + 32, tile_span(group)] = got.astype(jnp.bfloat16)


def faces_kernel(x_ref, g_ref, near_ref, far_ref):
    odd = (lax.axis_index("blk") & 1) == 1
    for rows, ref in ((slice(0, 32), x_ref), (slice(32, 64), g_ref)):
        lowest = ref[:, :FACE].astype(jnp.float32)
        highest = ref[:, FACE : 2 * FACE].astype(jnp.float32)
        near_ref[rows, :] = jnp.where(odd, lowest, highest).astype(jnp.bfloat16)
        far_ref[rows, :] = jnp.where(odd, highest, lowest).astype(jnp.bfloat16)


def by_side(near, far):
    odd = (lax.axis_index("blk") & 1) == 1
    near = near.astype(jnp.float32)
    far = far.astype(jnp.float32)
    return jnp.where(odd, near, far), jnp.where(odd, far, near)


def gather_kernel(x_ref, rule_ref, dense_ref, table):
    table[...] = x_ref[...].astype(jnp.float32)

    def step(j, carry):
        for d in range(3):
            k = 3 * j + d
            row = rule_ref[pl.ds(k, 1), :]
            for group in range(8):
                tiles = source_tiles(group, d - 1)
                if tiles[0] >= 8:
                    continue
                got = picked(row, group, tiles, lambda t: table[:, tile_span(t)])
                rows = pl.ds(pl.multiple_of(32 * k, 32), 32)
                dense_ref[rows, tile_span(group)] = got.astype(jnp.bfloat16)
        return carry

    lax.fori_loop(0, 9, step, 0)


def weight_kernel(
    dense_in, rule_ref, near_ref, far_ref, pair_ref, other_ref,
    dense_ref, grad_ref, keep_ref, send_ref, faces, terms,
):
    chan = lax.axis_index("ch")
    spot = lax.axis_index("blk") & 7
    for m in range(4):
        part = (pair_ref if m < 2 else other_ref)[32 * (m % 2) : 32 * (m % 2) + 32, :]
        grad_ref[pl.ds(pl.multiple_of(32 * (chan ^ m), 32), 32), :] = part
    faces[:, :FACE], faces[:, FACE:] = by_side(near_ref[:32, :], far_ref[:32, :])

    for j in range(9):
        for group, d in ((0, 0), (1, 2)):
            k = 3 * j + d
            row = rule_ref[k : k + 1, :]
            got = picked(row, group, (8 + group,), lambda t: faces[:, tile_span(t - 8)])
            dense_ref[32 * k : 32 * k + 32, tile_span(group)] = got.astype(jnp.bfloat16)
    terms[:864, :] = lax.dot_general(
        dense_ref[...], grad_ref[...], (((1,), (1,)), ((), ())),
        preferred_element_type=jnp.float32,
    ) * (1.0 / 256.0)
    terms[864:, :] = jnp.zeros((32, LANES), jnp.float32)
    for q in range(4):
        for odd, target in ((0, keep_ref), (1, send_ref)):
            start = pl.multiple_of(PART * (spot ^ (2 * q + odd)), 8)
            target[PART * q : PART * (q + 1), :] = terms[pl.ds(start, PART), :]


def forward_kernel(dense_ref, weight_ref, near_ref, far_ref, keep_ref, send_ref, sums):
    chan = lax.axis_index("ch")
    sums[...] = lax.dot_general(
        weight_ref[...], dense_ref[...], (((0,), (0,)), ((), ())),
        preferred_element_type=jnp.float32,
    )
    for m in range(4):
        target = send_ref if m % 2 else keep_ref
        rows = pl.ds(pl.multiple_of(32 * (chan ^ m), 32), 32)
        target[32 * (m // 2) : 32 * (m // 2) + 32, :VOX] = sums[rows, :]
    lower, upper = by_side(near_ref[32:, :], far_ref[32:, :])
    send_ref[:32, VOX:] = lower
    send_ref[32:, VOX:] = upper


def middle_kernel(keep_ref, came_ref, near_ref, far_ref, own_ref, send_ref):
    own_ref[...] = keep_ref[:32, :] + came_ref[:32, :VOX]
    send_ref[:, :VOX] = keep_ref[32:, :] + came_ref[32:, :VOX]
    lower, upper = by_side(near_ref[32:, :], far_ref[32:, :])
    send_ref[:, VOX : VOX + FACE] = lower
    send_ref[:, VOX + FACE : VOX + 2 * FACE] = upper
    send_ref[:, VOX + 2 * FACE : VOX + 3 * FACE] = came_ref[:32, VOX:]
    send_ref[:, VOX + 3 * FACE :] = came_ref[32:, VOX:]


def back_terms_kernel(weight_ref, grad_ref, terms_ref):
    terms_ref[...] = jnp.dot(
        weight_ref[...], grad_ref[...], preferred_element_type=jnp.float32
    )


def back_sum(groups, rule_ref, load):
    totals = {}
    for k in range(27):
        row = rule_ref[k : k + 1, :]
        rows = slice(32 * (26 - k), 32 * (26 - k) + 32)
        for group in groups:
            got = picked(row, group, source_tiles(group, k % 3 - 1), lambda t: load(rows, t))
            totals[group] = got if k == 0 else totals[group] + got
    return totals


def back_inner_kernel(groups, terms, rule_ref, *refs):
    totals = back_sum(groups, rule_ref, lambda rows, t: terms[rows, tile_span(t)])
    for group in groups:
        refs[-1][:, tile_span(group)] = totals[group]


def edge_kernel(
    terms, rule_ref, weight_ref, near_ref, far_ref, inner, own_ref, first_ref, second_ref,
    out_ref, grad_ref, faces, products,
):
    chan = lax.axis_index("ch")
    out_ref[...] = (own_ref[...] + second_ref[:, :VOX]).astype(jnp.bfloat16)
    lower, upper = by_side(near_ref[32:, :], far_ref[32:, :])
    pairs = (
        (lower, upper),
        (first_ref[:32, VOX:], first_ref[32:, VOX:]),
        (second_ref[:, VOX : VOX + FACE], second_ref[:, VOX + FACE : VOX + 2 * FACE]),
        (second_ref[:, VOX + 2 * FACE : VOX + 3 * FACE], second_ref[:, VOX + 3 * FACE :]),
    )
    for m, (lower, upper) in enumerate(pairs):
        rows = pl.ds(pl.multiple_of(32 * (chan ^ m), 32), 32)
        faces[rows, :FACE] = lower.astype(jnp.bfloat16)
        faces[rows, FACE:] = upper.astype(jnp.bfloat16)
    products[...] = jnp.dot(
        weight_ref[...], faces[...], preferred_element_type=jnp.float32
    )
    totals = back_sum(
        EDGE, rule_ref,
        lambda rows, t: products[rows, tile_span(t - 8)] if t >= 8 else terms[rows, tile_span(t)],
    )
    for group in range(8):
        values = totals[group] if group in EDGE else inner[:, tile_span(group)]
        grad_ref[:, tile_span(group)] = values.astype(jnp.bfloat16)


def split_sum_kernel(keep_ref, came_ref, *outs):
    for q, out in enumerate(outs):
        rows = slice(PART * q, PART * (q + 1))
        out[...] = keep_ref[rows, :] + came_ref[rows, :]


def sum_kernel(*refs):
    values = [ref[...] for ref in refs[:-1]]
    while len(values) > 1:
        values = [values[i] + values[i + 1] for i in range(0, len(values), 2)]
    refs[-1][...] = values[0]


def join_kernel(*refs):
    size = refs[0].shape[0]
    for q, ref in enumerate(refs[:-1]):
        refs[-1][size * q : size * (q + 1), :] = ref[...]


def place_kernel(*refs):
    out_ref, held = refs[-2:]
    spot = lax.axis_index("blk") & 7
    for q in range(4):
        held[2 * PART * q : 2 * PART * (q + 1), :] = refs[q][...]
    for p in range(8):
        count = min(PART, 864 - PART * p)
        start = pl.multiple_of(PART * (spot ^ p), 8)
        out_ref[PART * p : PART * p + count, :] = held[pl.ds(start, count), :]


def call(kernel, outs, args, scratch=(), aliases=None, flops=0, name=None):
    moved = sum(a.size * a.dtype.itemsize for a in list(args) + jax.tree.leaves(outs))
    return pl.pallas_call(
        kernel,
        out_shape=outs,
        in_specs=[VMEM] * len(args),
        out_specs=jax.tree.map(lambda _: VMEM, outs),
        scratch_shapes=list(scratch),
        input_output_aliases=aliases or {},
        compiler_params=pltpu.CompilerParams(vmem_limit_bytes=40 << 20),
        cost_estimate=pl.CostEstimate(flops=flops, bytes_accessed=moved, transcendentals=0),
        name=name,
    )(*args)


def f32(*shape):
    return jax.ShapeDtypeStruct(shape, jnp.float32)


def bf16(*shape):
    return jax.ShapeDtypeStruct(shape, jnp.bfloat16)


def swap(value, mask):
    count = lax.axis_size("blk")
    return lax.ppermute(value, "blk", [(i, i ^ mask) for i in range(count)])


def swap_far(value):
    count = lax.axis_size("blk")
    pairs = [(i, (i + 1 if i % 2 else i - 1) % count) for i in range(count)]
    return lax.ppermute(value, "blk", pairs)


def after(values, *others):
    return lax.optimization_barrier((*values, *others))[: len(values)]


def per_device(features, weight, grad_out, rulebook):
    weights = weight.reshape(864, 128)

    def over_ch(value, mask):
        return lax.ppermute(value, "ch", [(i, i ^ mask) for i in range(4)])

    x, g, rules = features, grad_out, rulebook
    near, far = call(
        faces_kernel, (bf16(64, FACE),) * 2, (x, g), flops=1 << 30, name="faces"
    )
    pair = call(join_kernel, bf16(64, VOX), (g, over_ch(g, 1)), name="join")
    near = swap(near, 1)
    far = swap_far(far)
    other = over_ch(pair, 2)
    dense = call(
        gather_kernel, bf16(864, VOX), (x, rules),
        [pltpu.VMEM((32, VOX), jnp.float32)], flops=3 << 30, name="gather",
    )
    dense, grads, keep, send = call(
        weight_kernel,
        (bf16(864, VOX), bf16(128, VOX), f32(4 * PART, 128), f32(4 * PART, 128)),
        (dense, rules, near, far, pair, other),
        [pltpu.VMEM((32, 2 * FACE), jnp.float32), pltpu.VMEM((8 * PART, 128), jnp.float32)],
        aliases={0: 0}, flops=1 << 30, name="weight_terms",
    )

    def inner_part(groups, inner=None):
        args = (back, rules) if inner is None else (back, rules, inner)
        return call(
            functools.partial(back_inner_kernel, groups), f32(32, VOX), args,
            aliases=None if inner is None else {2: 0}, flops=len(groups) << 30,
            name="back_inner",
        )

    came = swap(send, 1)
    ours, first = call(
        forward_kernel, (f32(64, VOX), f32(64, VOX + FACE)), (dense, weights, near, far),
        [pltpu.VMEM((128, VOX), jnp.float32)], flops=1 << 30, name="forward",
    )
    back = call(
        back_terms_kernel, f32(864, VOX), (weights, grads), flops=1 << 30, name="back_terms"
    )
    came, = after((came,), ours, back)
    pieces = call(split_sum_kernel, (f32(PART, 128),) * 4, (keep, came), name="sum_pair")
    others = [swap(pieces[q], 2 * q) for q in (1, 2, 3)]
    first, = after((first,), *pieces)
    first = over_ch(first, 1)
    inner = inner_part((2, 3))
    others = after(others, inner)
    total = call(sum_kernel, f32(PART, 128), (pieces[0], *others), name="sum_four")
    came = swap(total, 8)
    inner = inner_part((4, 5), inner)
    came, = after((came,), inner)
    total = call(sum_kernel, f32(PART, 128), (total, came), name="sum_two")
    others = [swap(total, m) for m in (16, 32, 48)]
    ours, first = after((ours, first), total)
    own, second = call(
        middle_kernel, (f32(32, VOX), f32(32, VOX + 4 * FACE)), (ours, first, near, far),
        name="middle",
    )
    second = over_ch(second, 2)
    inner = inner_part((6, 7), inner)
    others = after(others, inner, own)
    total = call(sum_kernel, f32(PART, 128), (total, *others), name="sum_four")
    both = call(join_kernel, f32(2 * PART, 128), (total, swap(total, 1)), name="join")
    others = [swap(both, 2 * q) for q in (1, 2, 3)]
    output, grad_features = call(
        edge_kernel, (bf16(32, VOX), bf16(32, VOX)),
        (back, rules, weights, near, far, inner, own, first, second),
        [pltpu.VMEM((128, 2 * FACE), jnp.bfloat16), pltpu.VMEM((864, 2 * FACE), jnp.float32)],
        flops=2 << 30, name="edge",
    )
    others = after(others, output)
    weight_grad = call(
        place_kernel, f32(864, 128), (both, *others),
        [pltpu.VMEM((8 * PART, 128), jnp.float32)], name="place",
    )
    return output, grad_features, weight_grad.reshape(27, 32, 128)


def solution(mesh):
    placed = (P("ch", "blk"), P(None, "ch", None), P("ch", "blk"), P(None, "blk"))
    return jax.shard_map(
        per_device,
        mesh=mesh,
        in_specs=placed,
        out_specs=(P("ch", "blk"), P("ch", "blk"), P(None, "ch", None)),
        check_vma=False,
    )
```

```python
import functools

import jax
import jax.numpy as jnp
from jax import lax
from jax.experimental import pallas as pl
from jax.experimental.pallas import tpu as pltpu
from jax.sharding import PartitionSpec as P

VOX = 1024
FACE = 128
LANES = 128
PART = 112
INNER = tuple(range(2, 8))
EDGE = (0, 1)
ORDER = (0, 1, 3, 2)
VMEM = pl.BlockSpec(memory_space=pltpu.VMEM)


def source_tiles(group, dz):
    if group == 0:
        return {-1: (8,), 0: (0,), 1: INNER}[dz]
    if group == 1:
        return {-1: INNER, 0: (1,), 1: (9,)}[dz]
    return {-1: (0,) + INNER, 0: INNER, 1: (1,) + INNER}[dz]


def picked(row, group, tiles, load):
    span = row[:, LANES * group : LANES * (group + 1)]
    index = jnp.broadcast_to(span, (32, LANES))
    lane = index & (LANES - 1)
    tile = index >> 7
    total = jnp.zeros((32, LANES), jnp.float32)
    for t in tiles:
        values = jnp.take_along_axis(load(t), lane, axis=1, mode="promise_in_bounds")
        total = jnp.where(tile == t, values, total)
    return total


def tile_span(t):
    return slice(LANES * t, LANES * (t + 1))


def faces_kernel(x_ref, g_ref, near_ref, far_ref):
    odd = (lax.axis_index("blk") & 1) == 1
    for rows, ref in ((slice(0, 32), x_ref), (slice(32, 64), g_ref)):
        lowest = ref[:, :FACE].astype(jnp.float32)
        highest = ref[:, FACE : 2 * FACE].astype(jnp.float32)
        near_ref[rows, :] = jnp.where(odd, lowest, highest).astype(jnp.bfloat16)
        far_ref[rows, :] = jnp.where(odd, highest, lowest).astype(jnp.bfloat16)


def by_side(near, far):
    odd = (lax.axis_index("blk") & 1) == 1
    near = near.astype(jnp.float32)
    far = far.astype(jnp.float32)
    return jnp.where(odd, near, far), jnp.where(odd, far, near)


def gather_kernel(x_ref, rule_ref, dense_ref, table):
    table[...] = x_ref[...].astype(jnp.float32)
    for k in range(27):
        row = rule_ref[k : k + 1, :]
        for group in range(8):
            tiles = source_tiles(group, k % 3 - 1)
            if tiles[0] >= 8:
                continue
            got = picked(row, group, tiles, lambda t: table[:, tile_span(t)])
            dense_ref[32 * k : 32 * k + 32, tile_span(group)] = got.astype(jnp.bfloat16)


def faces_kernel(x_ref, g_ref, near_ref, far_ref):
    odd = (lax.axis_index("blk") & 1) == 1
    for rows, ref in ((slice(0, 32), x_ref), (slice(32, 64), g_ref)):
        lowest = ref[:, :FACE].astype(jnp.float32)
        highest = ref[:, FACE : 2 * FACE].astype(jnp.float32)
        near_ref[rows, :] = jnp.where(odd, lowest, highest).astype(jnp.bfloat16)
        far_ref[rows, :] = jnp.where(odd, highest, lowest).astype(jnp.bfloat16)


def by_side(near, far):
    odd = (lax.axis_index("blk") & 1) == 1
    near = near.astype(jnp.float32)
    far = far.astype(jnp.float32)
    return jnp.where(odd, near, far), jnp.where(odd, far, near)


def gather_kernel(x_ref, rule_ref, dense_ref, table):
    table[...] = x_ref[...].astype(jnp.float32)

    def step(j, carry):
        for d in range(3):
            k = 3 * j + d
            row = rule_ref[pl.ds(k, 1), :]
            for group in range(8):
                tiles = source_tiles(group, d - 1)
                if tiles[0] >= 8:
                    continue
                got = picked(row, group, tiles, lambda t: table[:, tile_span(t)])
                rows = pl.ds(pl.multiple_of(32 * k, 32), 32)
                dense_ref[rows, tile_span(group)] = got.astype(jnp.bfloat16)
        return carry

    lax.fori_loop(0, 9, step, 0)


def weight_kernel(
    dense_in, rule_ref, near_ref, far_ref, pair_ref, other_ref,
    dense_ref, grad_ref, keep_ref, send_ref, faces, terms,
):
    chan = lax.axis_index("ch")
    spot = lax.axis_index("blk") & 7
    for i, m in enumerate(ORDER):
        part = (pair_ref if i < 2 else other_ref)[32 * (i % 2) : 32 * (i % 2) + 32, :]
        grad_ref[pl.ds(pl.multiple_of(32 * (chan ^ m), 32), 32), :] = part
    faces[:, :FACE], faces[:, FACE:] = by_side(near_ref[:32, :], far_ref[:32, :])

    for j in range(9):
        for group, d in ((0, 0), (1, 2)):
            k = 3 * j + d
            row = rule_ref[k : k + 1, :]
            got = picked(row, group, (8 + group,), lambda t: faces[:, tile_span(t - 8)])
            dense_ref[32 * k : 32 * k + 32, tile_span(group)] = got.astype(jnp.bfloat16)
    terms[:864, :] = lax.dot_general(
        dense_ref[...], grad_ref[...], (((1,), (1,)), ((), ())),
        preferred_element_type=jnp.float32,
    ) * (1.0 / 256.0)
    terms[864:, :] = jnp.zeros((32, LANES), jnp.float32)
    for i, q in enumerate((0, 3, 1, 2)):
        for odd, target in ((0, keep_ref), (1, send_ref)):
            start = pl.multiple_of(PART * (spot ^ (2 * q + odd)), 8)
            target[PART * i : PART * (i + 1), :] = terms[pl.ds(start, PART), :]


def forward_kernel(dense_ref, weight_ref, near_ref, far_ref, keep_ref, send_ref, sums):
    chan = lax.axis_index("ch")
    sums[...] = lax.dot_general(
        weight_ref[...], dense_ref[...], (((0,), (0,)), ((), ())),
        preferred_element_type=jnp.float32,
    )
    for target, parts in ((keep_ref, (0, 3)), (send_ref, (1, 2))):
        for i, m in enumerate(parts):
            rows = pl.ds(pl.multiple_of(32 * (chan ^ m), 32), 32)
            target[32 * i : 32 * i + 32, :VOX] = sums[rows, :]
    lower, upper = by_side(near_ref[32:, :], far_ref[32:, :])
    send_ref[:32, VOX:] = lower
    send_ref[32:, VOX:] = upper


def middle_kernel(keep_ref, came_ref, near_ref, far_ref, own_ref, send_ref):
    own_ref[...] = keep_ref[:32, :] + came_ref[:32, :VOX]
    send_ref[:, :VOX] = keep_ref[32:, :] + came_ref[32:, :VOX]
    lower, upper = by_side(near_ref[32:, :], far_ref[32:, :])
    send_ref[:, VOX : VOX + FACE] = lower
    send_ref[:, VOX + FACE : VOX + 2 * FACE] = upper
    send_ref[:, VOX + 2 * FACE : VOX + 3 * FACE] = came_ref[:32, VOX:]
    send_ref[:, VOX + 3 * FACE :] = came_ref[32:, VOX:]


def back_terms_kernel(weight_ref, grad_ref, terms_ref):
    terms_ref[...] = jnp.dot(
        weight_ref[...], grad_ref[...], preferred_element_type=jnp.float32
    )


def back_sum(groups, rule_ref, load):
    totals = {}
    for k in range(27):
        row = rule_ref[k : k + 1, :]
        rows = slice(32 * (26 - k), 32 * (26 - k) + 32)
        for group in groups:
            got = picked(row, group, source_tiles(group, k % 3 - 1), lambda t: load(rows, t))
            totals[group] = got if k == 0 else totals[group] + got
    return totals


def back_inner_kernel(groups, terms, rule_ref, *refs):
    totals = back_sum(groups, rule_ref, lambda rows, t: terms[rows, tile_span(t)])
    for group in groups:
        refs[-1][:, tile_span(group)] = totals[group]


def edge_kernel(
    terms, rule_ref, weight_ref, near_ref, far_ref, inner, own_ref, first_ref, second_ref,
    out_ref, grad_ref, faces, products,
):
    chan = lax.axis_index("ch")
    out_ref[...] = (own_ref[...] + second_ref[:, :VOX]).astype(jnp.bfloat16)
    lower, upper = by_side(near_ref[32:, :], far_ref[32:, :])
    pairs = (
        (lower, upper),
        (first_ref[:32, VOX:], first_ref[32:, VOX:]),
        (second_ref[:, VOX : VOX + FACE], second_ref[:, VOX + FACE : VOX + 2 * FACE]),
        (second_ref[:, VOX + 2 * FACE : VOX + 3 * FACE], second_ref[:, VOX + 3 * FACE :]),
    )
    for m, (lower, upper) in zip(ORDER, pairs):
        rows = pl.ds(pl.multiple_of(32 * (chan ^ m), 32), 32)
        faces[rows, :FACE] = lower.astype(jnp.bfloat16)
        faces[rows, FACE:] = upper.astype(jnp.bfloat16)
    products[...] = jnp.dot(
        weight_ref[...], faces[...], preferred_element_type=jnp.float32
    )
    totals = back_sum(
        EDGE, rule_ref,
        lambda rows, t: products[rows, tile_span(t - 8)] if t >= 8 else terms[rows, tile_span(t)],
    )
    for group in range(8):
        values = totals[group] if group in EDGE else inner[:, tile_span(group)]
        grad_ref[:, tile_span(group)] = values.astype(jnp.bfloat16)


def halve_kernel(keep_ref, came_ref, low_ref, high_ref):
    half = low_ref.shape[0]
    low_ref[...] = keep_ref[:half, :] + came_ref[:half, :]
    high_ref[...] = keep_ref[half:, :] + came_ref[half:, :]


def add_kernel(a_ref, b_ref, out_ref):
    out_ref[...] = a_ref[...] + b_ref[...]


def join_kernel(a_ref, b_ref, out_ref):
    half = a_ref.shape[0]
    out_ref[:half, :] = a_ref[...]
    out_ref[half:, :] = b_ref[...]


def place_kernel(even_ref, odd_ref, out_ref, held):
    spot = lax.axis_index("blk") & 7
    for i, q in enumerate((0, 3, 1, 2)):
        for odd, ref in enumerate((even_ref, odd_ref)):
            start = PART * (2 * q + odd)
            held[start : start + PART, :] = ref[PART * i : PART * (i + 1), :]
    for p in range(8):
        count = min(PART, 864 - PART * p)
        start = pl.multiple_of(PART * (spot ^ p), 8)
        out_ref[PART * p : PART * p + count, :] = held[pl.ds(start, count), :]


def call(kernel, outs, args, scratch=(), aliases=None, flops=0, name=None):
    moved = sum(a.size * a.dtype.itemsize for a in list(args) + jax.tree.leaves(outs))
    return pl.pallas_call(
        kernel,
        out_shape=outs,
        in_specs=[VMEM] * len(args),
        out_specs=jax.tree.map(lambda _: VMEM, outs),
        scratch_shapes=list(scratch),
        input_output_aliases=aliases or {},
        compiler_params=pltpu.CompilerParams(vmem_limit_bytes=40 << 20),
        cost_estimate=pl.CostEstimate(flops=flops, bytes_accessed=moved, transcendentals=0),
        name=name,
    )(*args)


def f32(*shape):
    return jax.ShapeDtypeStruct(shape, jnp.float32)


def bf16(*shape):
    return jax.ShapeDtypeStruct(shape, jnp.bfloat16)


def swap(value, mask):
    count = lax.axis_size("blk")
    return lax.ppermute(value, "blk", [(i, i ^ mask) for i in range(count)])


def swap_far(value):
    count = lax.axis_size("blk")
    pairs = [(i, (i + 1 if i % 2 else i - 1) % count) for i in range(count)]
    return lax.ppermute(value, "blk", pairs)


def after(values, *others):
    return lax.optimization_barrier((*values, *others))[: len(values)]


def per_device(features, weight, grad_out, rulebook):
    weights = weight.reshape(864, 128)

    def over_ch(value, mask):
        return lax.ppermute(value, "ch", [(i, i ^ mask) for i in range(4)])

    x, g, rules = features, grad_out, rulebook
    near, far = call(
        faces_kernel, (bf16(64, FACE),) * 2, (x, g), flops=1 << 30, name="faces"
    )
    pair = call(join_kernel, bf16(64, VOX), (g, over_ch(g, 1)), name="join")
    near = swap(near, 1)
    far = swap_far(far)
    other = over_ch(pair, 3)
    dense = call(
        gather_kernel, bf16(864, VOX), (x, rules),
        [pltpu.VMEM((32, VOX), jnp.float32)], flops=3 << 30, name="gather",
    )
    dense, grads, keep, send = call(
        weight_kernel,
        (bf16(864, VOX), bf16(128, VOX), f32(4 * PART, 128), f32(4 * PART, 128)),
        (dense, rules, near, far, pair, other),
        [pltpu.VMEM((32, 2 * FACE), jnp.float32), pltpu.VMEM((8 * PART, 128), jnp.float32)],
        aliases={0: 0}, flops=1 << 30, name="weight_terms",
    )

    def inner_part(groups, inner=None):
        args = (back, rules) if inner is None else (back, rules, inner)
        return call(
            functools.partial(back_inner_kernel, groups), f32(32, VOX), args,
            aliases=None if inner is None else {2: 0}, flops=len(groups) << 30,
            name="back_inner",
        )

    came = swap(send, 1)
    ours, first = call(
        forward_kernel, (f32(64, VOX), f32(64, VOX + FACE)), (dense, weights, near, far),
        [pltpu.VMEM((128, VOX), jnp.float32)], flops=1 << 30, name="forward",
    )
    back = call(
        back_terms_kernel, f32(864, VOX), (weights, grads), flops=1 << 30, name="back_terms"
    )
    came, = after((came,), ours, back)
    kept, sent = call(halve_kernel, (f32(2 * PART, 128),) * 2, (keep, came), name="halve")
    came = swap(sent, 2)
    first, = after((first,), kept)
    first = over_ch(first, 1)
    inner = inner_part((2,))
    came, = after((came,), inner)
    kept, sent = call(halve_kernel, (f32(PART, 128),) * 2, (kept, came), name="halve")
    came = swap(sent, 6)
    inner = inner_part((3,), inner)
    came, = after((came,), inner)
    total = call(add_kernel, f32(PART, 128), (kept, came), name="add")
    came = swap(total, 8)
    ours, first = after((ours, first), total)
    own, second = call(
        middle_kernel, (f32(32, VOX), f32(32, VOX + 4 * FACE)), (ours, first, near, far),
        name="middle",
    )
    second = over_ch(second, 3)
    came, = after((came,), own)
    total = call(add_kernel, f32(PART, 128), (total, came), name="add")
    for mask, groups in ((16, (4, 5)), (48, (6, 7))):
        came = swap(total, mask)
        inner = inner_part(groups, inner)
        came, = after((came,), inner)
        total = call(add_kernel, f32(PART, 128), (total, came), name="add")
    total = call(join_kernel, f32(2 * PART, 128), (total, swap(total, 6)), name="join")
    came = swap(total, 2)
    output, grad_features = call(
        edge_kernel, (bf16(32, VOX), bf16(32, VOX)),
        (back, rules, weights, near, far, inner, own, first, second),
        [pltpu.VMEM((128, 2 * FACE), jnp.bfloat16), pltpu.VMEM((864, 2 * FACE), jnp.float32)],
        flops=2 << 30, name="edge",
    )
    came, = after((came,), output)
    even = call(join_kernel, f32(4 * PART, 128), (total, came), name="join")
    odd = swap(even, 1)
    weight_grad = call(
        place_kernel, f32(864, 128), (even, odd),
        [pltpu.VMEM((8 * PART, 128), jnp.float32)], name="place",
    )
    return output, grad_features, weight_grad.reshape(27, 32, 128)


def solution(mesh):
    placed = (P("ch", "blk"), P(None, "ch", None), P("ch", "blk"), P(None, "blk"))
    return jax.shard_map(
        per_device,
        mesh=mesh,
        in_specs=placed,
        out_specs=(P("ch", "blk"), P("ch", "blk"), P(None, "ch", None)),
        check_vma=False,
    )
```

```python
import functools

import jax
import jax.numpy as jnp
from jax import lax
from jax.experimental import pallas as pl
from jax.experimental.pallas import tpu as pltpu
from jax.sharding import PartitionSpec as P

VOX = 1024
FACE = 128
LANES = 128
PART = 112
INNER = tuple(range(2, 8))
EDGE = (0, 1, 6, 7)
ORDER = (0, 1, 3, 2)
VMEM = pl.BlockSpec(memory_space=pltpu.VMEM)


def source_tiles(group, dz):
    if group == 0:
        return {-1: (8,), 0: (0,), 1: INNER}[dz]
    if group == 1:
        return {-1: INNER, 0: (1,), 1: (9,)}[dz]
    return {-1: (0,) + INNER, 0: INNER, 1: (1,) + INNER}[dz]


def picked(row, group, tiles, load):
    span = row[:, LANES * group : LANES * (group + 1)]
    index = jnp.broadcast_to(span, (32, LANES))
    lane = index & (LANES - 1)
    tile = index >> 7
    total = jnp.zeros((32, LANES), jnp.float32)
    for t in tiles:
        values = jnp.take_along_axis(load(t), lane, axis=1, mode="promise_in_bounds")
        total = jnp.where(tile == t, values, total)
    return total


def tile_span(t):
    return slice(LANES * t, LANES * (t + 1))


def faces_kernel(x_ref, g_ref, near_ref, far_ref):
    odd = (lax.axis_index("blk") & 1) == 1
    for rows, ref in ((slice(0, 32), x_ref), (slice(32, 64), g_ref)):
        lowest = ref[:, :FACE].astype(jnp.float32)
        highest = ref[:, FACE : 2 * FACE].astype(jnp.float32)
        near_ref[rows, :] = jnp.where(odd, lowest, highest).astype(jnp.bfloat16)
        far_ref[rows, :] = jnp.where(odd, highest, lowest).astype(jnp.bfloat16)


def by_side(near, far):
    odd = (lax.axis_index("blk") & 1) == 1
    near = near.astype(jnp.float32)
    far = far.astype(jnp.float32)
    return jnp.where(odd, near, far), jnp.where(odd, far, near)


def gather_kernel(x_ref, rule_ref, dense_ref, table):
    table[...] = x_ref[...].astype(jnp.float32)
    for k in range(27):
        row = rule_ref[k : k + 1, :]
        for group in range(8):
            tiles = source_tiles(group, k % 3 - 1)
            if tiles[0] >= 8:
                continue
            got = picked(row, group, tiles, lambda t: table[:, tile_span(t)])
            dense_ref[32 * k : 32 * k + 32, tile_span(group)] = got.astype(jnp.bfloat16)


def faces_kernel(x_ref, g_ref, near_ref, far_ref):
    odd = (lax.axis_index("blk") & 1) == 1
    for rows, ref in ((slice(0, 32), x_ref), (slice(32, 64), g_ref)):
        lowest = ref[:, :FACE].astype(jnp.float32)
        highest = ref[:, FACE : 2 * FACE].astype(jnp.float32)
        near_ref[rows, :] = jnp.where(odd, lowest, highest).astype(jnp.bfloat16)
        far_ref[rows, :] = jnp.where(odd, highest, lowest).astype(jnp.bfloat16)


def by_side(near, far):
    odd = (lax.axis_index("blk") & 1) == 1
    near = near.astype(jnp.float32)
    far = far.astype(jnp.float32)
    return jnp.where(odd, near, far), jnp.where(odd, far, near)


def gather_kernel(x_ref, rule_ref, dense_ref, table):
    table[...] = x_ref[...].astype(jnp.float32)

    def step(j, carry):
        for d in range(3):
            k = 3 * j + d
            row = rule_ref[pl.ds(k, 1), :]
            for group in range(8):
                tiles = source_tiles(group, d - 1)
                if tiles[0] >= 8:
                    continue
                got = picked(row, group, tiles, lambda t: table[:, tile_span(t)])
                rows = pl.ds(pl.multiple_of(32 * k, 32), 32)
                dense_ref[rows, tile_span(group)] = got.astype(jnp.bfloat16)
        return carry

    lax.fori_loop(0, 9, step, 0)


def weight_kernel(
    dense_in, rule_ref, near_ref, far_ref, pair_ref, other_ref,
    dense_ref, grad_ref, keep_ref, send_ref, faces, terms,
):
    chan = lax.axis_index("ch")
    spot = lax.axis_index("blk") & 7
    for i, m in enumerate(ORDER):
        part = (pair_ref if i < 2 else other_ref)[32 * (i % 2) : 32 * (i % 2) + 32, :]
        grad_ref[pl.ds(pl.multiple_of(32 * (chan ^ m), 32), 32), :] = part
    faces[:, :FACE], faces[:, FACE:] = by_side(near_ref[:32, :], far_ref[:32, :])

    for j in range(9):
        for group, d in ((0, 0), (1, 2)):
            k = 3 * j + d
            row = rule_ref[k : k + 1, :]
            got = picked(row, group, (8 + group,), lambda t: faces[:, tile_span(t - 8)])
            dense_ref[32 * k : 32 * k + 32, tile_span(group)] = got.astype(jnp.bfloat16)
    terms[:864, :] = lax.dot_general(
        dense_ref[...], grad_ref[...], (((1,), (1,)), ((), ())),
        preferred_element_type=jnp.float32,
    ) * (1.0 / 256.0)
    terms[864:, :] = jnp.zeros((32, LANES), jnp.float32)
    for q in range(4):
        for odd, target in ((0, keep_ref), (1, send_ref)):
            start = pl.multiple_of(PART * (spot ^ (2 * q + odd)), 8)
            target[PART * q : PART * (q + 1), :] = terms[pl.ds(start, PART), :]


def forward_kernel(dense_ref, weight_ref, near_ref, far_ref, keep_ref, send_ref, sums):
    chan = lax.axis_index("ch")
    sums[...] = lax.dot_general(
        weight_ref[...], dense_ref[...], (((0,), (0,)), ((), ())),
        preferred_element_type=jnp.float32,
    )
    for target, parts in ((keep_ref, (0, 3)), (send_ref, (1, 2))):
        for i, m in enumerate(parts):
            rows = pl.ds(pl.multiple_of(32 * (chan ^ m), 32), 32)
            target[32 * i : 32 * i + 32, :VOX] = sums[rows, :]
    lower, upper = by_side(near_ref[32:, :], far_ref[32:, :])
    send_ref[:32, VOX:] = lower
    send_ref[32:, VOX:] = upper


def middle_kernel(keep_ref, came_ref, near_ref, far_ref, own_ref, send_ref):
    own_ref[...] = keep_ref[:32, :] + came_ref[:32, :VOX]
    send_ref[:, :VOX] = keep_ref[32:, :] + came_ref[32:, :VOX]
    lower, upper = by_side(near_ref[32:, :], far_ref[32:, :])
    send_ref[:, VOX : VOX + FACE] = lower
    send_ref[:, VOX + FACE : VOX + 2 * FACE] = upper
    send_ref[:, VOX + 2 * FACE : VOX + 3 * FACE] = came_ref[:32, VOX:]
    send_ref[:, VOX + 3 * FACE :] = came_ref[32:, VOX:]


def back_terms_kernel(weight_ref, grad_ref, terms_ref):
    terms_ref[...] = jnp.dot(
        weight_ref[...], grad_ref[...], preferred_element_type=jnp.float32
    )


def back_sum(groups, rule_ref, load):
    totals = {}
    for k in range(27):
        row = rule_ref[k : k + 1, :]
        rows = slice(32 * (26 - k), 32 * (26 - k) + 32)
        for group in groups:
            got = picked(row, group, source_tiles(group, k % 3 - 1), lambda t: load(rows, t))
            totals[group] = got if k == 0 else totals[group] + got
    return totals


def back_inner_kernel(groups, terms, rule_ref, *refs):
    totals = back_sum(groups, rule_ref, lambda rows, t: terms[rows, tile_span(t)])
    for group in groups:
        refs[-1][:, tile_span(group)] = totals[group]


def edge_kernel(
    terms, rule_ref, weight_ref, near_ref, far_ref, inner, own_ref, first_ref, second_ref,
    out_ref, grad_ref, faces, products,
):
    chan = lax.axis_index("ch")
    out_ref[...] = (own_ref[...] + second_ref[:, :VOX]).astype(jnp.bfloat16)
    lower, upper = by_side(near_ref[32:, :], far_ref[32:, :])
    pairs = (
        (lower, upper),
        (first_ref[:32, VOX:], first_ref[32:, VOX:]),
        (second_ref[:, VOX : VOX + FACE], second_ref[:, VOX + FACE : VOX + 2 * FACE]),
        (second_ref[:, VOX + 2 * FACE : VOX + 3 * FACE], second_ref[:, VOX + 3 * FACE :]),
    )
    for m, (lower, upper) in zip(ORDER, pairs):
        rows = pl.ds(pl.multiple_of(32 * (chan ^ m), 32), 32)
        faces[rows, :FACE] = lower.astype(jnp.bfloat16)
        faces[rows, FACE:] = upper.astype(jnp.bfloat16)
    products[...] = jnp.dot(
        weight_ref[...], faces[...], preferred_element_type=jnp.float32
    )
    totals = back_sum(
        EDGE, rule_ref,
        lambda rows, t: products[rows, tile_span(t - 8)] if t >= 8 else terms[rows, tile_span(t)],
    )
    for group in range(8):
        values = totals[group] if group in EDGE else inner[:, tile_span(group)]
        grad_ref[:, tile_span(group)] = values.astype(jnp.bfloat16)


def split_sum_kernel(keep_ref, came_ref, *outs):
    for q, out in enumerate(outs):
        rows = slice(PART * q, PART * (q + 1))
        out[...] = keep_ref[rows, :] + came_ref[rows, :]


def sum_kernel(*refs):
    values = [ref[...] for ref in refs[:-1]]
    while len(values) > 1:
        values = [values[i] + values[i + 1] for i in range(0, len(values), 2)]
    refs[-1][...] = values[0]


def join_kernel(*refs):
    size = refs[0].shape[0]
    for q, ref in enumerate(refs[:-1]):
        refs[-1][size * q : size * (q + 1), :] = ref[...]


def place_kernel(*refs):
    out_ref, held = refs[-2:]
    spot = lax.axis_index("blk") & 7
    for q in range(4):
        held[2 * PART * q : 2 * PART * (q + 1), :] = refs[q][...]
    for p in range(8):
        count = min(PART, 864 - PART * p)
        start = pl.multiple_of(PART * (spot ^ p), 8)
        out_ref[PART * p : PART * p + count, :] = held[pl.ds(start, count), :]


def call(kernel, outs, args, scratch=(), aliases=None, flops=0, name=None):
    moved = sum(a.size * a.dtype.itemsize for a in list(args) + jax.tree.leaves(outs))
    return pl.pallas_call(
        kernel,
        out_shape=outs,
        in_specs=[VMEM] * len(args),
        out_specs=jax.tree.map(lambda _: VMEM, outs),
        scratch_shapes=list(scratch),
        input_output_aliases=aliases or {},
        compiler_params=pltpu.CompilerParams(vmem_limit_bytes=40 << 20),
        cost_estimate=pl.CostEstimate(flops=flops, bytes_accessed=moved, transcendentals=0),
        name=name,
    )(*args)


def f32(*shape):
    return jax.ShapeDtypeStruct(shape, jnp.float32)


def bf16(*shape):
    return jax.ShapeDtypeStruct(shape, jnp.bfloat16)


def swap(value, mask):
    count = lax.axis_size("blk")
    return lax.ppermute(value, "blk", [(i, i ^ mask) for i in range(count)])


def swap_far(value):
    count = lax.axis_size("blk")
    pairs = [(i, (i + 1 if i % 2 else i - 1) % count) for i in range(count)]
    return lax.ppermute(value, "blk", pairs)


def after(values, *others):
    return lax.optimization_barrier((*values, *others))[: len(values)]


def per_device(features, weight, grad_out, rulebook):
    weights = weight.reshape(864, 128)

    def over_ch(value, mask):
        return lax.ppermute(value, "ch", [(i, i ^ mask) for i in range(4)])

    x, g, rules = features, grad_out, rulebook
    near, far = call(
        faces_kernel, (bf16(64, FACE),) * 2, (x, g), flops=1 << 30, name="faces"
    )
    pair = call(join_kernel, bf16(64, VOX), (g, over_ch(g, 1)), name="join")
    near = swap(near, 1)
    far = swap_far(far)
    other = over_ch(pair, 3)
    dense = call(
        gather_kernel, bf16(864, VOX), (x, rules),
        [pltpu.VMEM((32, VOX), jnp.float32)], flops=3 << 30, name="gather",
    )
    dense, grads, keep, send = call(
        weight_kernel,
        (bf16(864, VOX), bf16(128, VOX), f32(4 * PART, 128), f32(4 * PART, 128)),
        (dense, rules, near, far, pair, other),
        [pltpu.VMEM((32, 2 * FACE), jnp.float32), pltpu.VMEM((8 * PART, 128), jnp.float32)],
        aliases={0: 0}, flops=1 << 30, name="weight_terms",
    )

    def inner_part(groups, inner=None):
        args = (back, rules) if inner is None else (back, rules, inner)
        return call(
            functools.partial(back_inner_kernel, groups), f32(32, VOX), args,
            aliases=None if inner is None else {2: 0}, flops=len(groups) << 30,
            name="back_inner",
        )

    came = swap(send, 1)
    ours, first = call(
        forward_kernel, (f32(64, VOX), f32(64, VOX + FACE)), (dense, weights, near, far),
        [pltpu.VMEM((128, VOX), jnp.float32)], flops=1 << 30, name="forward",
    )
    back = call(
        back_terms_kernel, f32(864, VOX), (weights, grads), flops=1 << 30, name="back_terms"
    )
    came, = after((came,), ours, back)
    pieces = call(split_sum_kernel, (f32(PART, 128),) * 4, (keep, came), name="sum_pair")
    others = [swap(pieces[q], 2 * q) for q in (1, 2, 3)]
    first, = after((first,), *pieces)
    first = over_ch(first, 1)
    inner = inner_part((2, 3))
    others = after(others, inner)
    total = call(sum_kernel, f32(PART, 128), (pieces[0], *others), name="sum_four")
    came = swap(total, 8)
    inner = inner_part((4, 5), inner)
    came, = after((came,), inner)
    total = call(sum_kernel, f32(PART, 128), (total, came), name="sum_two")
    others = [swap(total, m) for m in (16, 32, 48)]
    ours, first = after((ours, first), total)
    own, second = call(
        middle_kernel, (f32(32, VOX), f32(32, VOX + 4 * FACE)), (ours, first, near, far),
        name="middle",
    )
    second = over_ch(second, 3)
    others = after(others, own)
    total = call(sum_kernel, f32(PART, 128), (total, *others), name="sum_four")
    both = call(join_kernel, f32(2 * PART, 128), (total, swap(total, 1)), name="join")
    others = [swap(both, 2 * q) for q in (1, 2, 3)]
    output, grad_features = call(
        edge_kernel, (bf16(32, VOX), bf16(32, VOX)),
        (back, rules, weights, near, far, inner, own, first, second),
        [pltpu.VMEM((128, 2 * FACE), jnp.bfloat16), pltpu.VMEM((864, 2 * FACE), jnp.float32)],
        flops=2 << 30, name="edge",
    )
    others = after(others, output)
    weight_grad = call(
        place_kernel, f32(864, 128), (both, *others),
        [pltpu.VMEM((8 * PART, 128), jnp.float32)], name="place",
    )
    return output, grad_features, weight_grad.reshape(27, 32, 128)


def solution(mesh):
    placed = (P("ch", "blk"), P(None, "ch", None), P("ch", "blk"), P(None, "blk"))
    return jax.shard_map(
        per_device,
        mesh=mesh,
        in_specs=placed,
        out_specs=(P("ch", "blk"), P("ch", "blk"), P(None, "ch", None)),
        check_vma=False,
    )
```

```python
import functools

import jax
import jax.numpy as jnp
from jax import lax
from jax.experimental import pallas as pl
from jax.experimental.pallas import tpu as pltpu
from jax.sharding import PartitionSpec as P

VOX = 1024
FACE = 128
LANES = 128
PART = 112
INNER = tuple(range(2, 8))
EDGE = (0, 1)
ORDER = (0, 1, 3, 2)
VMEM = pl.BlockSpec(memory_space=pltpu.VMEM)


def source_tiles(group, dz):
    if group == 0:
        return {-1: (8,), 0: (0,), 1: INNER}[dz]
    if group == 1:
        return {-1: INNER, 0: (1,), 1: (9,)}[dz]
    return {-1: (0,) + INNER, 0: INNER, 1: (1,) + INNER}[dz]


def picked(row, group, tiles, load):
    span = row[:, LANES * group : LANES * (group + 1)]
    index = jnp.broadcast_to(span, (32, LANES))
    lane = index & (LANES - 1)
    tile = index >> 7
    total = jnp.zeros((32, LANES), jnp.float32)
    for t in tiles:
        values = jnp.take_along_axis(load(t), lane, axis=1, mode="promise_in_bounds")
        total = jnp.where(tile == t, values, total)
    return total


def tile_span(t):
    return slice(LANES * t, LANES * (t + 1))


def faces_kernel(x_ref, g_ref, near_ref, far_ref):
    odd = (lax.axis_index("blk") & 1) == 1
    for rows, ref in ((slice(0, 32), x_ref), (slice(32, 64), g_ref)):
        lowest = ref[:, :FACE].astype(jnp.float32)
        highest = ref[:, FACE : 2 * FACE].astype(jnp.float32)
        near_ref[rows, :] = jnp.where(odd, lowest, highest).astype(jnp.bfloat16)
        far_ref[rows, :] = jnp.where(odd, highest, lowest).astype(jnp.bfloat16)


def by_side(near, far):
    odd = (lax.axis_index("blk") & 1) == 1
    near = near.astype(jnp.float32)
    far = far.astype(jnp.float32)
    return jnp.where(odd, near, far), jnp.where(odd, far, near)


def gather_kernel(x_ref, rule_ref, dense_ref, table):
    table[...] = x_ref[...].astype(jnp.float32)
    for k in range(27):
        row = rule_ref[k : k + 1, :]
        for group in range(8):
            tiles = source_tiles(group, k % 3 - 1)
            if tiles[0] >= 8:
                continue
            got = picked(row, group, tiles, lambda t: table[:, tile_span(t)])
            dense_ref[32 * k : 32 * k + 32, tile_span(group)] = got.astype(jnp.bfloat16)


def faces_kernel(x_ref, g_ref, near_ref, far_ref):
    odd = (lax.axis_index("blk") & 1) == 1
    for rows, ref in ((slice(0, 32), x_ref), (slice(32, 64), g_ref)):
        lowest = ref[:, :FACE].astype(jnp.float32)
        highest = ref[:, FACE : 2 * FACE].astype(jnp.float32)
        near_ref[rows, :] = jnp.where(odd, lowest, highest).astype(jnp.bfloat16)
        far_ref[rows, :] = jnp.where(odd, highest, lowest).astype(jnp.bfloat16)


def by_side(near, far):
    odd = (lax.axis_index("blk") & 1) == 1
    near = near.astype(jnp.float32)
    far = far.astype(jnp.float32)
    return jnp.where(odd, near, far), jnp.where(odd, far, near)


def gather_kernel(x_ref, rule_ref, dense_ref, table):
    table[...] = x_ref[...].astype(jnp.float32)

    def step(j, carry):
        for d in range(3):
            k = 3 * j + d
            row = rule_ref[pl.ds(k, 1), :]
            for group in range(8):
                tiles = source_tiles(group, d - 1)
                if tiles[0] >= 8:
                    continue
                got = picked(row, group, tiles, lambda t: table[:, tile_span(t)])
                rows = pl.ds(pl.multiple_of(32 * k, 32), 32)
                dense_ref[rows, tile_span(group)] = got.astype(jnp.bfloat16)
        return carry

    lax.fori_loop(0, 9, step, 0)


def weight_kernel(
    dense_in, rule_ref, near_ref, far_ref, pair_ref, other_ref,
    dense_ref, grad_ref, keep_ref, send_ref, faces, terms,
):
    chan = lax.axis_index("ch")
    spot = lax.axis_index("blk") & 7
    for i, m in enumerate(ORDER):
        part = (pair_ref if i < 2 else other_ref)[32 * (i % 2) : 32 * (i % 2) + 32, :]
        grad_ref[pl.ds(pl.multiple_of(32 * (chan ^ m), 32), 32), :] = part
    faces[:, :FACE], faces[:, FACE:] = by_side(near_ref[:32, :], far_ref[:32, :])

    for j in range(9):
        for group, d in ((0, 0), (1, 2)):
            k = 3 * j + d
            row = rule_ref[k : k + 1, :]
            got = picked(row, group, (8 + group,), lambda t: faces[:, tile_span(t - 8)])
            dense_ref[32 * k : 32 * k + 32, tile_span(group)] = got.astype(jnp.bfloat16)
    terms[:864, :] = lax.dot_general(
        dense_ref[...], grad_ref[...], (((1,), (1,)), ((), ())),
        preferred_element_type=jnp.float32,
    ) * (1.0 / 256.0)
    terms[864:, :] = jnp.zeros((32, LANES), jnp.float32)
    for q in range(4):
        for odd, target in ((0, keep_ref), (1, send_ref)):
            start = pl.multiple_of(PART * (spot ^ (2 * q + odd)), 8)
            target[PART * q : PART * (q + 1), :] = terms[pl.ds(start, PART), :]


def forward_kernel(dense_ref, weight_ref, near_ref, far_ref, keep_ref, send_ref, sums):
    chan = lax.axis_index("ch")
    sums[...] = lax.dot_general(
        weight_ref[...], dense_ref[...], (((0,), (0,)), ((), ())),
        preferred_element_type=jnp.float32,
    )
    for target, parts in ((keep_ref, (0, 3)), (send_ref, (1, 2))):
        for i, m in enumerate(parts):
            rows = pl.ds(pl.multiple_of(32 * (chan ^ m), 32), 32)
            target[32 * i : 32 * i + 32, :VOX] = sums[rows, :]
    lower, upper = by_side(near_ref[32:, :], far_ref[32:, :])
    send_ref[:32, VOX:] = lower
    send_ref[32:, VOX:] = upper


def middle_kernel(keep_ref, came_ref, near_ref, far_ref, own_ref, send_ref):
    own_ref[...] = keep_ref[:32, :] + came_ref[:32, :VOX]
    send_ref[:, :VOX] = keep_ref[32:, :] + came_ref[32:, :VOX]
    lower, upper = by_side(near_ref[32:, :], far_ref[32:, :])
    send_ref[:, VOX : VOX + FACE] = lower
    send_ref[:, VOX + FACE : VOX + 2 * FACE] = upper
    send_ref[:, VOX + 2 * FACE : VOX + 3 * FACE] = came_ref[:32, VOX:]
    send_ref[:, VOX + 3 * FACE :] = came_ref[32:, VOX:]


def back_terms_kernel(weight_ref, grad_ref, terms_ref):
    terms_ref[...] = jnp.dot(
        weight_ref[...], grad_ref[...], preferred_element_type=jnp.float32
    )


def back_sum(groups, rule_ref, load):
    totals = {}
    for k in range(27):
        row = rule_ref[k : k + 1, :]
        rows = slice(32 * (26 - k), 32 * (26 - k) + 32)
        for group in groups:
            got = picked(row, group, source_tiles(group, k % 3 - 1), lambda t: load(rows, t))
            totals[group] = got if k == 0 else totals[group] + got
    return totals


def back_inner_kernel(groups, terms, rule_ref, *refs):
    totals = back_sum(groups, rule_ref, lambda rows, t: terms[rows, tile_span(t)])
    for group in groups:
        refs[-1][:, tile_span(group)] = totals[group]


def edge_kernel(
    terms, rule_ref, weight_ref, near_ref, far_ref, inner, own_ref, first_ref, second_ref,
    out_ref, grad_ref, faces, products,
):
    chan = lax.axis_index("ch")
    out_ref[...] = (own_ref[...] + second_ref[:, :VOX]).astype(jnp.bfloat16)
    lower, upper = by_side(near_ref[32:, :], far_ref[32:, :])
    pairs = (
        (lower, upper),
        (first_ref[:32, VOX:], first_ref[32:, VOX:]),
        (second_ref[:, VOX : VOX + FACE], second_ref[:, VOX + FACE : VOX + 2 * FACE]),
        (second_ref[:, VOX + 2 * FACE : VOX + 3 * FACE], second_ref[:, VOX + 3 * FACE :]),
    )
    for m, (lower, upper) in zip(ORDER, pairs):
        rows = pl.ds(pl.multiple_of(32 * (chan ^ m), 32), 32)
        faces[rows, :FACE] = lower.astype(jnp.bfloat16)
        faces[rows, FACE:] = upper.astype(jnp.bfloat16)
    products[...] = jnp.dot(
        weight_ref[...], faces[...], preferred_element_type=jnp.float32
    )
    totals = back_sum(
        EDGE, rule_ref,
        lambda rows, t: products[rows, tile_span(t - 8)] if t >= 8 else terms[rows, tile_span(t)],
    )
    for group in range(8):
        values = totals[group] if group in EDGE else inner[:, tile_span(group)]
        grad_ref[:, tile_span(group)] = values.astype(jnp.bfloat16)


def split_sum_kernel(keep_ref, came_ref, *outs):
    for q, out in enumerate(outs):
        rows = slice(PART * q, PART * (q + 1))
        out[...] = keep_ref[rows, :] + came_ref[rows, :]


def sum_kernel(*refs):
    values = [ref[...] for ref in refs[:-1]]
    while len(values) > 1:
        values = [values[i] + values[i + 1] for i in range(0, len(values), 2)]
    refs[-1][...] = values[0]


def join_kernel(*refs):
    size = refs[0].shape[0]
    for q, ref in enumerate(refs[:-1]):
        refs[-1][size * q : size * (q + 1), :] = ref[...]


def place_kernel(even_ref, odd_ref, out_ref, held):
    spot = lax.axis_index("blk") & 7
    for q in range(4):
        for odd, ref in enumerate((even_ref, odd_ref)):
            start = PART * (2 * q + odd)
            held[start : start + PART, :] = ref[PART * q : PART * (q + 1), :]
    for p in range(8):
        count = min(PART, 864 - PART * p)
        start = pl.multiple_of(PART * (spot ^ p), 8)
        out_ref[PART * p : PART * p + count, :] = held[pl.ds(start, count), :]


def call(kernel, outs, args, scratch=(), aliases=None, flops=0, name=None):
    moved = sum(a.size * a.dtype.itemsize for a in list(args) + jax.tree.leaves(outs))
    return pl.pallas_call(
        kernel,
        out_shape=outs,
        in_specs=[VMEM] * len(args),
        out_specs=jax.tree.map(lambda _: VMEM, outs),
        scratch_shapes=list(scratch),
        input_output_aliases=aliases or {},
        compiler_params=pltpu.CompilerParams(vmem_limit_bytes=40 << 20),
        cost_estimate=pl.CostEstimate(flops=flops, bytes_accessed=moved, transcendentals=0),
        name=name,
    )(*args)


def f32(*shape):
    return jax.ShapeDtypeStruct(shape, jnp.float32)


def bf16(*shape):
    return jax.ShapeDtypeStruct(shape, jnp.bfloat16)


def swap(value, mask):
    count = lax.axis_size("blk")
    return lax.ppermute(value, "blk", [(i, i ^ mask) for i in range(count)])


def swap_far(value):
    count = lax.axis_size("blk")
    pairs = [(i, (i + 1 if i % 2 else i - 1) % count) for i in range(count)]
    return lax.ppermute(value, "blk", pairs)


def after(values, *others):
    return lax.optimization_barrier((*values, *others))[: len(values)]


def per_device(features, weight, grad_out, rulebook):
    weights = weight.reshape(864, 128)

    def over_ch(value, mask):
        return lax.ppermute(value, "ch", [(i, i ^ mask) for i in range(4)])

    x, g, rules = features, grad_out, rulebook
    near, far = call(
        faces_kernel, (bf16(64, FACE),) * 2, (x, g), flops=1 << 30, name="faces"
    )
    pair = call(join_kernel, bf16(64, VOX), (g, over_ch(g, 1)), name="join")
    near = swap(near, 1)
    far = swap_far(far)
    other = over_ch(pair, 3)
    dense = call(
        gather_kernel, bf16(864, VOX), (x, rules),
        [pltpu.VMEM((32, VOX), jnp.float32)], flops=3 << 30, name="gather",
    )
    dense, grads, keep, send = call(
        weight_kernel,
        (bf16(864, VOX), bf16(128, VOX), f32(4 * PART, 128), f32(4 * PART, 128)),
        (dense, rules, near, far, pair, other),
        [pltpu.VMEM((32, 2 * FACE), jnp.float32), pltpu.VMEM((8 * PART, 128), jnp.float32)],
        aliases={0: 0}, flops=1 << 30, name="weight_terms",
    )

    def inner_part(groups, inner=None):
        args = (back, rules) if inner is None else (back, rules, inner)
        return call(
            functools.partial(back_inner_kernel, groups), f32(32, VOX), args,
            aliases=None if inner is None else {2: 0}, flops=len(groups) << 30,
            name="back_inner",
        )

    came = swap(send, 1)
    ours, first = call(
        forward_kernel, (f32(64, VOX), f32(64, VOX + FACE)), (dense, weights, near, far),
        [pltpu.VMEM((128, VOX), jnp.float32)], flops=1 << 30, name="forward",
    )
    back = call(
        back_terms_kernel, f32(864, VOX), (weights, grads), flops=1 << 30, name="back_terms"
    )
    came, = after((came,), ours, back)
    pieces = call(split_sum_kernel, (f32(PART, 128),) * 4, (keep, came), name="sum_pair")
    others = [swap(pieces[q], 2 * q) for q in (1, 2, 3)]
    first, = after((first,), *pieces)
    first = over_ch(first, 1)
    inner = inner_part((2, 3))
    others = after(others, inner)
    total = call(sum_kernel, f32(PART, 128), (pieces[0], *others), name="sum_four")
    came = swap(total, 8)
    inner = inner_part((4, 5), inner)
    came, = after((came,), inner)
    total = call(sum_kernel, f32(PART, 128), (total, came), name="sum_two")
    others = [swap(total, m) for m in (16, 32, 48)]
    ours, first = after((ours, first), total)
    own, second = call(
        middle_kernel, (f32(32, VOX), f32(32, VOX + 4 * FACE)), (ours, first, near, far),
        name="middle",
    )
    second = over_ch(second, 3)
    inner = inner_part((6, 7), inner)
    others = after(others, inner, own)
    total = call(sum_kernel, f32(PART, 128), (total, *others), name="sum_four")
    others = [swap(total, 2 * q) for q in (1, 2, 3)]
    output, grad_features = call(
        edge_kernel, (bf16(32, VOX), bf16(32, VOX)),
        (back, rules, weights, near, far, inner, own, first, second),
        [pltpu.VMEM((128, 2 * FACE), jnp.bfloat16), pltpu.VMEM((864, 2 * FACE), jnp.float32)],
        flops=2 << 30, name="edge",
    )
    others = after(others, output)
    even = call(join_kernel, f32(4 * PART, 128), (total, *others), name="join")
    odd = swap(even, 1)
    weight_grad = call(
        place_kernel, f32(864, 128), (even, odd),
        [pltpu.VMEM((8 * PART, 128), jnp.float32)], name="place",
    )
    return output, grad_features, weight_grad.reshape(27, 32, 128)


def solution(mesh):
    placed = (P("ch", "blk"), P(None, "ch", None), P("ch", "blk"), P(None, "blk"))
    return jax.shard_map(
        per_device,
        mesh=mesh,
        in_specs=placed,
        out_specs=(P("ch", "blk"), P("ch", "blk"), P(None, "ch", None)),
        check_vma=False,
    )
```

```python
import functools

import jax
import jax.numpy as jnp
from jax import lax
from jax.experimental import pallas as pl
from jax.experimental.pallas import tpu as pltpu
from jax.sharding import PartitionSpec as P

VOX = 1024
FACE = 128
LANES = 128
PART = 112
INNER = tuple(range(2, 8))
EDGE = (0, 1, 3)
ORDER = (0, 1, 3, 2)
VMEM = pl.BlockSpec(memory_space=pltpu.VMEM)


def source_tiles(group, dz):
    if group == 0:
        return {-1: (8,), 0: (0,), 1: INNER}[dz]
    if group == 1:
        return {-1: INNER, 0: (1,), 1: (9,)}[dz]
    return {-1: (0,) + INNER, 0: INNER, 1: (1,) + INNER}[dz]


def picked(row, group, tiles, load):
    span = row[:, LANES * group : LANES * (group + 1)]
    index = jnp.broadcast_to(span, (32, LANES))
    lane = index & (LANES - 1)
    tile = index >> 7
    total = jnp.zeros((32, LANES), jnp.float32)
    for t in tiles:
        values = jnp.take_along_axis(load(t), lane, axis=1, mode="promise_in_bounds")
        total = jnp.where(tile == t, values, total)
    return total


def tile_span(t):
    return slice(LANES * t, LANES * (t + 1))


def faces_kernel(x_ref, g_ref, near_ref, far_ref):
    odd = (lax.axis_index("blk") & 1) == 1
    for rows, ref in ((slice(0, 32), x_ref), (slice(32, 64), g_ref)):
        lowest = ref[:, :FACE].astype(jnp.float32)
        highest = ref[:, FACE : 2 * FACE].astype(jnp.float32)
        near_ref[rows, :] = jnp.where(odd, lowest, highest).astype(jnp.bfloat16)
        far_ref[rows, :] = jnp.where(odd, highest, lowest).astype(jnp.bfloat16)


def by_side(near, far):
    odd = (lax.axis_index("blk") & 1) == 1
    near = near.astype(jnp.float32)
    far = far.astype(jnp.float32)
    return jnp.where(odd, near, far), jnp.where(odd, far, near)


def gather_kernel(x_ref, rule_ref, dense_ref, table):
    table[...] = x_ref[...].astype(jnp.float32)
    for k in range(27):
        row = rule_ref[k : k + 1, :]
        for group in range(8):
            tiles = source_tiles(group, k % 3 - 1)
            if tiles[0] >= 8:
                continue
            got = picked(row, group, tiles, lambda t: table[:, tile_span(t)])
            dense_ref[32 * k : 32 * k + 32, tile_span(group)] = got.astype(jnp.bfloat16)


def faces_kernel(x_ref, g_ref, near_ref, far_ref):
    odd = (lax.axis_index("blk") & 1) == 1
    for rows, ref in ((slice(0, 32), x_ref), (slice(32, 64), g_ref)):
        lowest = ref[:, :FACE].astype(jnp.float32)
        highest = ref[:, FACE : 2 * FACE].astype(jnp.float32)
        near_ref[rows, :] = jnp.where(odd, lowest, highest).astype(jnp.bfloat16)
        far_ref[rows, :] = jnp.where(odd, highest, lowest).astype(jnp.bfloat16)


def by_side(near, far):
    odd = (lax.axis_index("blk") & 1) == 1
    near = near.astype(jnp.float32)
    far = far.astype(jnp.float32)
    return jnp.where(odd, near, far), jnp.where(odd, far, near)


def gather_kernel(x_ref, rule_ref, dense_ref, table):
    table[...] = x_ref[...].astype(jnp.float32)

    def step(j, carry):
        for d in range(3):
            k = 3 * j + d
            row = rule_ref[pl.ds(k, 1), :]
            for group in range(8):
                tiles = source_tiles(group, d - 1)
                if tiles[0] >= 8:
                    continue
                got = picked(row, group, tiles, lambda t: table[:, tile_span(t)])
                rows = pl.ds(pl.multiple_of(32 * k, 32), 32)
                dense_ref[rows, tile_span(group)] = got.astype(jnp.bfloat16)
        return carry

    lax.fori_loop(0, 9, step, 0)


def weight_kernel(
    dense_in, rule_ref, near_ref, far_ref, pair_ref, other_ref,
    dense_ref, grad_ref, keep_ref, send_ref, faces, terms,
):
    chan = lax.axis_index("ch")
    spot = lax.axis_index("blk") & 7
    for i, m in enumerate(ORDER):
        part = (pair_ref if i < 2 else other_ref)[32 * (i % 2) : 32 * (i % 2) + 32, :]
        grad_ref[pl.ds(pl.multiple_of(32 * (chan ^ m), 32), 32), :] = part
    faces[:, :FACE], faces[:, FACE:] = by_side(near_ref[:32, :], far_ref[:32, :])

    for j in range(9):
        for group, d in ((0, 0), (1, 2)):
            k = 3 * j + d
            row = rule_ref[k : k + 1, :]
            got = picked(row, group, (8 + group,), lambda t: faces[:, tile_span(t - 8)])
            dense_ref[32 * k : 32 * k + 32, tile_span(group)] = got.astype(jnp.bfloat16)
    terms[:864, :] = lax.dot_general(
        dense_ref[...], grad_ref[...], (((1,), (1,)), ((), ())),
        preferred_element_type=jnp.float32,
    ) * (1.0 / 256.0)
    terms[864:, :] = jnp.zeros((32, LANES), jnp.float32)
    for q in range(4):
        for odd, target in ((0, keep_ref), (1, send_ref)):
            start = pl.multiple_of(PART * (spot ^ (2 * q + odd)), 8)
            target[PART * q : PART * (q + 1), :] = terms[pl.ds(start, PART), :]


def forward_kernel(dense_ref, weight_ref, near_ref, far_ref, keep_ref, send_ref, sums):
    chan = lax.axis_index("ch")
    sums[...] = lax.dot_general(
        weight_ref[...], dense_ref[...], (((0,), (0,)), ((), ())),
        preferred_element_type=jnp.float32,
    )
    for target, parts in ((keep_ref, (0, 3)), (send_ref, (1, 2))):
        for i, m in enumerate(parts):
            rows = pl.ds(pl.multiple_of(32 * (chan ^ m), 32), 32)
            target[32 * i : 32 * i + 32, :VOX] = sums[rows, :]
    lower, upper = by_side(near_ref[32:, :], far_ref[32:, :])
    send_ref[:32, VOX:] = lower
    send_ref[32:, VOX:] = upper


def middle_kernel(keep_ref, came_ref, near_ref, far_ref, own_ref, send_ref):
    own_ref[...] = keep_ref[:32, :] + came_ref[:32, :VOX]
    send_ref[:, :VOX] = keep_ref[32:, :] + came_ref[32:, :VOX]
    lower, upper = by_side(near_ref[32:, :], far_ref[32:, :])
    send_ref[:, VOX : VOX + FACE] = lower
    send_ref[:, VOX + FACE : VOX + 2 * FACE] = upper
    send_ref[:, VOX + 2 * FACE : VOX + 3 * FACE] = came_ref[:32, VOX:]
    send_ref[:, VOX + 3 * FACE :] = came_ref[32:, VOX:]


def back_terms_kernel(weight_ref, grad_ref, terms_ref):
    terms_ref[...] = jnp.dot(
        weight_ref[...], grad_ref[...], preferred_element_type=jnp.float32
    )


def back_sum(groups, rule_ref, load):
    totals = {}
    for k in range(27):
        row = rule_ref[k : k + 1, :]
        rows = slice(32 * (26 - k), 32 * (26 - k) + 32)
        for group in groups:
            got = picked(row, group, source_tiles(group, k % 3 - 1), lambda t: load(rows, t))
            totals[group] = got if k == 0 else totals[group] + got
    return totals


def back_inner_kernel(groups, terms, rule_ref, *refs):
    totals = back_sum(groups, rule_ref, lambda rows, t: terms[rows, tile_span(t)])
    for group in groups:
        refs[-1][:, tile_span(group)] = totals[group]


def edge_kernel(
    terms, rule_ref, weight_ref, near_ref, far_ref, inner, own_ref, first_ref, second_ref,
    out_ref, grad_ref, faces, products,
):
    chan = lax.axis_index("ch")
    out_ref[...] = (own_ref[...] + second_ref[:, :VOX]).astype(jnp.bfloat16)
    lower, upper = by_side(near_ref[32:, :], far_ref[32:, :])
    pairs = (
        (lower, upper),
        (first_ref[:32, VOX:], first_ref[32:, VOX:]),
        (second_ref[:, VOX : VOX + FACE], second_ref[:, VOX + FACE : VOX + 2 * FACE]),
        (second_ref[:, VOX + 2 * FACE : VOX + 3 * FACE], second_ref[:, VOX + 3 * FACE :]),
    )
    for m, (lower, upper) in zip(ORDER, pairs):
        rows = pl.ds(pl.multiple_of(32 * (chan ^ m), 32), 32)
        faces[rows, :FACE] = lower.astype(jnp.bfloat16)
        faces[rows, FACE:] = upper.astype(jnp.bfloat16)
    products[...] = jnp.dot(
        weight_ref[...], faces[...], preferred_element_type=jnp.float32
    )
    totals = back_sum(
        EDGE, rule_ref,
        lambda rows, t: products[rows, tile_span(t - 8)] if t >= 8 else terms[rows, tile_span(t)],
    )
    for group in range(8):
        values = totals[group] if group in EDGE else inner[:, tile_span(group)]
        grad_ref[:, tile_span(group)] = values.astype(jnp.bfloat16)


def split_sum_kernel(keep_ref, came_ref, *outs):
    for q, out in enumerate(outs):
        rows = slice(PART * q, PART * (q + 1))
        out[...] = keep_ref[rows, :] + came_ref[rows, :]


def sum_kernel(*refs):
    values = [ref[...] for ref in refs[:-1]]
    while len(values) > 1:
        values = [values[i] + values[i + 1] for i in range(0, len(values), 2)]
    refs[-1][...] = values[0]


def join_kernel(*refs):
    size = refs[0].shape[0]
    for q, ref in enumerate(refs[:-1]):
        refs[-1][size * q : size * (q + 1), :] = ref[...]


def place_kernel(even_ref, odd_ref, out_ref):
    spot = lax.axis_index("blk") & 7
    short = 864 - 7 * PART
    for q in range(4):
        for odd, ref in enumerate((even_ref, odd_ref)):
            part = spot ^ (2 * q + odd)
            start = pl.multiple_of(PART * part, 8)
            out_ref[pl.ds(start, short), :] = ref[PART * q : PART * q + short, :]

            @pl.when(part < 7)
            def _():
                rows = pl.ds(pl.multiple_of(start + short, 8), PART - short)
                out_ref[rows, :] = ref[PART * q + short : PART * (q + 1), :]


def call(kernel, outs, args, scratch=(), aliases=None, flops=0, name=None):
    moved = sum(a.size * a.dtype.itemsize for a in list(args) + jax.tree.leaves(outs))
    return pl.pallas_call(
        kernel,
        out_shape=outs,
        in_specs=[VMEM] * len(args),
        out_specs=jax.tree.map(lambda _: VMEM, outs),
        scratch_shapes=list(scratch),
        input_output_aliases=aliases or {},
        compiler_params=pltpu.CompilerParams(vmem_limit_bytes=40 << 20),
        cost_estimate=pl.CostEstimate(flops=flops, bytes_accessed=moved, transcendentals=0),
        name=name,
    )(*args)


def f32(*shape):
    return jax.ShapeDtypeStruct(shape, jnp.float32)


def bf16(*shape):
    return jax.ShapeDtypeStruct(shape, jnp.bfloat16)


def swap(value, mask):
    count = lax.axis_size("blk")
    return lax.ppermute(value, "blk", [(i, i ^ mask) for i in range(count)])


def swap_far(value):
    count = lax.axis_size("blk")
    pairs = [(i, (i + 1 if i % 2 else i - 1) % count) for i in range(count)]
    return lax.ppermute(value, "blk", pairs)


def after(values, *others):
    return lax.optimization_barrier((*values, *others))[: len(values)]


def per_device(features, weight, grad_out, rulebook):
    weights = weight.reshape(864, 128)

    def over_ch(value, mask):
        return lax.ppermute(value, "ch", [(i, i ^ mask) for i in range(4)])

    x, g, rules = features, grad_out, rulebook
    near, far = call(
        faces_kernel, (bf16(64, FACE),) * 2, (x, g), flops=1 << 30, name="faces"
    )
    pair = call(join_kernel, bf16(64, VOX), (g, over_ch(g, 1)), name="join")
    near = swap(near, 1)
    far = swap_far(far)
    other = over_ch(pair, 3)
    dense = call(
        gather_kernel, bf16(864, VOX), (x, rules),
        [pltpu.VMEM((32, VOX), jnp.float32)], flops=3 << 30, name="gather",
    )
    dense, grads, keep, send = call(
        weight_kernel,
        (bf16(864, VOX), bf16(128, VOX), f32(4 * PART, 128), f32(4 * PART, 128)),
        (dense, rules, near, far, pair, other),
        [pltpu.VMEM((32, 2 * FACE), jnp.float32), pltpu.VMEM((8 * PART, 128), jnp.float32)],
        aliases={0: 0}, flops=1 << 30, name="weight_terms",
    )

    def inner_part(groups, inner=None):
        args = (back, rules) if inner is None else (back, rules, inner)
        return call(
            functools.partial(back_inner_kernel, groups), f32(32, VOX), args,
            aliases=None if inner is None else {2: 0}, flops=len(groups) << 30,
            name="back_inner",
        )

    came = swap(send, 1)
    ours, first = call(
        forward_kernel, (f32(64, VOX), f32(64, VOX + FACE)), (dense, weights, near, far),
        [pltpu.VMEM((128, VOX), jnp.float32)], flops=1 << 30, name="forward",
    )
    back = call(
        back_terms_kernel, f32(864, VOX), (weights, grads), flops=1 << 30, name="back_terms"
    )
    came, = after((came,), ours, back)
    pieces = call(split_sum_kernel, (f32(PART, 128),) * 4, (keep, came), name="sum_pair")
    others = [swap(pieces[q], 2 * q) for q in (1, 2, 3)]
    first, = after((first,), *pieces)
    first = over_ch(first, 1)
    inner = inner_part((2,))
    others = after(others, inner)
    total = call(sum_kernel, f32(PART, 128), (pieces[0], *others), name="sum_four")
    came = swap(total, 48)
    inner = inner_part((4, 5), inner)
    came, = after((came,), inner)
    total = call(sum_kernel, f32(PART, 128), (total, came), name="sum_two")
    others = [swap(total, m) for m in (8, 16, 24)]
    ours, first = after((ours, first), total)
    own, second = call(
        middle_kernel, (f32(32, VOX), f32(32, VOX + 4 * FACE)), (ours, first, near, far),
        name="middle",
    )
    second = over_ch(second, 3)
    inner = inner_part((6, 7), inner)
    others = after(others, inner, own)
    total = call(sum_kernel, f32(PART, 128), (total, *others), name="sum_four")
    others = [swap(total, 2 * q) for q in (1, 2, 3)]
    output, grad_features = call(
        edge_kernel, (bf16(32, VOX), bf16(32, VOX)),
        (back, rules, weights, near, far, inner, own, first, second),
        [pltpu.VMEM((128, 2 * FACE), jnp.bfloat16), pltpu.VMEM((864, 2 * FACE), jnp.float32)],
        flops=2 << 30, name="edge",
    )
    others = after(others, output)
    even = call(join_kernel, f32(4 * PART, 128), (total, *others), name="join")
    odd = swap(even, 1)
    weight_grad = call(
        place_kernel, f32(864, 128), (even, odd), name="place",
    )
    return output, grad_features, weight_grad.reshape(27, 32, 128)


def solution(mesh):
    placed = (P("ch", "blk"), P(None, "ch", None), P("ch", "blk"), P(None, "blk"))
    return jax.shard_map(
        per_device,
        mesh=mesh,
        in_specs=placed,
        out_specs=(P("ch", "blk"), P("ch", "blk"), P(None, "ch", None)),
        check_vma=False,
    )
```

```python
import functools

import jax
import jax.numpy as jnp
from jax import lax
from jax.experimental import pallas as pl
from jax.experimental.pallas import tpu as pltpu
from jax.sharding import PartitionSpec as P

VOX = 1024
FACE = 128
LANES = 128
PART = 112
INNER = tuple(range(2, 8))
EDGE = (0, 1)
ORDER = (0, 1, 3, 2)
VMEM = pl.BlockSpec(memory_space=pltpu.VMEM)


def source_tiles(group, dz):
    if group == 0:
        return {-1: (8,), 0: (0,), 1: INNER}[dz]
    if group == 1:
        return {-1: INNER, 0: (1,), 1: (9,)}[dz]
    return {-1: (0,) + INNER, 0: INNER, 1: (1,) + INNER}[dz]


def picked(row, group, tiles, load):
    span = row[:, LANES * group : LANES * (group + 1)]
    index = jnp.broadcast_to(span, (32, LANES))
    lane = index & (LANES - 1)
    tile = index >> 7
    total = jnp.zeros((32, LANES), jnp.float32)
    for t in tiles:
        values = jnp.take_along_axis(load(t), lane, axis=1, mode="promise_in_bounds")
        total = jnp.where(tile == t, values, total)
    return total


def tile_span(t):
    return slice(LANES * t, LANES * (t + 1))


def faces_kernel(x_ref, g_ref, near_ref, far_ref):
    odd = (lax.axis_index("blk") & 1) == 1
    for rows, ref in ((slice(0, 32), x_ref), (slice(32, 64), g_ref)):
        lowest = ref[:, :FACE].astype(jnp.float32)
        highest = ref[:, FACE : 2 * FACE].astype(jnp.float32)
        near_ref[rows, :] = jnp.where(odd, lowest, highest).astype(jnp.bfloat16)
        far_ref[rows, :] = jnp.where(odd, highest, lowest).astype(jnp.bfloat16)


def by_side(near, far):
    odd = (lax.axis_index("blk") & 1) == 1
    near = near.astype(jnp.float32)
    far = far.astype(jnp.float32)
    return jnp.where(odd, near, far), jnp.where(odd, far, near)


def gather_kernel(x_ref, rule_ref, dense_ref, table):
    table[...] = x_ref[...].astype(jnp.float32)
    for k in range(27):
        row = rule_ref[k : k + 1, :]
        for group in range(8):
            tiles = source_tiles(group, k % 3 - 1)
            if tiles[0] >= 8:
                continue
            got = picked(row, group, tiles, lambda t: table[:, tile_span(t)])
            dense_ref[32 * k : 32 * k + 32, tile_span(group)] = got.astype(jnp.bfloat16)


def faces_kernel(x_ref, g_ref, near_ref, far_ref):
    odd = (lax.axis_index("blk") & 1) == 1
    for rows, ref in ((slice(0, 32), x_ref), (slice(32, 64), g_ref)):
        lowest = ref[:, :FACE].astype(jnp.float32)
        highest = ref[:, FACE : 2 * FACE].astype(jnp.float32)
        near_ref[rows, :] = jnp.where(odd, lowest, highest).astype(jnp.bfloat16)
        far_ref[rows, :] = jnp.where(odd, highest, lowest).astype(jnp.bfloat16)


def by_side(near, far):
    odd = (lax.axis_index("blk") & 1) == 1
    near = near.astype(jnp.float32)
    far = far.astype(jnp.float32)
    return jnp.where(odd, near, far), jnp.where(odd, far, near)


def gather_kernel(x_ref, rule_ref, dense_ref, table):
    table[...] = x_ref[...].astype(jnp.float32)

    def step(j, carry):
        for d in range(3):
            k = 3 * j + d
            row = rule_ref[pl.ds(k, 1), :]
            for group in range(8):
                tiles = source_tiles(group, d - 1)
                if tiles[0] >= 8:
                    continue
                got = picked(row, group, tiles, lambda t: table[:, tile_span(t)])
                rows = pl.ds(pl.multiple_of(32 * k, 32), 32)
                dense_ref[rows, tile_span(group)] = got.astype(jnp.bfloat16)
        return carry

    lax.fori_loop(0, 9, step, 0)


def weight_kernel(
    dense_in, rule_ref, near_ref, far_ref, pair_ref, other_ref,
    dense_ref, grad_ref, keep_ref, send_ref, faces, terms,
):
    chan = lax.axis_index("ch")
    spot = lax.axis_index("blk") & 7
    for i, m in enumerate(ORDER):
        part = (pair_ref if i < 2 else other_ref)[32 * (i % 2) : 32 * (i % 2) + 32, :]
        grad_ref[pl.ds(pl.multiple_of(32 * (chan ^ m), 32), 32), :] = part
    faces[:, :FACE], faces[:, FACE:] = by_side(near_ref[:32, :], far_ref[:32, :])

    for j in range(9):
        for group, d in ((0, 0), (1, 2)):
            k = 3 * j + d
            row = rule_ref[k : k + 1, :]
            got = picked(row, group, (8 + group,), lambda t: faces[:, tile_span(t - 8)])
            dense_ref[32 * k : 32 * k + 32, tile_span(group)] = got.astype(jnp.bfloat16)
    terms[:864, :] = lax.dot_general(
        dense_ref[...], grad_ref[...], (((1,), (1,)), ((), ())),
        preferred_element_type=jnp.float32,
    ) * (1.0 / 256.0)
    terms[864:, :] = jnp.zeros((32, LANES), jnp.float32)
    for q in range(4):
        for odd, target in ((0, keep_ref), (1, send_ref)):
            start = pl.multiple_of(PART * (spot ^ (2 * q + odd)), 8)
            target[PART * q : PART * (q + 1), :] = terms[pl.ds(start, PART), :]


def forward_kernel(dense_ref, weight_ref, near_ref, far_ref, keep_ref, send_ref, sums):
    chan = lax.axis_index("ch")
    sums[...] = lax.dot_general(
        weight_ref[...], dense_ref[...], (((0,), (0,)), ((), ())),
        preferred_element_type=jnp.float32,
    )
    for target, parts in ((keep_ref, (0, 3)), (send_ref, (1, 2))):
        for i, m in enumerate(parts):
            rows = pl.ds(pl.multiple_of(32 * (chan ^ m), 32), 32)
            target[32 * i : 32 * i + 32, :VOX] = sums[rows, :]
    lower, upper = by_side(near_ref[32:, :], far_ref[32:, :])
    send_ref[:32, VOX:] = lower
    send_ref[32:, VOX:] = upper


def middle_kernel(keep_ref, came_ref, near_ref, far_ref, own_ref, send_ref):
    own_ref[...] = keep_ref[:32, :] + came_ref[:32, :VOX]
    send_ref[:, :VOX] = keep_ref[32:, :] + came_ref[32:, :VOX]
    lower, upper = by_side(near_ref[32:, :], far_ref[32:, :])
    send_ref[:, VOX : VOX + FACE] = lower
    send_ref[:, VOX + FACE : VOX + 2 * FACE] = upper
    send_ref[:, VOX + 2 * FACE : VOX + 3 * FACE] = came_ref[:32, VOX:]
    send_ref[:, VOX + 3 * FACE :] = came_ref[32:, VOX:]


def back_terms_kernel(weight_ref, grad_ref, terms_ref):
    terms_ref[...] = jnp.dot(
        weight_ref[...], grad_ref[...], preferred_element_type=jnp.float32
    )


def back_sum(groups, rule_ref, load):
    totals = {}
    for k in range(27):
        row = rule_ref[k : k + 1, :]
        rows = slice(32 * (26 - k), 32 * (26 - k) + 32)
        for group in groups:
            got = picked(row, group, source_tiles(group, k % 3 - 1), lambda t: load(rows, t))
            totals[group] = got if k == 0 else totals[group] + got
    return totals


def back_inner_kernel(groups, terms, rule_ref, *refs):
    totals = back_sum(groups, rule_ref, lambda rows, t: terms[rows, tile_span(t)])
    for group in groups:
        refs[-1][:, tile_span(group)] = totals[group]


def edge_kernel(
    terms, rule_ref, weight_ref, near_ref, far_ref, inner, own_ref, first_ref, second_ref,
    out_ref, grad_ref, faces, products,
):
    chan = lax.axis_index("ch")
    out_ref[...] = (own_ref[...] + second_ref[:, :VOX]).astype(jnp.bfloat16)
    lower, upper = by_side(near_ref[32:, :], far_ref[32:, :])
    pairs = (
        (lower, upper),
        (first_ref[:32, VOX:], first_ref[32:, VOX:]),
        (second_ref[:, VOX : VOX + FACE], second_ref[:, VOX + FACE : VOX + 2 * FACE]),
        (second_ref[:, VOX + 2 * FACE : VOX + 3 * FACE], second_ref[:, VOX + 3 * FACE :]),
    )
    for m, (lower, upper) in zip(ORDER, pairs):
        rows = pl.ds(pl.multiple_of(32 * (chan ^ m), 32), 32)
        faces[rows, :FACE] = lower.astype(jnp.bfloat16)
        faces[rows, FACE:] = upper.astype(jnp.bfloat16)
    products[...] = jnp.dot(
        weight_ref[...], faces[...], preferred_element_type=jnp.float32
    )
    totals = back_sum(
        EDGE, rule_ref,
        lambda rows, t: products[rows, tile_span(t - 8)] if t >= 8 else terms[rows, tile_span(t)],
    )
    for group in range(8):
        values = totals[group] if group in EDGE else inner[:, tile_span(group)]
        grad_ref[:, tile_span(group)] = values.astype(jnp.bfloat16)


def split_sum_kernel(keep_ref, came_ref, *outs):
    for q, out in enumerate(outs):
        rows = slice(PART * q, PART * (q + 1))
        out[...] = keep_ref[rows, :] + came_ref[rows, :]


def sum_kernel(*refs):
    values = [ref[...] for ref in refs[:-1]]
    while len(values) > 1:
        values = [values[i] + values[i + 1] for i in range(0, len(values), 2)]
    refs[-1][...] = values[0]


def join_kernel(*refs):
    size = refs[0].shape[0]
    for q, ref in enumerate(refs[:-1]):
        refs[-1][size * q : size * (q + 1), :] = ref[...]


def place_kernel(even_ref, odd_ref, out_ref):
    spot = lax.axis_index("blk") & 7
    short = 864 - 7 * PART
    for q in range(4):
        for odd, ref in enumerate((even_ref, odd_ref)):
            part = spot ^ (2 * q + odd)
            start = pl.multiple_of(PART * part, 8)
            out_ref[pl.ds(start, short), :] = ref[PART * q : PART * q + short, :]

            @pl.when(part < 7)
            def _():
                rows = pl.ds(pl.multiple_of(start + short, 8), PART - short)
                out_ref[rows, :] = ref[PART * q + short : PART * (q + 1), :]


def call(kernel, outs, args, scratch=(), aliases=None, flops=0, name=None):
    moved = sum(a.size * a.dtype.itemsize for a in list(args) + jax.tree.leaves(outs))
    return pl.pallas_call(
        kernel,
        out_shape=outs,
        in_specs=[VMEM] * len(args),
        out_specs=jax.tree.map(lambda _: VMEM, outs),
        scratch_shapes=list(scratch),
        input_output_aliases=aliases or {},
        compiler_params=pltpu.CompilerParams(vmem_limit_bytes=40 << 20),
        cost_estimate=pl.CostEstimate(flops=flops, bytes_accessed=moved, transcendentals=0),
        name=name,
    )(*args)


def f32(*shape):
    return jax.ShapeDtypeStruct(shape, jnp.float32)


def bf16(*shape):
    return jax.ShapeDtypeStruct(shape, jnp.bfloat16)


def swap(value, mask):
    count = lax.axis_size("blk")
    return lax.ppermute(value, "blk", [(i, i ^ mask) for i in range(count)])


def swap_far(value):
    count = lax.axis_size("blk")
    pairs = [(i, (i + 1 if i % 2 else i - 1) % count) for i in range(count)]
    return lax.ppermute(value, "blk", pairs)


def after(values, *others):
    return lax.optimization_barrier((*values, *others))[: len(values)]


def per_device(features, weight, grad_out, rulebook):
    weights = weight.reshape(864, 128)

    def over_ch(value, mask):
        return lax.ppermute(value, "ch", [(i, i ^ mask) for i in range(4)])

    x, g, rules = features, grad_out, rulebook
    cut = pl.BlockSpec((32, 2 * FACE), lambda i: (0, 0))
    face = pl.BlockSpec((64, FACE), lambda i: (0, 0))
    near, far = pl.pallas_call(
        faces_kernel, out_shape=(bf16(64, FACE),) * 2, grid=(1,),
        in_specs=[cut, cut], out_specs=(face, face),
        compiler_params=pltpu.CompilerParams(vmem_limit_bytes=56 << 20),
        cost_estimate=pl.CostEstimate(flops=1 << 30, bytes_accessed=1 << 16, transcendentals=0),
        name="faces",
    )(x, g)
    pair = call(join_kernel, bf16(64, VOX), (g, over_ch(g, 1)), name="join")
    near = swap(near, 1)
    far = swap_far(far)
    other = over_ch(pair, 3)
    dense = call(
        gather_kernel, bf16(864, VOX), (x, rules),
        [pltpu.VMEM((32, VOX), jnp.float32)], flops=3 << 30, name="gather",
    )
    dense, grads, keep, send = call(
        weight_kernel,
        (bf16(864, VOX), bf16(128, VOX), f32(4 * PART, 128), f32(4 * PART, 128)),
        (dense, rules, near, far, pair, other),
        [pltpu.VMEM((32, 2 * FACE), jnp.float32), pltpu.VMEM((8 * PART, 128), jnp.float32)],
        aliases={0: 0}, flops=1 << 30, name="weight_terms",
    )

    def inner_part(groups, inner=None):
        args = (back, rules) if inner is None else (back, rules, inner)
        return call(
            functools.partial(back_inner_kernel, groups), f32(32, VOX), args,
            aliases=None if inner is None else {2: 0}, flops=len(groups) << 30,
            name="back_inner",
        )

    came = swap(send, 1)
    ours, first = call(
        forward_kernel, (f32(64, VOX), f32(64, VOX + FACE)), (dense, weights, near, far),
        [pltpu.VMEM((128, VOX), jnp.float32)], flops=1 << 30, name="forward",
    )
    back = call(
        back_terms_kernel, f32(864, VOX), (weights, grads), flops=1 << 30, name="back_terms"
    )
    came, = after((came,), ours, back)
    pieces = call(split_sum_kernel, (f32(PART, 128),) * 4, (keep, came), name="sum_pair")
    others = [swap(pieces[q], 2 * q) for q in (1, 2, 3)]
    first, = after((first,), *pieces)
    first = over_ch(first, 1)
    inner = inner_part((2, 3))
    others = after(others, inner)
    total = call(sum_kernel, f32(PART, 128), (pieces[0], *others), name="sum_four")
    came = swap(total, 48)
    inner = inner_part((4, 5), inner)
    ours, first = after((ours, first), inner)
    own, second = call(
        middle_kernel, (f32(32, VOX), f32(32, VOX + 4 * FACE)), (ours, first, near, far),
        name="middle",
    )
    second = over_ch(second, 3)
    came, = after((came,), own)
    total = call(sum_kernel, f32(PART, 128), (total, came), name="sum_two")
    others = [swap(total, m) for m in (8, 16, 24)]
    inner = inner_part((6, 7), inner)
    others = after(others, inner)
    total = call(sum_kernel, f32(PART, 128), (total, *others), name="sum_four")
    others = [swap(total, 2 * q) for q in (1, 2, 3)]
    output, grad_features = call(
        edge_kernel, (bf16(32, VOX), bf16(32, VOX)),
        (back, rules, weights, near, far, inner, own, first, second),
        [pltpu.VMEM((128, 2 * FACE), jnp.bfloat16), pltpu.VMEM((864, 2 * FACE), jnp.float32)],
        flops=2 << 30, name="edge",
    )
    others = after(others, output)
    even = call(join_kernel, f32(4 * PART, 128), (total, *others), name="join")
    odd = swap(even, 1)
    weight_grad = call(
        place_kernel, f32(864, 128), (even, odd), name="place",
    )
    return output, grad_features, weight_grad.reshape(27, 32, 128)


def solution(mesh):
    placed = (P("ch", "blk"), P(None, "ch", None), P("ch", "blk"), P(None, "blk"))
    return jax.shard_map(
        per_device,
        mesh=mesh,
        in_specs=placed,
        out_specs=(P("ch", "blk"), P("ch", "blk"), P(None, "ch", None)),
        check_vma=False,
    )
```

```python
import functools

import jax
import jax.numpy as jnp
from jax import lax
from jax.experimental import pallas as pl
from jax.experimental.pallas import tpu as pltpu
from jax.sharding import PartitionSpec as P

VOX = 1024
FACE = 128
LANES = 128
PART = 112
INNER = tuple(range(2, 8))
EDGE = (0, 1)
ORDER = (0, 1, 3, 2)
VMEM = pl.BlockSpec(memory_space=pltpu.VMEM)


def source_tiles(group, dz):
    if group == 0:
        return {-1: (8,), 0: (0,), 1: INNER}[dz]
    if group == 1:
        return {-1: INNER, 0: (1,), 1: (9,)}[dz]
    return {-1: (0,) + INNER, 0: INNER, 1: (1,) + INNER}[dz]


def picked(row, group, tiles, load):
    span = row[:, LANES * group : LANES * (group + 1)]
    index = jnp.broadcast_to(span, (32, LANES))
    lane = index & (LANES - 1)
    tile = index >> 7
    total = jnp.zeros((32, LANES), jnp.float32)
    for t in tiles:
        values = jnp.take_along_axis(load(t), lane, axis=1, mode="promise_in_bounds")
        total = jnp.where(tile == t, values, total)
    return total


def tile_span(t):
    return slice(LANES * t, LANES * (t + 1))


def faces_kernel(x_ref, g_ref, near_ref, far_ref):
    odd = (lax.axis_index("blk") & 1) == 1
    for rows, ref in ((slice(0, 32), x_ref), (slice(32, 64), g_ref)):
        lowest = ref[:, :FACE].astype(jnp.float32)
        highest = ref[:, FACE : 2 * FACE].astype(jnp.float32)
        near_ref[rows, :] = jnp.where(odd, lowest, highest).astype(jnp.bfloat16)
        far_ref[rows, :] = jnp.where(odd, highest, lowest).astype(jnp.bfloat16)


def by_side(near, far):
    odd = (lax.axis_index("blk") & 1) == 1
    near = near.astype(jnp.float32)
    far = far.astype(jnp.float32)
    return jnp.where(odd, near, far), jnp.where(odd, far, near)


def gather_kernel(x_ref, rule_ref, dense_ref, table):
    table[...] = x_ref[...].astype(jnp.float32)
    for k in range(27):
        row = rule_ref[k : k + 1, :]
        for group in range(8):
            tiles = source_tiles(group, k % 3 - 1)
            if tiles[0] >= 8:
                continue
            got = picked(row, group, tiles, lambda t: table[:, tile_span(t)])
            dense_ref[32 * k : 32 * k + 32, tile_span(group)] = got.astype(jnp.bfloat16)


def faces_kernel(x_ref, g_ref, near_ref, far_ref):
    odd = (lax.axis_index("blk") & 1) == 1
    for rows, ref in ((slice(0, 32), x_ref), (slice(32, 64), g_ref)):
        lowest = ref[:, :FACE].astype(jnp.float32)
        highest = ref[:, FACE : 2 * FACE].astype(jnp.float32)
        near_ref[rows, :] = jnp.where(odd, lowest, highest).astype(jnp.bfloat16)
        far_ref[rows, :] = jnp.where(odd, highest, lowest).astype(jnp.bfloat16)


def by_side(near, far):
    odd = (lax.axis_index("blk") & 1) == 1
    near = near.astype(jnp.float32)
    far = far.astype(jnp.float32)
    return jnp.where(odd, near, far), jnp.where(odd, far, near)


def gather_kernel(x_ref, rule_ref, dense_ref, table):
    table[...] = x_ref[...].astype(jnp.float32)

    def step(j, carry):
        for d in range(3):
            k = 3 * j + d
            row = rule_ref[pl.ds(k, 1), :]
            for group in range(8):
                tiles = source_tiles(group, d - 1)
                if tiles[0] >= 8:
                    continue
                got = picked(row, group, tiles, lambda t: table[:, tile_span(t)])
                rows = pl.ds(pl.multiple_of(32 * k, 32), 32)
                dense_ref[rows, tile_span(group)] = got.astype(jnp.bfloat16)
        return carry

    lax.fori_loop(0, 9, step, 0)


def weight_kernel(
    dense_in, rule_ref, near_ref, far_ref, pair_ref, other_ref,
    dense_ref, grad_ref, keep_ref, send_ref, faces, terms,
):
    chan = lax.axis_index("ch")
    spot = lax.axis_index("blk") & 7
    for i, m in enumerate(ORDER):
        part = (pair_ref if i < 2 else other_ref)[32 * (i % 2) : 32 * (i % 2) + 32, :]
        grad_ref[pl.ds(pl.multiple_of(32 * (chan ^ m), 32), 32), :] = part
    faces[:, :FACE], faces[:, FACE:] = by_side(near_ref[:32, :], far_ref[:32, :])

    for j in range(9):
        for group, d in ((0, 0), (1, 2)):
            k = 3 * j + d
            row = rule_ref[k : k + 1, :]
            got = picked(row, group, (8 + group,), lambda t: faces[:, tile_span(t - 8)])
            dense_ref[32 * k : 32 * k + 32, tile_span(group)] = got.astype(jnp.bfloat16)
    terms[:864, :] = lax.dot_general(
        dense_ref[...], grad_ref[...], (((1,), (1,)), ((), ())),
        preferred_element_type=jnp.float32,
    ) * (1.0 / 256.0)
    terms[864:, :] = jnp.zeros((32, LANES), jnp.float32)
    for q in range(4):
        for odd, target in ((0, keep_ref), (1, send_ref)):
            start = pl.multiple_of(PART * (spot ^ (2 * q + odd)), 8)
            target[PART * q : PART * (q + 1), :] = terms[pl.ds(start, PART), :]


def forward_kernel(dense_ref, weight_ref, near_ref, far_ref, keep_ref, send_ref, sums):
    chan = lax.axis_index("ch")
    sums[...] = lax.dot_general(
        weight_ref[...], dense_ref[...], (((0,), (0,)), ((), ())),
        preferred_element_type=jnp.float32,
    )
    for target, parts in ((keep_ref, (0, 3)), (send_ref, (1, 2))):
        for i, m in enumerate(parts):
            rows = pl.ds(pl.multiple_of(32 * (chan ^ m), 32), 32)
            target[32 * i : 32 * i + 32, :VOX] = sums[rows, :]
    lower, upper = by_side(near_ref[32:, :], far_ref[32:, :])
    send_ref[:32, VOX:] = lower
    send_ref[32:, VOX:] = upper


def middle_kernel(keep_ref, came_ref, near_ref, far_ref, own_ref, send_ref):
    own_ref[...] = keep_ref[:32, :] + came_ref[:32, :VOX]
    send_ref[:, :VOX] = keep_ref[32:, :] + came_ref[32:, :VOX]
    lower, upper = by_side(near_ref[32:, :], far_ref[32:, :])
    send_ref[:, VOX : VOX + FACE] = lower
    send_ref[:, VOX + FACE : VOX + 2 * FACE] = upper
    send_ref[:, VOX + 2 * FACE : VOX + 3 * FACE] = came_ref[:32, VOX:]
    send_ref[:, VOX + 3 * FACE :] = came_ref[32:, VOX:]


def back_terms_kernel(weight_ref, grad_ref, terms_ref):
    terms_ref[...] = jnp.dot(
        weight_ref[...], grad_ref[...], preferred_element_type=jnp.float32
    )


def back_sum(groups, rule_ref, load):
    totals = {}
    for k in range(27):
        row = rule_ref[k : k + 1, :]
        rows = slice(32 * (26 - k), 32 * (26 - k) + 32)
        for group in groups:
            got = picked(row, group, source_tiles(group, k % 3 - 1), lambda t: load(rows, t))
            totals[group] = got if k == 0 else totals[group] + got
    return totals


def back_inner_kernel(groups, terms, rule_ref, *refs):
    totals = back_sum(groups, rule_ref, lambda rows, t: terms[rows, tile_span(t)])
    for group in groups:
        refs[-1][:, tile_span(group)] = totals[group]


def edge_kernel(
    terms, rule_ref, weight_ref, near_ref, far_ref, inner, own_ref, first_ref, second_ref,
    out_ref, grad_ref, faces, products,
):
    chan = lax.axis_index("ch")
    out_ref[...] = (own_ref[...] + second_ref[:, :VOX]).astype(jnp.bfloat16)
    lower, upper = by_side(near_ref[32:, :], far_ref[32:, :])
    pairs = (
        (lower, upper),
        (first_ref[:32, VOX:], first_ref[32:, VOX:]),
        (second_ref[:, VOX : VOX + FACE], second_ref[:, VOX + FACE : VOX + 2 * FACE]),
        (second_ref[:, VOX + 2 * FACE : VOX + 3 * FACE], second_ref[:, VOX + 3 * FACE :]),
    )
    for m, (lower, upper) in zip(ORDER, pairs):
        rows = pl.ds(pl.multiple_of(32 * (chan ^ m), 32), 32)
        faces[rows, :FACE] = lower.astype(jnp.bfloat16)
        faces[rows, FACE:] = upper.astype(jnp.bfloat16)
    products[...] = jnp.dot(
        weight_ref[...], faces[...], preferred_element_type=jnp.float32
    )
    totals = back_sum(
        EDGE, rule_ref,
        lambda rows, t: products[rows, tile_span(t - 8)] if t >= 8 else terms[rows, tile_span(t)],
    )
    for group in range(8):
        values = totals[group] if group in EDGE else inner[:, tile_span(group)]
        grad_ref[:, tile_span(group)] = values.astype(jnp.bfloat16)


def split_sum_kernel(keep_ref, came_ref, *outs):
    for q, out in enumerate(outs):
        rows = slice(PART * q, PART * (q + 1))
        out[...] = keep_ref[rows, :] + came_ref[rows, :]


def sum_kernel(*refs):
    values = [ref[...] for ref in refs[:-1]]
    while len(values) > 1:
        values = [values[i] + values[i + 1] for i in range(0, len(values), 2)]
    refs[-1][...] = values[0]


def join_kernel(*refs):
    size = refs[0].shape[0]
    for q, ref in enumerate(refs[:-1]):
        refs[-1][size * q : size * (q + 1), :] = ref[...]


def place_kernel(*refs):
    out_ref, sems = refs[-2:]
    spot = lax.axis_index("blk") & 7
    short = 864 - 7 * PART

    def copies(r):
        part = spot ^ r
        start = pl.multiple_of(PART * part, 8)
        head = pltpu.make_async_copy(
            refs[r].at[pl.ds(0, short), :], out_ref.at[pl.ds(start, short), :], sems.at[r, 0]
        )
        rest = pl.ds(pl.multiple_of(start + short, 8), PART - short)
        tail = pltpu.make_async_copy(
            refs[r].at[pl.ds(short, PART - short), :], out_ref.at[rest, :], sems.at[r, 1]
        )
        return part, head, tail

    for r in range(8):
        part, head, tail = copies(r)
        head.start()

        @pl.when(part < 7)
        def _():
            tail.start()

    for r in range(8):
        part, head, tail = copies(r)
        head.wait()

        @pl.when(part < 7)
        def _():
            tail.wait()


def call(kernel, outs, args, scratch=(), aliases=None, flops=0, name=None):
    moved = sum(a.size * a.dtype.itemsize for a in list(args) + jax.tree.leaves(outs))
    return pl.pallas_call(
        kernel,
        out_shape=outs,
        in_specs=[VMEM] * len(args),
        out_specs=jax.tree.map(lambda _: VMEM, outs),
        scratch_shapes=list(scratch),
        input_output_aliases=aliases or {},
        compiler_params=pltpu.CompilerParams(vmem_limit_bytes=40 << 20),
        cost_estimate=pl.CostEstimate(flops=flops, bytes_accessed=moved, transcendentals=0),
        name=name,
    )(*args)


def f32(*shape):
    return jax.ShapeDtypeStruct(shape, jnp.float32)


def bf16(*shape):
    return jax.ShapeDtypeStruct(shape, jnp.bfloat16)


def swap(value, mask):
    count = lax.axis_size("blk")
    return lax.ppermute(value, "blk", [(i, i ^ mask) for i in range(count)])


def swap_far(value):
    count = lax.axis_size("blk")
    pairs = [(i, (i + 1 if i % 2 else i - 1) % count) for i in range(count)]
    return lax.ppermute(value, "blk", pairs)


def after(values, *others):
    return lax.optimization_barrier((*values, *others))[: len(values)]


def per_device(features, weight, grad_out, rulebook):
    weights = weight.reshape(864, 128)

    def over_ch(value, mask):
        return lax.ppermute(value, "ch", [(i, i ^ mask) for i in range(4)])

    x, g, rules = features, grad_out, rulebook
    cut = pl.BlockSpec((32, 2 * FACE), lambda i: (0, 0))
    face = pl.BlockSpec((64, FACE), lambda i: (0, 0))
    near, far = pl.pallas_call(
        faces_kernel, out_shape=(bf16(64, FACE),) * 2, grid=(1,),
        in_specs=[cut, cut], out_specs=(face, face),
        compiler_params=pltpu.CompilerParams(vmem_limit_bytes=56 << 20),
        cost_estimate=pl.CostEstimate(flops=1 << 30, bytes_accessed=1 << 16, transcendentals=0),
        name="faces",
    )(x, g)
    pair = call(join_kernel, bf16(64, VOX), (g, over_ch(g, 1)), name="join")
    near = swap(near, 1)
    far = swap_far(far)
    other = over_ch(pair, 3)
    dense = call(
        gather_kernel, bf16(864, VOX), (x, rules),
        [pltpu.VMEM((32, VOX), jnp.float32)], flops=3 << 30, name="gather",
    )
    dense, grads, keep, send = call(
        weight_kernel,
        (bf16(864, VOX), bf16(128, VOX), f32(4 * PART, 128), f32(4 * PART, 128)),
        (dense, rules, near, far, pair, other),
        [pltpu.VMEM((32, 2 * FACE), jnp.float32), pltpu.VMEM((8 * PART, 128), jnp.float32)],
        aliases={0: 0}, flops=1 << 30, name="weight_terms",
    )

    def inner_part(groups, inner=None):
        args = (back, rules) if inner is None else (back, rules, inner)
        return call(
            functools.partial(back_inner_kernel, groups), f32(32, VOX), args,
            aliases=None if inner is None else {2: 0}, flops=len(groups) << 30,
            name="back_inner",
        )

    came = swap(send, 1)
    ours, first = call(
        forward_kernel, (f32(64, VOX), f32(64, VOX + FACE)), (dense, weights, near, far),
        [pltpu.VMEM((128, VOX), jnp.float32)], flops=1 << 30, name="forward",
    )
    back = call(
        back_terms_kernel, f32(864, VOX), (weights, grads), flops=1 << 30, name="back_terms"
    )
    came, = after((came,), ours, back)
    pieces = call(split_sum_kernel, (f32(PART, 128),) * 4, (keep, came), name="sum_pair")
    others = [swap(pieces[q], 2 * q) for q in (1, 2, 3)]
    first, = after((first,), *pieces)
    first = over_ch(first, 1)
    inner = inner_part((2, 3))
    others = after(others, inner)
    total = call(sum_kernel, f32(PART, 128), (pieces[0], *others), name="sum_four")
    came = swap(total, 48)
    inner = inner_part((4, 5), inner)
    ours, first = after((ours, first), inner)
    own, second = call(
        middle_kernel, (f32(32, VOX), f32(32, VOX + 4 * FACE)), (ours, first, near, far),
        name="middle",
    )
    second = over_ch(second, 3)
    came, = after((came,), own)
    total = call(sum_kernel, f32(PART, 128), (total, came), name="sum_two")
    others = [swap(total, m) for m in (8, 16, 24)]
    inner = inner_part((6, 7), inner)
    others = after(others, inner)
    total = call(sum_kernel, f32(PART, 128), (total, *others), name="sum_four")
    others = [swap(total, 2 * q) for q in (1, 2, 3)]
    output, grad_features = call(
        edge_kernel, (bf16(32, VOX), bf16(32, VOX)),
        (back, rules, weights, near, far, inner, own, first, second),
        [pltpu.VMEM((128, 2 * FACE), jnp.bfloat16), pltpu.VMEM((864, 2 * FACE), jnp.float32)],
        flops=2 << 30, name="edge",
    )
    others = after(others, output)
    even = [total, *others]
    odd = [swap(part, 1) for part in even]
    parts = [part for pair in zip(even, odd) for part in pair]
    weight_grad = pl.pallas_call(
        place_kernel, out_shape=f32(864, 128), in_specs=[VMEM] * 8,
        out_specs=pl.BlockSpec(memory_space=pltpu.HBM),
        scratch_shapes=[pltpu.SemaphoreType.DMA((8, 2))],
        compiler_params=pltpu.CompilerParams(vmem_limit_bytes=40 << 20), name="place",
    )(*parts)
    return output, grad_features, weight_grad.reshape(27, 32, 128)


def solution(mesh):
    placed = (P("ch", "blk"), P(None, "ch", None), P("ch", "blk"), P(None, "blk"))
    return jax.shard_map(
        per_device,
        mesh=mesh,
        in_specs=placed,
        out_specs=(P("ch", "blk"), P("ch", "blk"), P(None, "ch", None)),
        check_vma=False,
    )
```

```python
import functools

import jax
import jax.numpy as jnp
from jax import lax
from jax.experimental import pallas as pl
from jax.experimental.pallas import tpu as pltpu
from jax.sharding import PartitionSpec as P

VOX = 1024
FACE = 128
LANES = 128
PART = 112
INNER = tuple(range(2, 8))
EDGE = (0, 1)
X1, X3, Z1, Z2, Z6 = 2, 6, 8, 16, 48
ORDER = (0, 1, 3, 2)
VMEM = pl.BlockSpec(memory_space=pltpu.VMEM)


def source_tiles(group, dz):
    if group == 0:
        return {-1: (8,), 0: (0,), 1: INNER}[dz]
    if group == 1:
        return {-1: INNER, 0: (1,), 1: (9,)}[dz]
    return {-1: (0,) + INNER, 0: INNER, 1: (1,) + INNER}[dz]


def picked(row, group, tiles, load):
    span = row[:, LANES * group : LANES * (group + 1)]
    index = jnp.broadcast_to(span, (32, LANES))
    lane = index & (LANES - 1)
    tile = index >> 7
    total = jnp.zeros((32, LANES), jnp.float32)
    for t in tiles:
        values = jnp.take_along_axis(load(t), lane, axis=1, mode="promise_in_bounds")
        total = jnp.where(tile == t, values, total)
    return total


def own_part():
    place = lax.axis_index("blk")
    return (place & 1) | ((place ^ (place >> 1)) & 2) | ((place >> 1) & 4)


def tile_span(t):
    return slice(LANES * t, LANES * (t + 1))


def faces_kernel(x_ref, g_ref, near_ref, far_ref):
    odd = (lax.axis_index("blk") & 1) == 1
    for rows, ref in ((slice(0, 32), x_ref), (slice(32, 64), g_ref)):
        lowest = ref[:, :FACE].astype(jnp.float32)
        highest = ref[:, FACE : 2 * FACE].astype(jnp.float32)
        near_ref[rows, :] = jnp.where(odd, lowest, highest).astype(jnp.bfloat16)
        far_ref[rows, :] = jnp.where(odd, highest, lowest).astype(jnp.bfloat16)


def by_side(near, far):
    odd = (lax.axis_index("blk") & 1) == 1
    near = near.astype(jnp.float32)
    far = far.astype(jnp.float32)
    return jnp.where(odd, near, far), jnp.where(odd, far, near)


def gather_kernel(x_ref, rule_ref, dense_ref, table):
    table[...] = x_ref[...].astype(jnp.float32)
    for k in range(27):
        row = rule_ref[k : k + 1, :]
        for group in range(8):
            tiles = source_tiles(group, k % 3 - 1)
            if tiles[0] >= 8:
                continue
            got = picked(row, group, tiles, lambda t: table[:, tile_span(t)])
            dense_ref[32 * k : 32 * k + 32, tile_span(group)] = got.astype(jnp.bfloat16)


def faces_kernel(x_ref, g_ref, near_ref, far_ref):
    odd = (lax.axis_index("blk") & 1) == 1
    for rows, ref in ((slice(0, 32), x_ref), (slice(32, 64), g_ref)):
        lowest = ref[:, :FACE].astype(jnp.float32)
        highest = ref[:, FACE : 2 * FACE].astype(jnp.float32)
        near_ref[rows, :] = jnp.where(odd, lowest, highest).astype(jnp.bfloat16)
        far_ref[rows, :] = jnp.where(odd, highest, lowest).astype(jnp.bfloat16)


def by_side(near, far):
    odd = (lax.axis_index("blk") & 1) == 1
    near = near.astype(jnp.float32)
    far = far.astype(jnp.float32)
    return jnp.where(odd, near, far), jnp.where(odd, far, near)


def gather_kernel(x_ref, rule_ref, dense_ref, table):
    table[...] = x_ref[...].astype(jnp.float32)

    def step(j, carry):
        for d in range(3):
            k = 3 * j + d
            row = rule_ref[pl.ds(k, 1), :]
            for group in range(8):
                tiles = source_tiles(group, d - 1)
                if tiles[0] >= 8:
                    continue
                got = picked(row, group, tiles, lambda t: table[:, tile_span(t)])
                rows = pl.ds(pl.multiple_of(32 * k, 32), 32)
                dense_ref[rows, tile_span(group)] = got.astype(jnp.bfloat16)
        return carry

    lax.fori_loop(0, 9, step, 0)


def weight_kernel(
    dense_in, rule_ref, near_ref, far_ref, pair_ref, other_ref,
    dense_ref, grad_ref, keep_ref, send_ref, faces, terms,
):
    chan = lax.axis_index("ch")
    spot = own_part()
    for i, m in enumerate(ORDER):
        part = (pair_ref if i < 2 else other_ref)[32 * (i % 2) : 32 * (i % 2) + 32, :]
        grad_ref[pl.ds(pl.multiple_of(32 * (chan ^ m), 32), 32), :] = part
    faces[:, :FACE], faces[:, FACE:] = by_side(near_ref[:32, :], far_ref[:32, :])

    for j in range(9):
        for group, d in ((0, 0), (1, 2)):
            k = 3 * j + d
            row = rule_ref[k : k + 1, :]
            got = picked(row, group, (8 + group,), lambda t: faces[:, tile_span(t - 8)])
            dense_ref[32 * k : 32 * k + 32, tile_span(group)] = got.astype(jnp.bfloat16)
    terms[:864, :] = lax.dot_general(
        dense_ref[...], grad_ref[...], (((1,), (1,)), ((), ())),
        preferred_element_type=jnp.float32,
    ) * (1.0 / 256.0)
    terms[864:, :] = jnp.zeros((32, LANES), jnp.float32)
    for q in range(4):
        for odd, target in ((0, keep_ref), (1, send_ref)):
            start = pl.multiple_of(PART * (spot ^ (2 * q + odd)), 8)
            target[PART * q : PART * (q + 1), :] = terms[pl.ds(start, PART), :]


def forward_kernel(dense_ref, weight_ref, near_ref, far_ref, keep_ref, send_ref, sums):
    chan = lax.axis_index("ch")
    sums[...] = lax.dot_general(
        weight_ref[...], dense_ref[...], (((0,), (0,)), ((), ())),
        preferred_element_type=jnp.float32,
    )
    for target, parts in ((keep_ref, (0, 3)), (send_ref, (1, 2))):
        for i, m in enumerate(parts):
            rows = pl.ds(pl.multiple_of(32 * (chan ^ m), 32), 32)
            target[32 * i : 32 * i + 32, :VOX] = sums[rows, :]
    lower, upper = by_side(near_ref[32:, :], far_ref[32:, :])
    send_ref[:32, VOX:] = lower
    send_ref[32:, VOX:] = upper


def middle_kernel(keep_ref, came_ref, near_ref, far_ref, own_ref, send_ref):
    own_ref[...] = keep_ref[:32, :] + came_ref[:32, :VOX]
    send_ref[:, :VOX] = keep_ref[32:, :] + came_ref[32:, :VOX]
    lower, upper = by_side(near_ref[32:, :], far_ref[32:, :])
    send_ref[:, VOX : VOX + FACE] = lower
    send_ref[:, VOX + FACE : VOX + 2 * FACE] = upper
    send_ref[:, VOX + 2 * FACE : VOX + 3 * FACE] = came_ref[:32, VOX:]
    send_ref[:, VOX + 3 * FACE :] = came_ref[32:, VOX:]


def back_terms_kernel(weight_ref, grad_ref, terms_ref):
    terms_ref[...] = jnp.dot(
        weight_ref[...], grad_ref[...], preferred_element_type=jnp.float32
    )


def back_sum(groups, rule_ref, load):
    totals = {}
    for k in range(27):
        row = rule_ref[k : k + 1, :]
        rows = slice(32 * (26 - k), 32 * (26 - k) + 32)
        for group in groups:
            got = picked(row, group, source_tiles(group, k % 3 - 1), lambda t: load(rows, t))
            totals[group] = got if k == 0 else totals[group] + got
    return totals


def back_inner_kernel(groups, terms, rule_ref, *refs):
    totals = back_sum(groups, rule_ref, lambda rows, t: terms[rows, tile_span(t)])
    for group in groups:
        refs[-1][:, tile_span(group)] = totals[group]


def edge_kernel(
    terms, rule_ref, weight_ref, near_ref, far_ref, inner, own_ref, first_ref, second_ref,
    out_ref, grad_ref, faces, products,
):
    chan = lax.axis_index("ch")
    out_ref[...] = (own_ref[...] + second_ref[:, :VOX]).astype(jnp.bfloat16)
    lower, upper = by_side(near_ref[32:, :], far_ref[32:, :])
    pairs = (
        (lower, upper),
        (first_ref[:32, VOX:], first_ref[32:, VOX:]),
        (second_ref[:, VOX : VOX + FACE], second_ref[:, VOX + FACE : VOX + 2 * FACE]),
        (second_ref[:, VOX + 2 * FACE : VOX + 3 * FACE], second_ref[:, VOX + 3 * FACE :]),
    )
    for m, (lower, upper) in zip(ORDER, pairs):
        rows = pl.ds(pl.multiple_of(32 * (chan ^ m), 32), 32)
        faces[rows, :FACE] = lower.astype(jnp.bfloat16)
        faces[rows, FACE:] = upper.astype(jnp.bfloat16)
    products[...] = jnp.dot(
        weight_ref[...], faces[...], preferred_element_type=jnp.float32
    )
    totals = back_sum(
        EDGE, rule_ref,
        lambda rows, t: products[rows, tile_span(t - 8)] if t >= 8 else terms[rows, tile_span(t)],
    )
    for group in range(8):
        values = totals[group] if group in EDGE else inner[:, tile_span(group)]
        grad_ref[:, tile_span(group)] = values.astype(jnp.bfloat16)


def split_sum_kernel(keep_ref, came_ref, *outs):
    for q, out in enumerate(outs):
        rows = slice(PART * q, PART * (q + 1))
        out[...] = keep_ref[rows, :] + came_ref[rows, :]


def sum_kernel(*refs):
    values = [ref[...] for ref in refs[:-1]]
    while len(values) > 1:
        values = [values[i] + values[i + 1] for i in range(0, len(values), 2)]
    refs[-1][...] = values[0]


def join_kernel(*refs):
    size = refs[0].shape[0]
    for q, ref in enumerate(refs[:-1]):
        refs[-1][size * q : size * (q + 1), :] = ref[...]


def place_kernel(even_ref, odd_ref, out_ref):
    spot = own_part()
    short = 864 - 7 * PART
    for q in range(4):
        for odd, ref in enumerate((even_ref, odd_ref)):
            part = spot ^ (2 * q + odd)
            start = pl.multiple_of(PART * part, 8)
            out_ref[pl.ds(start, short), :] = ref[PART * q : PART * q + short, :]

            @pl.when(part < 7)
            def _():
                rows = pl.ds(pl.multiple_of(start + short, 8), PART - short)
                out_ref[rows, :] = ref[PART * q + short : PART * (q + 1), :]


def call(kernel, outs, args, scratch=(), aliases=None, flops=0, name=None):
    moved = sum(a.size * a.dtype.itemsize for a in list(args) + jax.tree.leaves(outs))
    return pl.pallas_call(
        kernel,
        out_shape=outs,
        in_specs=[VMEM] * len(args),
        out_specs=jax.tree.map(lambda _: VMEM, outs),
        scratch_shapes=list(scratch),
        input_output_aliases=aliases or {},
        compiler_params=pltpu.CompilerParams(vmem_limit_bytes=40 << 20),
        cost_estimate=pl.CostEstimate(flops=flops, bytes_accessed=moved, transcendentals=0),
        name=name,
    )(*args)


def f32(*shape):
    return jax.ShapeDtypeStruct(shape, jnp.float32)


def bf16(*shape):
    return jax.ShapeDtypeStruct(shape, jnp.bfloat16)


def swap(value, mask):
    count = lax.axis_size("blk")
    return lax.ppermute(value, "blk", [(i, i ^ mask) for i in range(count)])


def swap_far(value):
    count = lax.axis_size("blk")
    pairs = [(i, (i + 1 if i % 2 else i - 1) % count) for i in range(count)]
    return lax.ppermute(value, "blk", pairs)


def after(values, *others):
    return lax.optimization_barrier((*values, *others))[: len(values)]


def per_device(features, weight, grad_out, rulebook):
    weights = weight.reshape(864, 128)

    def over_ch(value, mask):
        return lax.ppermute(value, "ch", [(i, i ^ mask) for i in range(4)])

    x, g, rules = features, grad_out, rulebook
    cut = pl.BlockSpec((32, 2 * FACE), lambda i: (0, 0))
    face = pl.BlockSpec((64, FACE), lambda i: (0, 0))
    near, far = pl.pallas_call(
        faces_kernel, out_shape=(bf16(64, FACE),) * 2, grid=(1,),
        in_specs=[cut, cut], out_specs=(face, face),
        compiler_params=pltpu.CompilerParams(vmem_limit_bytes=56 << 20),
        cost_estimate=pl.CostEstimate(flops=1 << 30, bytes_accessed=1 << 16, transcendentals=0),
        name="faces",
    )(x, g)
    pair = call(join_kernel, bf16(64, VOX), (g, over_ch(g, 1)), name="join")
    near = swap(near, 1)
    far = swap_far(far)
    other = over_ch(pair, 3)
    dense = call(
        gather_kernel, bf16(864, VOX), (x, rules),
        [pltpu.VMEM((32, VOX), jnp.float32)], flops=3 << 30, name="gather",
    )
    dense, grads, keep, send = call(
        weight_kernel,
        (bf16(864, VOX), bf16(128, VOX), f32(4 * PART, 128), f32(4 * PART, 128)),
        (dense, rules, near, far, pair, other),
        [pltpu.VMEM((32, 2 * FACE), jnp.float32), pltpu.VMEM((8 * PART, 128), jnp.float32)],
        aliases={0: 0}, flops=1 << 30, name="weight_terms",
    )

    def inner_part(groups, inner=None):
        args = (back, rules) if inner is None else (back, rules, inner)
        return call(
            functools.partial(back_inner_kernel, groups), f32(32, VOX), args,
            aliases=None if inner is None else {2: 0}, flops=len(groups) << 30,
            name="back_inner",
        )

    came = swap(send, 1)
    ours, first = call(
        forward_kernel, (f32(64, VOX), f32(64, VOX + FACE)), (dense, weights, near, far),
        [pltpu.VMEM((128, VOX), jnp.float32)], flops=1 << 30, name="forward",
    )
    back = call(
        back_terms_kernel, f32(864, VOX), (weights, grads), flops=1 << 30, name="back_terms"
    )
    came, = after((came,), ours, back)
    pieces = call(split_sum_kernel, (f32(PART, 128),) * 4, (keep, came), name="sum_pair")
    others = [swap(pieces[q], m) for q, m in ((1, X1), (2, Z1), (3, X1 | Z1))]
    first, = after((first,), *pieces)
    first = over_ch(first, 1)
    inner = inner_part((2, 3))
    others = after(others, inner)
    total = call(sum_kernel, f32(PART, 128), (pieces[0], *others), name="sum_four")
    came = swap(total, Z6)
    inner = inner_part((4, 5), inner)
    ours, first = after((ours, first), inner)
    own, second = call(
        middle_kernel, (f32(32, VOX), f32(32, VOX + 4 * FACE)), (ours, first, near, far),
        name="middle",
    )
    second = over_ch(second, 3)
    came, = after((came,), own)
    total = call(sum_kernel, f32(PART, 128), (total, came), name="sum_two")
    others = [swap(total, m) for m in (X3, Z2, X3 | Z2)]
    inner = inner_part((6, 7), inner)
    others = after(others, inner)
    total = call(sum_kernel, f32(PART, 128), (total, *others), name="sum_four")
    others = [swap(total, m) for m in (X1, Z1, X1 | Z1)]
    output, grad_features = call(
        edge_kernel, (bf16(32, VOX), bf16(32, VOX)),
        (back, rules, weights, near, far, inner, own, first, second),
        [pltpu.VMEM((128, 2 * FACE), jnp.bfloat16), pltpu.VMEM((864, 2 * FACE), jnp.float32)],
        flops=2 << 30, name="edge",
    )
    others = after(others, output)
    even = call(join_kernel, f32(4 * PART, 128), (total, *others), name="join")
    odd = swap(even, 1)
    weight_grad = call(
        place_kernel, f32(864, 128), (even, odd), name="place",
    )
    return output, grad_features, weight_grad.reshape(27, 32, 128)


def solution(mesh):
    placed = (P("ch", "blk"), P(None, "ch", None), P("ch", "blk"), P(None, "blk"))
    return jax.shard_map(
        per_device,
        mesh=mesh,
        in_specs=placed,
        out_specs=(P("ch", "blk"), P("ch", "blk"), P(None, "ch", None)),
        check_vma=False,
    )
```

```python
import functools

import jax
import jax.numpy as jnp
from jax import lax
from jax.experimental import pallas as pl
from jax.experimental.pallas import tpu as pltpu
from jax.sharding import PartitionSpec as P

VOX = 1024
FACE = 128
LANES = 128
PART = 112
INNER = tuple(range(2, 8))
EDGE = (0, 1)
X1, X3, Z1, Z2, Z6 = 2, 6, 8, 16, 48
ORDER = (0, 1, 3, 2)
VMEM = pl.BlockSpec(memory_space=pltpu.VMEM)


def source_tiles(group, dz):
    if group == 0:
        return {-1: (8,), 0: (0,), 1: INNER}[dz]
    if group == 1:
        return {-1: INNER, 0: (1,), 1: (9,)}[dz]
    return {-1: (0,) + INNER, 0: INNER, 1: (1,) + INNER}[dz]


def picked(row, group, tiles, load):
    span = row[:, LANES * group : LANES * (group + 1)]
    index = jnp.broadcast_to(span, (32, LANES))
    lane = index & (LANES - 1)
    tile = index >> 7
    total = jnp.zeros((32, LANES), jnp.float32)
    for t in tiles:
        values = jnp.take_along_axis(load(t), lane, axis=1, mode="promise_in_bounds")
        total = jnp.where(tile == t, values, total)
    return total


def own_part():
    place = lax.axis_index("blk")
    return (place & 1) | ((place ^ (place >> 1)) & 2) | ((place >> 1) & 4)


def tile_span(t):
    return slice(LANES * t, LANES * (t + 1))


def faces_kernel(x_ref, g_ref, near_ref, far_ref):
    odd = (lax.axis_index("blk") & 1) == 1
    for rows, ref in ((slice(0, 32), x_ref), (slice(32, 64), g_ref)):
        lowest = ref[:, :FACE].astype(jnp.float32)
        highest = ref[:, FACE : 2 * FACE].astype(jnp.float32)
        near_ref[rows, :] = jnp.where(odd, lowest, highest).astype(jnp.bfloat16)
        far_ref[rows, :] = jnp.where(odd, highest, lowest).astype(jnp.bfloat16)


def by_side(near, far):
    odd = (lax.axis_index("blk") & 1) == 1
    near = near.astype(jnp.float32)
    far = far.astype(jnp.float32)
    return jnp.where(odd, near, far), jnp.where(odd, far, near)


def gather_kernel(x_ref, rule_ref, dense_ref, table):
    table[...] = x_ref[...].astype(jnp.float32)
    for k in range(27):
        row = rule_ref[k : k + 1, :]
        for group in range(8):
            tiles = source_tiles(group, k % 3 - 1)
            if tiles[0] >= 8:
                continue
            got = picked(row, group, tiles, lambda t: table[:, tile_span(t)])
            dense_ref[32 * k : 32 * k + 32, tile_span(group)] = got.astype(jnp.bfloat16)


def faces_kernel(x_ref, g_ref, near_ref, far_ref):
    odd = (lax.axis_index("blk") & 1) == 1
    for rows, ref in ((slice(0, 32), x_ref), (slice(32, 64), g_ref)):
        lowest = ref[:, :FACE].astype(jnp.float32)
        highest = ref[:, FACE : 2 * FACE].astype(jnp.float32)
        near_ref[rows, :] = jnp.where(odd, lowest, highest).astype(jnp.bfloat16)
        far_ref[rows, :] = jnp.where(odd, highest, lowest).astype(jnp.bfloat16)


def by_side(near, far):
    odd = (lax.axis_index("blk") & 1) == 1
    near = near.astype(jnp.float32)
    far = far.astype(jnp.float32)
    return jnp.where(odd, near, far), jnp.where(odd, far, near)


def gather_kernel(x_ref, rule_ref, dense_ref, table):
    table[...] = x_ref[...].astype(jnp.float32)

    def step(j, carry):
        for d in range(3):
            k = 3 * j + d
            row = rule_ref[pl.ds(k, 1), :]
            for group in range(8):
                tiles = source_tiles(group, d - 1)
                if tiles[0] >= 8:
                    continue
                got = picked(row, group, tiles, lambda t: table[:, tile_span(t)])
                rows = pl.ds(pl.multiple_of(32 * k, 32), 32)
                dense_ref[rows, tile_span(group)] = got.astype(jnp.bfloat16)
        return carry

    lax.fori_loop(0, 9, step, 0)


def weight_kernel(
    dense_in, rule_ref, near_ref, far_ref, pair_ref, other_ref,
    dense_ref, grad_ref, keep_ref, send_ref, faces, terms,
):
    chan = lax.axis_index("ch")
    spot = own_part()
    for i, m in enumerate(ORDER):
        part = (pair_ref if i < 2 else other_ref)[32 * (i % 2) : 32 * (i % 2) + 32, :]
        grad_ref[pl.ds(pl.multiple_of(32 * (chan ^ m), 32), 32), :] = part
    faces[:, :FACE], faces[:, FACE:] = by_side(near_ref[:32, :], far_ref[:32, :])

    for j in range(9):
        for group, d in ((0, 0), (1, 2)):
            k = 3 * j + d
            row = rule_ref[k : k + 1, :]
            got = picked(row, group, (8 + group,), lambda t: faces[:, tile_span(t - 8)])
            dense_ref[32 * k : 32 * k + 32, tile_span(group)] = got.astype(jnp.bfloat16)
    terms[:864, :] = lax.dot_general(
        dense_ref[...], grad_ref[...], (((1,), (1,)), ((), ())),
        preferred_element_type=jnp.float32,
    ) * (1.0 / 256.0)
    terms[864:, :] = jnp.zeros((32, LANES), jnp.float32)
    for q in range(4):
        for odd, target in ((0, keep_ref), (1, send_ref)):
            start = pl.multiple_of(PART * (spot ^ (2 * q + odd)), 8)
            target[PART * q : PART * (q + 1), :] = terms[pl.ds(start, PART), :]


def forward_kernel(dense_ref, weight_ref, near_ref, far_ref, keep_ref, send_ref, sums):
    chan = lax.axis_index("ch")
    sums[...] = lax.dot_general(
        weight_ref[...], dense_ref[...], (((0,), (0,)), ((), ())),
        preferred_element_type=jnp.float32,
    )
    for target, parts in ((keep_ref, (0, 3)), (send_ref, (1, 2))):
        for i, m in enumerate(parts):
            rows = pl.ds(pl.multiple_of(32 * (chan ^ m), 32), 32)
            target[32 * i : 32 * i + 32, :VOX] = sums[rows, :]
    lower, upper = by_side(near_ref[32:, :], far_ref[32:, :])
    send_ref[:32, VOX:] = lower
    send_ref[32:, VOX:] = upper


def middle_kernel(keep_ref, came_ref, near_ref, far_ref, own_ref, send_ref):
    own_ref[...] = keep_ref[:32, :] + came_ref[:32, :VOX]
    send_ref[:, :VOX] = keep_ref[32:, :] + came_ref[32:, :VOX]
    lower, upper = by_side(near_ref[32:, :], far_ref[32:, :])
    send_ref[:, VOX : VOX + FACE] = lower
    send_ref[:, VOX + FACE : VOX + 2 * FACE] = upper
    send_ref[:, VOX + 2 * FACE : VOX + 3 * FACE] = came_ref[:32, VOX:]
    send_ref[:, VOX + 3 * FACE :] = came_ref[32:, VOX:]


def back_terms_kernel(weight_ref, grad_ref, terms_ref):
    terms_ref[...] = jnp.dot(
        weight_ref[...], grad_ref[...], preferred_element_type=jnp.float32
    )


def back_sum(groups, rule_ref, load):
    totals = {}
    for k in range(27):
        row = rule_ref[k : k + 1, :]
        rows = slice(32 * (26 - k), 32 * (26 - k) + 32)
        for group in groups:
            got = picked(row, group, source_tiles(group, k % 3 - 1), lambda t: load(rows, t))
            totals[group] = got if k == 0 else totals[group] + got
    return totals


def back_inner_kernel(groups, terms, rule_ref, *refs):
    totals = back_sum(groups, rule_ref, lambda rows, t: terms[rows, tile_span(t)])
    for group in groups:
        refs[-1][:, tile_span(group)] = totals[group]


def edge_kernel(
    terms, rule_ref, weight_ref, near_ref, far_ref, inner, own_ref, first_ref, second_ref,
    out_ref, grad_ref, faces, products,
):
    chan = lax.axis_index("ch")
    out_ref[...] = (own_ref[...] + second_ref[:, :VOX]).astype(jnp.bfloat16)
    lower, upper = by_side(near_ref[32:, :], far_ref[32:, :])
    pairs = (
        (lower, upper),
        (first_ref[:32, VOX:], first_ref[32:, VOX:]),
        (second_ref[:, VOX : VOX + FACE], second_ref[:, VOX + FACE : VOX + 2 * FACE]),
        (second_ref[:, VOX + 2 * FACE : VOX + 3 * FACE], second_ref[:, VOX + 3 * FACE :]),
    )
    for m, (lower, upper) in zip(ORDER, pairs):
        rows = pl.ds(pl.multiple_of(32 * (chan ^ m), 32), 32)
        faces[rows, :FACE] = lower.astype(jnp.bfloat16)
        faces[rows, FACE:] = upper.astype(jnp.bfloat16)
    products[...] = jnp.dot(
        weight_ref[...], faces[...], preferred_element_type=jnp.float32
    )
    totals = back_sum(
        EDGE, rule_ref,
        lambda rows, t: products[rows, tile_span(t - 8)] if t >= 8 else terms[rows, tile_span(t)],
    )
    for group in range(8):
        values = totals[group] if group in EDGE else inner[:, tile_span(group)]
        grad_ref[:, tile_span(group)] = values.astype(jnp.bfloat16)


def split_sum_kernel(keep_ref, came_ref, *outs):
    for q, out in enumerate(outs):
        rows = slice(PART * q, PART * (q + 1))
        out[...] = keep_ref[rows, :] + came_ref[rows, :]


def sum_kernel(*refs):
    values = [ref[...] for ref in refs[:-1]]
    while len(values) > 1:
        values = [values[i] + values[i + 1] for i in range(0, len(values), 2)]
    refs[-1][...] = values[0]


def join_kernel(*refs):
    size = refs[0].shape[0]
    for q, ref in enumerate(refs[:-1]):
        refs[-1][size * q : size * (q + 1), :] = ref[...]


def place_kernel(even_ref, odd_ref, out_ref):
    spot = own_part()
    short = 864 - 7 * PART
    for q in range(4):
        for odd, ref in enumerate((even_ref, odd_ref)):
            part = spot ^ (2 * q + odd)
            start = pl.multiple_of(PART * part, 8)
            out_ref[pl.ds(start, short), :] = ref[PART * q : PART * q + short, :]

            @pl.when(part < 7)
            def _():
                rows = pl.ds(pl.multiple_of(start + short, 8), PART - short)
                out_ref[rows, :] = ref[PART * q + short : PART * (q + 1), :]


def call(kernel, outs, args, scratch=(), aliases=None, flops=0, name=None):
    moved = sum(a.size * a.dtype.itemsize for a in list(args) + jax.tree.leaves(outs))
    return pl.pallas_call(
        kernel,
        out_shape=outs,
        in_specs=[VMEM] * len(args),
        out_specs=jax.tree.map(lambda _: VMEM, outs),
        scratch_shapes=list(scratch),
        input_output_aliases=aliases or {},
        compiler_params=pltpu.CompilerParams(vmem_limit_bytes=40 << 20),
        cost_estimate=pl.CostEstimate(flops=flops, bytes_accessed=moved, transcendentals=0),
        name=name,
    )(*args)


def f32(*shape):
    return jax.ShapeDtypeStruct(shape, jnp.float32)


def bf16(*shape):
    return jax.ShapeDtypeStruct(shape, jnp.bfloat16)


def swap(value, mask):
    count = lax.axis_size("blk")
    return lax.ppermute(value, "blk", [(i, i ^ mask) for i in range(count)])


def swap_far(value):
    count = lax.axis_size("blk")
    pairs = [(i, (i + 1 if i % 2 else i - 1) % count) for i in range(count)]
    return lax.ppermute(value, "blk", pairs)


def after(values, *others):
    return lax.optimization_barrier((*values, *others))[: len(values)]


def per_device(features, weight, grad_out, rulebook):
    weights = weight.reshape(864, 128)

    def over_ch(value, mask):
        return lax.ppermute(value, "ch", [(i, i ^ mask) for i in range(4)])

    x, g, rules = features, grad_out, rulebook
    cut = pl.BlockSpec((32, 2 * FACE), lambda i: (0, 0))
    face = pl.BlockSpec((64, FACE), lambda i: (0, 0))
    near, far = pl.pallas_call(
        faces_kernel, out_shape=(bf16(64, FACE),) * 2, grid=(1,),
        in_specs=[cut, cut], out_specs=(face, face),
        compiler_params=pltpu.CompilerParams(vmem_limit_bytes=56 << 20),
        cost_estimate=pl.CostEstimate(flops=1 << 30, bytes_accessed=1 << 16, transcendentals=0),
        name="faces",
    )(x, g)
    pair = call(join_kernel, bf16(64, VOX), (g, over_ch(g, 1)), name="join")
    near = swap(near, 1)
    far = swap_far(far)
    other = over_ch(pair, 3)
    dense = call(
        gather_kernel, bf16(864, VOX), (x, rules),
        [pltpu.VMEM((32, VOX), jnp.float32)], flops=3 << 30, name="gather",
    )
    dense, grads, keep, send = call(
        weight_kernel,
        (bf16(864, VOX), bf16(128, VOX), f32(4 * PART, 128), f32(4 * PART, 128)),
        (dense, rules, near, far, pair, other),
        [pltpu.VMEM((32, 2 * FACE), jnp.float32), pltpu.VMEM((8 * PART, 128), jnp.float32)],
        aliases={0: 0}, flops=1 << 30, name="weight_terms",
    )

    def inner_part(groups, inner=None):
        args = (back, rules) if inner is None else (back, rules, inner)
        return call(
            functools.partial(back_inner_kernel, groups), f32(32, VOX), args,
            aliases=None if inner is None else {2: 0}, flops=len(groups) << 30,
            name="back_inner",
        )

    came = swap(send, 1)
    ours, first = call(
        forward_kernel, (f32(64, VOX), f32(64, VOX + FACE)), (dense, weights, near, far),
        [pltpu.VMEM((128, VOX), jnp.float32)], flops=1 << 30, name="forward",
    )
    back = call(
        back_terms_kernel, f32(864, VOX), (weights, grads), flops=1 << 30, name="back_terms"
    )
    came, = after((came,), ours, back)
    pieces = call(split_sum_kernel, (f32(PART, 128),) * 4, (keep, came), name="sum_pair")
    others = [swap(pieces[q], m) for q, m in ((1, X1), (2, Z1), (3, X1 | Z1))]
    first, = after((first,), *pieces)
    first = over_ch(first, 1)
    inner = inner_part((2, 3))
    others = after(others, inner)
    total = call(sum_kernel, f32(PART, 128), (pieces[0], *others), name="sum_four")
    came = swap(total, Z6)
    inner = inner_part((4, 5, 6), inner)
    ours, first = after((ours, first), inner)
    own, second = call(
        middle_kernel, (f32(32, VOX), f32(32, VOX + 4 * FACE)), (ours, first, near, far),
        name="middle",
    )
    second = over_ch(second, 3)
    came, = after((came,), own)
    total = call(sum_kernel, f32(PART, 128), (total, came), name="sum_two")
    others = [swap(total, m) for m in (X3, Z2, X3 | Z2)]
    inner = inner_part((7,), inner)
    others = after(others, inner)
    total = call(sum_kernel, f32(PART, 128), (total, *others), name="sum_four")
    others = [swap(total, m) for m in (X1, Z1, X1 | Z1)]
    output, grad_features = call(
        edge_kernel, (bf16(32, VOX), bf16(32, VOX)),
        (back, rules, weights, near, far, inner, own, first, second),
        [pltpu.VMEM((128, 2 * FACE), jnp.bfloat16), pltpu.VMEM((864, 2 * FACE), jnp.float32)],
        flops=2 << 30, name="edge",
    )
    others = after(others, output)
    even = call(join_kernel, f32(4 * PART, 128), (total, *others), name="join")
    odd = swap(even, 1)
    weight_grad = call(
        place_kernel, f32(864, 128), (even, odd), name="place",
    )
    return output, grad_features, weight_grad.reshape(27, 32, 128)


def solution(mesh):
    placed = (P("ch", "blk"), P(None, "ch", None), P("ch", "blk"), P(None, "blk"))
    return jax.shard_map(
        per_device,
        mesh=mesh,
        in_specs=placed,
        out_specs=(P("ch", "blk"), P("ch", "blk"), P(None, "ch", None)),
        check_vma=False,
    )
```

```python
import functools

import jax
import jax.numpy as jnp
from jax import lax
from jax.experimental import pallas as pl
from jax.experimental.pallas import tpu as pltpu
from jax.sharding import PartitionSpec as P

VOX = 1024
FACE = 128
LANES = 128
PART = 112
INNER = tuple(range(2, 8))
EDGE = (0, 1)
X1, X3, Z1, Z3, Z6 = 2, 6, 8, 24, 48
ORDER = (0, 1, 3, 2)
VMEM = pl.BlockSpec(memory_space=pltpu.VMEM)


def source_tiles(group, dz):
    if group == 0:
        return {-1: (8,), 0: (0,), 1: INNER}[dz]
    if group == 1:
        return {-1: INNER, 0: (1,), 1: (9,)}[dz]
    return {-1: (0,) + INNER, 0: INNER, 1: (1,) + INNER}[dz]


def picked(row, group, tiles, load):
    span = row[:, LANES * group : LANES * (group + 1)]
    index = jnp.broadcast_to(span, (32, LANES))
    lane = index & (LANES - 1)
    tile = index >> 7
    total = jnp.zeros((32, LANES), jnp.float32)
    for t in tiles:
        values = jnp.take_along_axis(load(t), lane, axis=1, mode="promise_in_bounds")
        total = jnp.where(tile == t, values, total)
    return total


def own_part():
    place = lax.axis_index("blk")
    over_x = (place >> 1) ^ (place >> 2)
    over_z = (place >> 3) ^ (place >> 4) ^ (place >> 5)
    return (place & 1) | ((over_x & 1) << 1) | ((over_z & 1) << 2)


def tile_span(t):
    return slice(LANES * t, LANES * (t + 1))


def faces_kernel(x_ref, g_ref, near_ref, far_ref):
    odd = (lax.axis_index("blk") & 1) == 1
    for rows, ref in ((slice(0, 32), x_ref), (slice(32, 64), g_ref)):
        lowest = ref[:, :FACE].astype(jnp.float32)
        highest = ref[:, FACE : 2 * FACE].astype(jnp.float32)
        near_ref[rows, :] = jnp.where(odd, lowest, highest).astype(jnp.bfloat16)
        far_ref[rows, :] = jnp.where(odd, highest, lowest).astype(jnp.bfloat16)


def by_side(near, far):
    odd = (lax.axis_index("blk") & 1) == 1
    near = near.astype(jnp.float32)
    far = far.astype(jnp.float32)
    return jnp.where(odd, near, far), jnp.where(odd, far, near)


def gather_kernel(x_ref, rule_ref, dense_ref, table):
    table[...] = x_ref[...].astype(jnp.float32)
    for k in range(27):
        row = rule_ref[k : k + 1, :]
        for group in range(8):
            tiles = source_tiles(group, k % 3 - 1)
            if tiles[0] >= 8:
                continue
            got = picked(row, group, tiles, lambda t: table[:, tile_span(t)])
            dense_ref[32 * k : 32 * k + 32, tile_span(group)] = got.astype(jnp.bfloat16)


def faces_kernel(x_ref, g_ref, near_ref, far_ref):
    odd = (lax.axis_index("blk") & 1) == 1
    for rows, ref in ((slice(0, 32), x_ref), (slice(32, 64), g_ref)):
        lowest = ref[:, :FACE].astype(jnp.float32)
        highest = ref[:, FACE : 2 * FACE].astype(jnp.float32)
        near_ref[rows, :] = jnp.where(odd, lowest, highest).astype(jnp.bfloat16)
        far_ref[rows, :] = jnp.where(odd, highest, lowest).astype(jnp.bfloat16)


def by_side(near, far):
    odd = (lax.axis_index("blk") & 1) == 1
    near = near.astype(jnp.float32)
    far = far.astype(jnp.float32)
    return jnp.where(odd, near, far), jnp.where(odd, far, near)


def gather_kernel(x_ref, rule_ref, dense_ref, table):
    table[...] = x_ref[...].astype(jnp.float32)

    def step(j, carry):
        for d in range(3):
            k = 3 * j + d
            row = rule_ref[pl.ds(k, 1), :]
            for group in range(8):
                tiles = source_tiles(group, d - 1)
                if tiles[0] >= 8:
                    continue
                got = picked(row, group, tiles, lambda t: table[:, tile_span(t)])
                rows = pl.ds(pl.multiple_of(32 * k, 32), 32)
                dense_ref[rows, tile_span(group)] = got.astype(jnp.bfloat16)
        return carry

    lax.fori_loop(0, 9, step, 0)


def weight_kernel(
    dense_in, rule_ref, near_ref, far_ref, pair_ref, other_ref,
    dense_ref, grad_ref, keep_ref, send_ref, faces, terms,
):
    chan = lax.axis_index("ch")
    spot = own_part()
    for i, m in enumerate(ORDER):
        part = (pair_ref if i < 2 else other_ref)[32 * (i % 2) : 32 * (i % 2) + 32, :]
        grad_ref[pl.ds(pl.multiple_of(32 * (chan ^ m), 32), 32), :] = part
    faces[:, :FACE], faces[:, FACE:] = by_side(near_ref[:32, :], far_ref[:32, :])

    for j in range(9):
        for group, d in ((0, 0), (1, 2)):
            k = 3 * j + d
            row = rule_ref[k : k + 1, :]
            got = picked(row, group, (8 + group,), lambda t: faces[:, tile_span(t - 8)])
            dense_ref[32 * k : 32 * k + 32, tile_span(group)] = got.astype(jnp.bfloat16)
    terms[:864, :] = lax.dot_general(
        dense_ref[...], grad_ref[...], (((1,), (1,)), ((), ())),
        preferred_element_type=jnp.float32,
    ) * (1.0 / 256.0)
    terms[864:, :] = jnp.zeros((32, LANES), jnp.float32)
    for q in range(4):
        for odd, target in ((0, keep_ref), (1, send_ref)):
            start = pl.multiple_of(PART * (spot ^ (2 * q + odd)), 8)
            target[PART * q : PART * (q + 1), :] = terms[pl.ds(start, PART), :]


def forward_kernel(dense_ref, weight_ref, near_ref, far_ref, keep_ref, send_ref, sums):
    chan = lax.axis_index("ch")
    sums[...] = lax.dot_general(
        weight_ref[...], dense_ref[...], (((0,), (0,)), ((), ())),
        preferred_element_type=jnp.float32,
    )
    for target, parts in ((keep_ref, (0, 3)), (send_ref, (1, 2))):
        for i, m in enumerate(parts):
            rows = pl.ds(pl.multiple_of(32 * (chan ^ m), 32), 32)
            target[32 * i : 32 * i + 32, :VOX] = sums[rows, :]
    lower, upper = by_side(near_ref[32:, :], far_ref[32:, :])
    send_ref[:32, VOX:] = lower
    send_ref[32:, VOX:] = upper


def middle_kernel(keep_ref, came_ref, near_ref, far_ref, own_ref, send_ref):
    own_ref[...] = keep_ref[:32, :] + came_ref[:32, :VOX]
    send_ref[:, :VOX] = keep_ref[32:, :] + came_ref[32:, :VOX]
    lower, upper = by_side(near_ref[32:, :], far_ref[32:, :])
    send_ref[:, VOX : VOX + FACE] = lower
    send_ref[:, VOX + FACE : VOX + 2 * FACE] = upper
    send_ref[:, VOX + 2 * FACE : VOX + 3 * FACE] = came_ref[:32, VOX:]
    send_ref[:, VOX + 3 * FACE :] = came_ref[32:, VOX:]


def back_terms_kernel(weight_ref, grad_ref, terms_ref):
    terms_ref[...] = jnp.dot(
        weight_ref[...], grad_ref[...], preferred_element_type=jnp.float32
    )


def back_sum(groups, rule_ref, load):
    totals = {}
    for k in range(27):
        row = rule_ref[k : k + 1, :]
        rows = slice(32 * (26 - k), 32 * (26 - k) + 32)
        for group in groups:
            got = picked(row, group, source_tiles(group, k % 3 - 1), lambda t: load(rows, t))
            totals[group] = got if k == 0 else totals[group] + got
    return totals


def back_inner_kernel(groups, terms, rule_ref, *refs):
    totals = back_sum(groups, rule_ref, lambda rows, t: terms[rows, tile_span(t)])
    for group in groups:
        refs[-1][:, tile_span(group)] = totals[group]


def edge_kernel(
    terms, rule_ref, weight_ref, near_ref, far_ref, inner, own_ref, first_ref, second_ref,
    out_ref, grad_ref, faces, products,
):
    chan = lax.axis_index("ch")
    out_ref[...] = (own_ref[...] + second_ref[:, :VOX]).astype(jnp.bfloat16)
    lower, upper = by_side(near_ref[32:, :], far_ref[32:, :])
    pairs = (
        (lower, upper),
        (first_ref[:32, VOX:], first_ref[32:, VOX:]),
        (second_ref[:, VOX : VOX + FACE], second_ref[:, VOX + FACE : VOX + 2 * FACE]),
        (second_ref[:, VOX + 2 * FACE : VOX + 3 * FACE], second_ref[:, VOX + 3 * FACE :]),
    )
    for m, (lower, upper) in zip(ORDER, pairs):
        rows = pl.ds(pl.multiple_of(32 * (chan ^ m), 32), 32)
        faces[rows, :FACE] = lower.astype(jnp.bfloat16)
        faces[rows, FACE:] = upper.astype(jnp.bfloat16)
    products[...] = jnp.dot(
        weight_ref[...], faces[...], preferred_element_type=jnp.float32
    )
    totals = back_sum(
        EDGE, rule_ref,
        lambda rows, t: products[rows, tile_span(t - 8)] if t >= 8 else terms[rows, tile_span(t)],
    )
    for group in range(8):
        values = totals[group] if group in EDGE else inner[:, tile_span(group)]
        grad_ref[:, tile_span(group)] = values.astype(jnp.bfloat16)


def split_sum_kernel(keep_ref, came_ref, *outs):
    for q, out in enumerate(outs):
        rows = slice(PART * q, PART * (q + 1))
        out[...] = keep_ref[rows, :] + came_ref[rows, :]


def sum_kernel(*refs):
    values = [ref[...] for ref in refs[:-1]]
    while len(values) > 1:
        values = [values[i] + values[i + 1] for i in range(0, len(values), 2)]
    refs[-1][...] = values[0]


def join_kernel(*refs):
    size = refs[0].shape[0]
    for q, ref in enumerate(refs[:-1]):
        refs[-1][size * q : size * (q + 1), :] = ref[...]


def place_kernel(even_ref, odd_ref, out_ref):
    spot = own_part()
    short = 864 - 7 * PART
    for q in range(4):
        for odd, ref in enumerate((even_ref, odd_ref)):
            part = spot ^ (2 * q + odd)
            start = pl.multiple_of(PART * part, 8)
            out_ref[pl.ds(start, short), :] = ref[PART * q : PART * q + short, :]

            @pl.when(part < 7)
            def _():
                rows = pl.ds(pl.multiple_of(start + short, 8), PART - short)
                out_ref[rows, :] = ref[PART * q + short : PART * (q + 1), :]


def call(kernel, outs, args, scratch=(), aliases=None, flops=0, name=None):
    moved = sum(a.size * a.dtype.itemsize for a in list(args) + jax.tree.leaves(outs))
    return pl.pallas_call(
        kernel,
        out_shape=outs,
        in_specs=[VMEM] * len(args),
        out_specs=jax.tree.map(lambda _: VMEM, outs),
        scratch_shapes=list(scratch),
        input_output_aliases=aliases or {},
        compiler_params=pltpu.CompilerParams(vmem_limit_bytes=40 << 20),
        cost_estimate=pl.CostEstimate(flops=flops, bytes_accessed=moved, transcendentals=0),
        name=name,
    )(*args)


def f32(*shape):
    return jax.ShapeDtypeStruct(shape, jnp.float32)


def bf16(*shape):
    return jax.ShapeDtypeStruct(shape, jnp.bfloat16)


def swap(value, mask):
    count = lax.axis_size("blk")
    return lax.ppermute(value, "blk", [(i, i ^ mask) for i in range(count)])


def swap_far(value):
    count = lax.axis_size("blk")
    pairs = [(i, (i + 1 if i % 2 else i - 1) % count) for i in range(count)]
    return lax.ppermute(value, "blk", pairs)


def after(values, *others):
    return lax.optimization_barrier((*values, *others))[: len(values)]


def per_device(features, weight, grad_out, rulebook):
    weights = weight.reshape(864, 128)

    def over_ch(value, mask):
        return lax.ppermute(value, "ch", [(i, i ^ mask) for i in range(4)])

    x, g, rules = features, grad_out, rulebook
    cut = pl.BlockSpec((32, 2 * FACE), lambda i: (0, 0))
    face = pl.BlockSpec((64, FACE), lambda i: (0, 0))
    near, far = pl.pallas_call(
        faces_kernel, out_shape=(bf16(64, FACE),) * 2, grid=(1,),
        in_specs=[cut, cut], out_specs=(face, face),
        compiler_params=pltpu.CompilerParams(vmem_limit_bytes=56 << 20),
        cost_estimate=pl.CostEstimate(flops=1 << 30, bytes_accessed=1 << 16, transcendentals=0),
        name="faces",
    )(x, g)
    pair = call(join_kernel, bf16(64, VOX), (g, over_ch(g, 1)), name="join")
    near = swap(near, 1)
    far = swap_far(far)
    other = over_ch(pair, 3)
    dense = call(
        gather_kernel, bf16(864, VOX), (x, rules),
        [pltpu.VMEM((32, VOX), jnp.float32)], flops=3 << 30, name="gather",
    )
    dense, grads, keep, send = call(
        weight_kernel,
        (bf16(864, VOX), bf16(128, VOX), f32(4 * PART, 128), f32(4 * PART, 128)),
        (dense, rules, near, far, pair, other),
        [pltpu.VMEM((32, 2 * FACE), jnp.float32), pltpu.VMEM((8 * PART, 128), jnp.float32)],
        aliases={0: 0}, flops=1 << 30, name="weight_terms",
    )

    def inner_part(groups, inner=None):
        args = (back, rules) if inner is None else (back, rules, inner)
        return call(
            functools.partial(back_inner_kernel, groups), f32(32, VOX), args,
            aliases=None if inner is None else {2: 0}, flops=len(groups) << 30,
            name="back_inner",
        )

    came = swap(send, 1)
    ours, first = call(
        forward_kernel, (f32(64, VOX), f32(64, VOX + FACE)), (dense, weights, near, far),
        [pltpu.VMEM((128, VOX), jnp.float32)], flops=1 << 30, name="forward",
    )
    back = call(
        back_terms_kernel, f32(864, VOX), (weights, grads), flops=1 << 30, name="back_terms"
    )
    came, = after((came,), ours, back)
    pieces = call(split_sum_kernel, (f32(PART, 128),) * 4, (keep, came), name="sum_pair")
    others = [swap(pieces[q], m) for q, m in ((1, X1), (2, Z1), (3, X1 | Z1))]
    first, = after((first,), *pieces)
    first = over_ch(first, 1)
    inner = inner_part((2, 3))
    others = after(others, inner)
    total = call(sum_kernel, f32(PART, 128), (pieces[0], *others), name="sum_four")
    came = swap(total, X3)
    inner = inner_part((4, 5), inner)
    came, = after((came,), inner)
    total = call(sum_kernel, f32(PART, 128), (total, came), name="sum_two")
    others = [swap(total, m) for m in (Z3, Z6, Z3 ^ Z6)]
    ours, first = after((ours, first), total)
    own, second = call(
        middle_kernel, (f32(32, VOX), f32(32, VOX + 4 * FACE)), (ours, first, near, far),
        name="middle",
    )
    second = over_ch(second, 3)
    inner = inner_part((6, 7), inner)
    others = after(others, inner, own)
    total = call(sum_kernel, f32(PART, 128), (total, *others), name="sum_four")
    others = [swap(total, m) for m in (X1, Z1, X1 | Z1)]
    output, grad_features = call(
        edge_kernel, (bf16(32, VOX), bf16(32, VOX)),
        (back, rules, weights, near, far, inner, own, first, second),
        [pltpu.VMEM((128, 2 * FACE), jnp.bfloat16), pltpu.VMEM((864, 2 * FACE), jnp.float32)],
        flops=2 << 30, name="edge",
    )
    others = after(others, output)
    even = call(join_kernel, f32(4 * PART, 128), (total, *others), name="join")
    odd = swap(even, 1)
    weight_grad = call(
        place_kernel, f32(864, 128), (even, odd), name="place",
    )
    return output, grad_features, weight_grad.reshape(27, 32, 128)


def solution(mesh):
    placed = (P("ch", "blk"), P(None, "ch", None), P("ch", "blk"), P(None, "blk"))
    return jax.shard_map(
        per_device,
        mesh=mesh,
        in_specs=placed,
        out_specs=(P("ch", "blk"), P("ch", "blk"), P(None, "ch", None)),
        check_vma=False,
    )
```

```python
import functools

import jax
import jax.numpy as jnp
from jax import lax
from jax.experimental import pallas as pl
from jax.experimental.pallas import tpu as pltpu
from jax.sharding import PartitionSpec as P

VOX = 1024
FACE = 128
LANES = 128
PART = 112
INNER = tuple(range(2, 8))
EDGE = (0, 1)
X1, X3, Z1, Z3, Z6 = 2, 6, 8, 24, 48
ORDER = (0, 1, 3, 2)
VMEM = pl.BlockSpec(memory_space=pltpu.VMEM)


def source_tiles(group, dz):
    if group == 0:
        return {-1: (8,), 0: (0,), 1: INNER}[dz]
    if group == 1:
        return {-1: INNER, 0: (1,), 1: (9,)}[dz]
    return {-1: (0,) + INNER, 0: INNER, 1: (1,) + INNER}[dz]


def picked(row, group, tiles, load):
    span = row[:, LANES * group : LANES * (group + 1)]
    index = jnp.broadcast_to(span, (32, LANES))
    lane = index & (LANES - 1)
    tile = index >> 7
    total = jnp.zeros((32, LANES), jnp.float32)
    for t in tiles:
        values = jnp.take_along_axis(load(t), lane, axis=1, mode="promise_in_bounds")
        total = jnp.where(tile == t, values, total)
    return total


def own_part():
    place = lax.axis_index("blk")
    over_x = (place >> 1) ^ (place >> 2)
    over_z = (place >> 3) ^ (place >> 4) ^ (place >> 5)
    return (place & 1) | ((over_x & 1) << 1) | ((over_z & 1) << 2)


def tile_span(t):
    return slice(LANES * t, LANES * (t + 1))


def faces_kernel(x_ref, g_ref, near_ref, far_ref):
    odd = (lax.axis_index("blk") & 1) == 1
    for rows, ref in ((slice(0, 32), x_ref), (slice(32, 64), g_ref)):
        lowest = ref[:, :FACE].astype(jnp.float32)
        highest = ref[:, FACE : 2 * FACE].astype(jnp.float32)
        near_ref[rows, :] = jnp.where(odd, lowest, highest).astype(jnp.bfloat16)
        far_ref[rows, :] = jnp.where(odd, highest, lowest).astype(jnp.bfloat16)


def by_side(near, far):
    odd = (lax.axis_index("blk") & 1) == 1
    near = near.astype(jnp.float32)
    far = far.astype(jnp.float32)
    return jnp.where(odd, near, far), jnp.where(odd, far, near)


def gather_kernel(x_ref, rule_ref, dense_ref, table):
    table[...] = x_ref[...].astype(jnp.float32)
    for k in range(27):
        row = rule_ref[k : k + 1, :]
        for group in range(8):
            tiles = source_tiles(group, k % 3 - 1)
            if tiles[0] >= 8:
                continue
            got = picked(row, group, tiles, lambda t: table[:, tile_span(t)])
            dense_ref[32 * k : 32 * k + 32, tile_span(group)] = got.astype(jnp.bfloat16)


def faces_kernel(x_ref, g_ref, near_ref, far_ref):
    odd = (lax.axis_index("blk") & 1) == 1
    for rows, ref in ((slice(0, 32), x_ref), (slice(32, 64), g_ref)):
        lowest = ref[:, :FACE].astype(jnp.float32)
        highest = ref[:, FACE : 2 * FACE].astype(jnp.float32)
        near_ref[rows, :] = jnp.where(odd, lowest, highest).astype(jnp.bfloat16)
        far_ref[rows, :] = jnp.where(odd, highest, lowest).astype(jnp.bfloat16)


def by_side(near, far):
    odd = (lax.axis_index("blk") & 1) == 1
    near = near.astype(jnp.float32)
    far = far.astype(jnp.float32)
    return jnp.where(odd, near, far), jnp.where(odd, far, near)


def gather_kernel(x_ref, rule_ref, dense_ref, table):
    table[...] = x_ref[...].astype(jnp.float32)

    def step(j, carry):
        for d in range(3):
            k = 3 * j + d
            row = rule_ref[pl.ds(k, 1), :]
            for group in range(8):
                tiles = source_tiles(group, d - 1)
                if tiles[0] >= 8:
                    continue
                got = picked(row, group, tiles, lambda t: table[:, tile_span(t)])
                rows = pl.ds(pl.multiple_of(32 * k, 32), 32)
                dense_ref[rows, tile_span(group)] = got.astype(jnp.bfloat16)
        return carry

    lax.fori_loop(0, 9, step, 0)


def weight_kernel(
    dense_in, rule_ref, near_ref, far_ref, pair_ref, other_ref,
    dense_ref, grad_ref, keep_ref, send_ref, faces, terms,
):
    chan = lax.axis_index("ch")
    spot = own_part()
    for i, m in enumerate(ORDER):
        part = (pair_ref if i < 2 else other_ref)[32 * (i % 2) : 32 * (i % 2) + 32, :]
        grad_ref[pl.ds(pl.multiple_of(32 * (chan ^ m), 32), 32), :] = part
    faces[:, :FACE], faces[:, FACE:] = by_side(near_ref[:32, :], far_ref[:32, :])

    for j in range(9):
        for group, d in ((0, 0), (1, 2)):
            k = 3 * j + d
            row = rule_ref[k : k + 1, :]
            got = picked(row, group, (8 + group,), lambda t: faces[:, tile_span(t - 8)])
            dense_ref[32 * k : 32 * k + 32, tile_span(group)] = got.astype(jnp.bfloat16)
    terms[:864, :] = lax.dot_general(
        dense_ref[...], grad_ref[...], (((1,), (1,)), ((), ())),
        preferred_element_type=jnp.float32,
    ) * (1.0 / 256.0)
    terms[864:, :] = jnp.zeros((32, LANES), jnp.float32)
    for q in range(4):
        for odd, target in ((0, keep_ref), (1, send_ref)):
            start = pl.multiple_of(PART * (spot ^ (2 * q + odd)), 8)
            target[PART * q : PART * (q + 1), :] = terms[pl.ds(start, PART), :]


def forward_kernel(dense_ref, weight_ref, near_ref, far_ref, keep_ref, send_ref, sums):
    chan = lax.axis_index("ch")
    sums[...] = lax.dot_general(
        weight_ref[...], dense_ref[...], (((0,), (0,)), ((), ())),
        preferred_element_type=jnp.float32,
    )
    for target, parts in ((keep_ref, (0, 3)), (send_ref, (1, 2))):
        for i, m in enumerate(parts):
            rows = pl.ds(pl.multiple_of(32 * (chan ^ m), 32), 32)
            target[32 * i : 32 * i + 32, :VOX] = sums[rows, :]
    lower, upper = by_side(near_ref[32:, :], far_ref[32:, :])
    send_ref[:32, VOX:] = lower
    send_ref[32:, VOX:] = upper


def middle_kernel(keep_ref, came_ref, near_ref, far_ref, own_ref, send_ref):
    own_ref[...] = keep_ref[:32, :] + came_ref[:32, :VOX]
    send_ref[:, :VOX] = keep_ref[32:, :] + came_ref[32:, :VOX]
    lower, upper = by_side(near_ref[32:, :], far_ref[32:, :])
    send_ref[:, VOX : VOX + FACE] = lower
    send_ref[:, VOX + FACE : VOX + 2 * FACE] = upper
    send_ref[:, VOX + 2 * FACE : VOX + 3 * FACE] = came_ref[:32, VOX:]
    send_ref[:, VOX + 3 * FACE :] = came_ref[32:, VOX:]


def back_terms_kernel(weight_ref, grad_ref, terms_ref):
    terms_ref[...] = jnp.dot(
        weight_ref[...], grad_ref[...], preferred_element_type=jnp.float32
    )


def back_sum(groups, rule_ref, load):
    totals = {}
    for k in range(27):
        row = rule_ref[k : k + 1, :]
        rows = slice(32 * (26 - k), 32 * (26 - k) + 32)
        for group in groups:
            got = picked(row, group, source_tiles(group, k % 3 - 1), lambda t: load(rows, t))
            totals[group] = got if k == 0 else totals[group] + got
    return totals


def back_inner_kernel(groups, terms, rule_ref, *refs):
    totals = back_sum(groups, rule_ref, lambda rows, t: terms[rows, tile_span(t)])
    for group in groups:
        refs[-1][:, tile_span(group)] = totals[group]


def edge_kernel(
    terms, rule_ref, weight_ref, near_ref, far_ref, inner, own_ref, first_ref, second_ref,
    out_ref, grad_ref, faces, products,
):
    chan = lax.axis_index("ch")
    out_ref[...] = (own_ref[...] + second_ref[:, :VOX]).astype(jnp.bfloat16)
    lower, upper = by_side(near_ref[32:, :], far_ref[32:, :])
    pairs = (
        (lower, upper),
        (first_ref[:32, VOX:], first_ref[32:, VOX:]),
        (second_ref[:, VOX : VOX + FACE], second_ref[:, VOX + FACE : VOX + 2 * FACE]),
        (second_ref[:, VOX + 2 * FACE : VOX + 3 * FACE], second_ref[:, VOX + 3 * FACE :]),
    )
    for m, (lower, upper) in zip(ORDER, pairs):
        rows = pl.ds(pl.multiple_of(32 * (chan ^ m), 32), 32)
        faces[rows, :FACE] = lower.astype(jnp.bfloat16)
        faces[rows, FACE:] = upper.astype(jnp.bfloat16)
    products[...] = jnp.dot(
        weight_ref[...], faces[...], preferred_element_type=jnp.float32
    )
    totals = back_sum(
        EDGE, rule_ref,
        lambda rows, t: products[rows, tile_span(t - 8)] if t >= 8 else terms[rows, tile_span(t)],
    )
    for group in range(8):
        values = totals[group] if group in EDGE else inner[:, tile_span(group)]
        grad_ref[:, tile_span(group)] = values.astype(jnp.bfloat16)


def split_sum_kernel(keep_ref, came_ref, *outs):
    for q, out in enumerate(outs):
        rows = slice(PART * q, PART * (q + 1))
        out[...] = keep_ref[rows, :] + came_ref[rows, :]


def sum_kernel(*refs):
    values = [ref[...] for ref in refs[:-1]]
    while len(values) > 1:
        values = [values[i] + values[i + 1] for i in range(0, len(values), 2)]
    refs[-1][...] = values[0]


def join_kernel(*refs):
    size = refs[0].shape[0]
    for q, ref in enumerate(refs[:-1]):
        refs[-1][size * q : size * (q + 1), :] = ref[...]


def place_kernel(even_ref, odd_ref, out_ref):
    spot = own_part()
    short = 864 - 7 * PART
    for q in range(4):
        for odd, ref in enumerate((even_ref, odd_ref)):
            part = spot ^ (2 * q + odd)
            start = pl.multiple_of(PART * part, 8)
            out_ref[pl.ds(start, short), :] = ref[PART * q : PART * q + short, :]

            @pl.when(part < 7)
            def _():
                rows = pl.ds(pl.multiple_of(start + short, 8), PART - short)
                out_ref[rows, :] = ref[PART * q + short : PART * (q + 1), :]


def call(kernel, outs, args, scratch=(), aliases=None, flops=0, name=None):
    moved = sum(a.size * a.dtype.itemsize for a in list(args) + jax.tree.leaves(outs))
    return pl.pallas_call(
        kernel,
        out_shape=outs,
        in_specs=[VMEM] * len(args),
        out_specs=jax.tree.map(lambda _: VMEM, outs),
        scratch_shapes=list(scratch),
        input_output_aliases=aliases or {},
        compiler_params=pltpu.CompilerParams(vmem_limit_bytes=40 << 20),
        cost_estimate=pl.CostEstimate(flops=flops, bytes_accessed=moved, transcendentals=0),
        name=name,
    )(*args)


def f32(*shape):
    return jax.ShapeDtypeStruct(shape, jnp.float32)


def bf16(*shape):
    return jax.ShapeDtypeStruct(shape, jnp.bfloat16)


def swap(value, mask):
    count = lax.axis_size("blk")
    return lax.ppermute(value, "blk", [(i, i ^ mask) for i in range(count)])


def swap_far(value):
    count = lax.axis_size("blk")
    pairs = [(i, (i + 1 if i % 2 else i - 1) % count) for i in range(count)]
    return lax.ppermute(value, "blk", pairs)


def after(values, *others):
    return lax.optimization_barrier((*values, *others))[: len(values)]


def per_device(features, weight, grad_out, rulebook):
    weights = weight.reshape(864, 128)

    def over_ch(value, mask):
        return lax.ppermute(value, "ch", [(i, i ^ mask) for i in range(4)])

    x, g, rules = features, grad_out, rulebook
    cut = pl.BlockSpec((32, 2 * FACE), lambda i: (0, 0))
    face = pl.BlockSpec((64, FACE), lambda i: (0, 0))
    near, far = pl.pallas_call(
        faces_kernel, out_shape=(bf16(64, FACE),) * 2, grid=(1,),
        in_specs=[cut, cut], out_specs=(face, face),
        compiler_params=pltpu.CompilerParams(vmem_limit_bytes=56 << 20),
        cost_estimate=pl.CostEstimate(flops=1 << 30, bytes_accessed=1 << 16, transcendentals=0),
        name="faces",
    )(x, g)
    pair = call(join_kernel, bf16(64, VOX), (g, over_ch(g, 1)), name="join")
    near = swap(near, 1)
    far = swap_far(far)
    other = over_ch(pair, 3)
    dense = call(
        gather_kernel, bf16(864, VOX), (x, rules),
        [pltpu.VMEM((32, VOX), jnp.float32)], flops=3 << 30, name="gather",
    )
    dense, grads, keep, send = call(
        weight_kernel,
        (bf16(864, VOX), bf16(128, VOX), f32(4 * PART, 128), f32(4 * PART, 128)),
        (dense, rules, near, far, pair, other),
        [pltpu.VMEM((32, 2 * FACE), jnp.float32), pltpu.VMEM((8 * PART, 128), jnp.float32)],
        aliases={0: 0}, flops=1 << 30, name="weight_terms",
    )

    def inner_part(groups, inner=None):
        args = (back, rules) if inner is None else (back, rules, inner)
        return call(
            functools.partial(back_inner_kernel, groups), f32(32, VOX), args,
            aliases=None if inner is None else {2: 0}, flops=max(2, len(groups)) << 30,
            name="back_inner",
        )

    came = swap(send, 1)
    ours, first = call(
        forward_kernel, (f32(64, VOX), f32(64, VOX + FACE)), (dense, weights, near, far),
        [pltpu.VMEM((128, VOX), jnp.float32)], flops=1 << 30, name="forward",
    )
    back = call(
        back_terms_kernel, f32(864, VOX), (weights, grads), flops=1 << 30, name="back_terms"
    )
    came, = after((came,), ours, back)
    pieces = call(split_sum_kernel, (f32(PART, 128),) * 4, (keep, came), name="sum_pair")
    others = [swap(pieces[q], m) for q, m in ((1, X1), (2, Z1), (3, X1 | Z1))]
    first, = after((first,), *pieces)
    first = over_ch(first, 1)
    inner = inner_part((2, 3))
    others = after(others, inner)
    total = call(sum_kernel, f32(PART, 128), (pieces[0], *others), name="sum_four")
    came = swap(total, X3)
    inner, = after((inner,), total)
    inner = inner_part((4, 5, 6), inner)
    came, = after((came,), inner)
    total = call(sum_kernel, f32(PART, 128), (total, came), name="sum_two")
    others = [swap(total, m) for m in (Z3, Z6, Z3 ^ Z6)]
    ours, first = after((ours, first), total)
    own, second = call(
        middle_kernel, (f32(32, VOX), f32(32, VOX + 4 * FACE)), (ours, first, near, far),
        name="middle",
    )
    second = over_ch(second, 3)
    inner = inner_part((7,), inner)
    others = after(others, inner, own)
    total = call(sum_kernel, f32(PART, 128), (total, *others), name="sum_four")
    others = [swap(total, m) for m in (X1, Z1, X1 | Z1)]
    output, grad_features = call(
        edge_kernel, (bf16(32, VOX), bf16(32, VOX)),
        (back, rules, weights, near, far, inner, own, first, second),
        [pltpu.VMEM((128, 2 * FACE), jnp.bfloat16), pltpu.VMEM((864, 2 * FACE), jnp.float32)],
        flops=2 << 30, name="edge",
    )
    others = after(others, output)
    even = call(join_kernel, f32(4 * PART, 128), (total, *others), name="join")
    odd = swap(even, 1)
    weight_grad = call(
        place_kernel, f32(864, 128), (even, odd), name="place",
    )
    return output, grad_features, weight_grad.reshape(27, 32, 128)


def solution(mesh):
    placed = (P("ch", "blk"), P(None, "ch", None), P("ch", "blk"), P(None, "blk"))
    return jax.shard_map(
        per_device,
        mesh=mesh,
        in_specs=placed,
        out_specs=(P("ch", "blk"), P("ch", "blk"), P(None, "ch", None)),
        check_vma=False,
    )
```

```python
import functools

import jax
import jax.numpy as jnp
from jax import lax
from jax.experimental import pallas as pl
from jax.experimental.pallas import tpu as pltpu
from jax.sharding import PartitionSpec as P

VOX = 1024
FACE = 128
LANES = 128
PART = 112
INNER = tuple(range(2, 8))
EDGE = (0, 1)
X1, X3, Z1, Z3, Z6 = 2, 6, 8, 24, 48
ORDER = (0, 1, 3, 2)
VMEM = pl.BlockSpec(memory_space=pltpu.VMEM)


def source_tiles(group, dz):
    if group == 0:
        return {-1: (8,), 0: (0,), 1: INNER}[dz]
    if group == 1:
        return {-1: INNER, 0: (1,), 1: (9,)}[dz]
    return {-1: (0,) + INNER, 0: INNER, 1: (1,) + INNER}[dz]


def picked(row, group, tiles, load):
    span = row[:, LANES * group : LANES * (group + 1)]
    index = jnp.broadcast_to(span, (32, LANES))
    lane = index & (LANES - 1)
    tile = index >> 7
    total = jnp.zeros((32, LANES), jnp.float32)
    for t in tiles:
        values = jnp.take_along_axis(load(t), lane, axis=1, mode="promise_in_bounds")
        total = jnp.where(tile == t, values, total)
    return total


def own_part():
    place = lax.axis_index("blk")
    over_x = (place >> 1) ^ (place >> 2)
    over_z = (place >> 3) ^ (place >> 4) ^ (place >> 5)
    return (place & 1) | ((over_x & 1) << 1) | ((over_z & 1) << 2)


def tile_span(t):
    return slice(LANES * t, LANES * (t + 1))


def faces_kernel(x_ref, g_ref, near_ref, far_ref):
    odd = (lax.axis_index("blk") & 1) == 1
    for rows, ref in ((slice(0, 32), x_ref), (slice(32, 64), g_ref)):
        lowest = ref[:, :FACE].astype(jnp.float32)
        highest = ref[:, FACE : 2 * FACE].astype(jnp.float32)
        near_ref[rows, :] = jnp.where(odd, lowest, highest).astype(jnp.bfloat16)
        far_ref[rows, :] = jnp.where(odd, highest, lowest).astype(jnp.bfloat16)


def by_side(near, far):
    odd = (lax.axis_index("blk") & 1) == 1
    near = near.astype(jnp.float32)
    far = far.astype(jnp.float32)
    return jnp.where(odd, near, far), jnp.where(odd, far, near)


def gather_kernel(x_ref, rule_ref, dense_ref, table):
    table[...] = x_ref[...].astype(jnp.float32)
    for k in range(27):
        row = rule_ref[k : k + 1, :]
        for group in range(8):
            tiles = source_tiles(group, k % 3 - 1)
            if tiles[0] >= 8:
                continue
            got = picked(row, group, tiles, lambda t: table[:, tile_span(t)])
            dense_ref[32 * k : 32 * k + 32, tile_span(group)] = got.astype(jnp.bfloat16)


def faces_kernel(x_ref, g_ref, near_ref, far_ref):
    odd = (lax.axis_index("blk") & 1) == 1
    for rows, ref in ((slice(0, 32), x_ref), (slice(32, 64), g_ref)):
        lowest = ref[:, :FACE].astype(jnp.float32)
        highest = ref[:, FACE : 2 * FACE].astype(jnp.float32)
        near_ref[rows, :] = jnp.where(odd, lowest, highest).astype(jnp.bfloat16)
        far_ref[rows, :] = jnp.where(odd, highest, lowest).astype(jnp.bfloat16)


def by_side(near, far):
    odd = (lax.axis_index("blk") & 1) == 1
    near = near.astype(jnp.float32)
    far = far.astype(jnp.float32)
    return jnp.where(odd, near, far), jnp.where(odd, far, near)


def gather_kernel(x_ref, rule_ref, dense_ref, table):
    table[...] = x_ref[...].astype(jnp.float32)

    def step(j, carry):
        for d in range(3):
            k = 3 * j + d
            row = rule_ref[pl.ds(k, 1), :]
            for group in range(8):
                tiles = source_tiles(group, d - 1)
                if tiles[0] >= 8:
                    continue
                got = picked(row, group, tiles, lambda t: table[:, tile_span(t)])
                rows = pl.ds(pl.multiple_of(32 * k, 32), 32)
                dense_ref[rows, tile_span(group)] = got.astype(jnp.bfloat16)
        return carry

    lax.fori_loop(0, 9, step, 0)


def weight_kernel(
    dense_in, rule_ref, near_ref, far_ref, pair_ref, other_ref,
    dense_ref, grad_ref, keep_ref, send_ref, faces, terms,
):
    chan = lax.axis_index("ch")
    spot = own_part()
    for i, m in enumerate(ORDER):
        part = (pair_ref if i < 2 else other_ref)[32 * (i % 2) : 32 * (i % 2) + 32, :]
        grad_ref[pl.ds(pl.multiple_of(32 * (chan ^ m), 32), 32), :] = part
    faces[:, :FACE], faces[:, FACE:] = by_side(near_ref[:32, :], far_ref[:32, :])

    for j in range(9):
        for group, d in ((0, 0), (1, 2)):
            k = 3 * j + d
            row = rule_ref[k : k + 1, :]
            got = picked(row, group, (8 + group,), lambda t: faces[:, tile_span(t - 8)])
            dense_ref[32 * k : 32 * k + 32, tile_span(group)] = got.astype(jnp.bfloat16)
    terms[:864, :] = lax.dot_general(
        dense_ref[...], grad_ref[...], (((1,), (1,)), ((), ())),
        preferred_element_type=jnp.float32,
    ) * (1.0 / 256.0)
    terms[864:, :] = jnp.zeros((32, LANES), jnp.float32)
    for q in range(4):
        for odd, target in ((0, keep_ref), (1, send_ref)):
            start = pl.multiple_of(PART * (spot ^ (2 * q + odd)), 8)
            target[PART * q : PART * (q + 1), :] = terms[pl.ds(start, PART), :]


def forward_kernel(dense_ref, weight_ref, near_ref, far_ref, keep_ref, send_ref, sums):
    chan = lax.axis_index("ch")
    sums[...] = lax.dot_general(
        weight_ref[...], dense_ref[...], (((0,), (0,)), ((), ())),
        preferred_element_type=jnp.float32,
    )
    for target, parts in ((keep_ref, (0, 3)), (send_ref, (1, 2))):
        for i, m in enumerate(parts):
            rows = pl.ds(pl.multiple_of(32 * (chan ^ m), 32), 32)
            target[32 * i : 32 * i + 32, :VOX] = sums[rows, :]
    lower, upper = by_side(near_ref[32:, :], far_ref[32:, :])
    send_ref[:32, VOX:] = lower
    send_ref[32:, VOX:] = upper


def middle_kernel(keep_ref, came_ref, near_ref, far_ref, own_ref, send_ref):
    own_ref[...] = keep_ref[:32, :] + came_ref[:32, :VOX]
    send_ref[:, :VOX] = keep_ref[32:, :] + came_ref[32:, :VOX]
    lower, upper = by_side(near_ref[32:, :], far_ref[32:, :])
    send_ref[:, VOX : VOX + FACE] = lower
    send_ref[:, VOX + FACE : VOX + 2 * FACE] = upper
    send_ref[:, VOX + 2 * FACE : VOX + 3 * FACE] = came_ref[:32, VOX:]
    send_ref[:, VOX + 3 * FACE :] = came_ref[32:, VOX:]


def back_terms_kernel(weight_ref, grad_ref, terms_ref):
    terms_ref[...] = jnp.dot(
        weight_ref[...], grad_ref[...], preferred_element_type=jnp.float32
    )


def back_sum(groups, rule_ref, load):
    totals = {}
    for k in range(27):
        row = rule_ref[k : k + 1, :]
        rows = slice(32 * (26 - k), 32 * (26 - k) + 32)
        for group in groups:
            got = picked(row, group, source_tiles(group, k % 3 - 1), lambda t: load(rows, t))
            totals[group] = got if k == 0 else totals[group] + got
    return totals


def back_inner_kernel(groups, terms, rule_ref, *refs):
    totals = back_sum(groups, rule_ref, lambda rows, t: terms[rows, tile_span(t)])
    for group in groups:
        refs[-1][:, tile_span(group)] = totals[group]


def edge_kernel(
    terms, rule_ref, weight_ref, near_ref, far_ref, inner, own_ref, first_ref, second_ref,
    out_ref, grad_ref, faces, products,
):
    chan = lax.axis_index("ch")
    out_ref[...] = (own_ref[...] + second_ref[:, :VOX]).astype(jnp.bfloat16)
    lower, upper = by_side(near_ref[32:, :], far_ref[32:, :])
    pairs = (
        (lower, upper),
        (first_ref[:32, VOX:], first_ref[32:, VOX:]),
        (second_ref[:, VOX : VOX + FACE], second_ref[:, VOX + FACE : VOX + 2 * FACE]),
        (second_ref[:, VOX + 2 * FACE : VOX + 3 * FACE], second_ref[:, VOX + 3 * FACE :]),
    )
    for m, (lower, upper) in zip(ORDER, pairs):
        rows = pl.ds(pl.multiple_of(32 * (chan ^ m), 32), 32)
        faces[rows, :FACE] = lower.astype(jnp.bfloat16)
        faces[rows, FACE:] = upper.astype(jnp.bfloat16)
    products[...] = jnp.dot(
        weight_ref[...], faces[...], preferred_element_type=jnp.float32
    )
    totals = back_sum(
        EDGE, rule_ref,
        lambda rows, t: products[rows, tile_span(t - 8)] if t >= 8 else terms[rows, tile_span(t)],
    )
    for group in range(8):
        values = totals[group] if group in EDGE else inner[:, tile_span(group)]
        grad_ref[:, tile_span(group)] = values.astype(jnp.bfloat16)


def split_sum_kernel(keep_ref, came_ref, *outs):
    for q, out in enumerate(outs):
        rows = slice(PART * q, PART * (q + 1))
        out[...] = keep_ref[rows, :] + came_ref[rows, :]


def sum_kernel(*refs):
    values = [ref[...] for ref in refs[:-1]]
    while len(values) > 1:
        values = [values[i] + values[i + 1] for i in range(0, len(values), 2)]
    refs[-1][...] = values[0]


def join_kernel(*refs):
    size = refs[0].shape[0]
    for q, ref in enumerate(refs[:-1]):
        refs[-1][size * q : size * (q + 1), :] = ref[...]


def place_kernel(even_ref, odd_ref, out_ref):
    spot = own_part()
    short = 864 - 7 * PART
    for q in range(4):
        for odd, ref in enumerate((even_ref, odd_ref)):
            part = spot ^ (2 * q + odd)
            start = pl.multiple_of(PART * part, 8)
            out_ref[pl.ds(start, short), :] = ref[PART * q : PART * q + short, :]

            @pl.when(part < 7)
            def _():
                rows = pl.ds(pl.multiple_of(start + short, 8), PART - short)
                out_ref[rows, :] = ref[PART * q + short : PART * (q + 1), :]


def call(kernel, outs, args, scratch=(), aliases=None, flops=0, name=None):
    moved = sum(a.size * a.dtype.itemsize for a in list(args) + jax.tree.leaves(outs))
    return pl.pallas_call(
        kernel,
        out_shape=outs,
        in_specs=[VMEM] * len(args),
        out_specs=jax.tree.map(lambda _: VMEM, outs),
        scratch_shapes=list(scratch),
        input_output_aliases=aliases or {},
        compiler_params=pltpu.CompilerParams(vmem_limit_bytes=40 << 20),
        cost_estimate=pl.CostEstimate(flops=flops, bytes_accessed=moved, transcendentals=0),
        name=name,
    )(*args)


def f32(*shape):
    return jax.ShapeDtypeStruct(shape, jnp.float32)


def bf16(*shape):
    return jax.ShapeDtypeStruct(shape, jnp.bfloat16)


def swap(value, mask):
    count = lax.axis_size("blk")
    return lax.ppermute(value, "blk", [(i, i ^ mask) for i in range(count)])


def swap_far(value):
    count = lax.axis_size("blk")
    pairs = [(i, (i + 1 if i % 2 else i - 1) % count) for i in range(count)]
    return lax.ppermute(value, "blk", pairs)


def after(values, *others):
    return lax.optimization_barrier((*values, *others))[: len(values)]


def per_device(features, weight, grad_out, rulebook):
    weights = weight.reshape(864, 128)

    def over_ch(value, mask):
        return lax.ppermute(value, "ch", [(i, i ^ mask) for i in range(4)])

    x, g, rules = features, grad_out, rulebook
    cut = pl.BlockSpec((32, 2 * FACE), lambda i: (0, 0))
    face = pl.BlockSpec((64, FACE), lambda i: (0, 0))
    near, far = pl.pallas_call(
        faces_kernel, out_shape=(bf16(64, FACE),) * 2, grid=(1,),
        in_specs=[cut, cut], out_specs=(face, face),
        compiler_params=pltpu.CompilerParams(vmem_limit_bytes=56 << 20),
        cost_estimate=pl.CostEstimate(flops=1 << 30, bytes_accessed=1 << 16, transcendentals=0),
        name="faces",
    )(x, g)
    pair = call(join_kernel, bf16(64, VOX), (g, over_ch(g, 1)), name="join")
    near = swap(near, 1)
    far = swap_far(far)
    other = over_ch(pair, 3)
    dense = call(
        gather_kernel, bf16(864, VOX), (x, rules),
        [pltpu.VMEM((32, VOX), jnp.float32)], flops=3 << 30, name="gather",
    )
    dense, grads, keep, send = call(
        weight_kernel,
        (bf16(864, VOX), bf16(128, VOX), f32(4 * PART, 128), f32(4 * PART, 128)),
        (dense, rules, near, far, pair, other),
        [pltpu.VMEM((32, 2 * FACE), jnp.float32), pltpu.VMEM((8 * PART, 128), jnp.float32)],
        aliases={0: 0}, flops=1 << 30, name="weight_terms",
    )

    def inner_part(groups, inner=None):
        args = (back, rules) if inner is None else (back, rules, inner)
        return call(
            functools.partial(back_inner_kernel, groups), f32(32, VOX), args,
            aliases=None if inner is None else {2: 0}, flops=max(2, len(groups)) << 30,
            name="back_inner",
        )

    came = swap(send, 1)
    ours, first = call(
        forward_kernel, (f32(64, VOX), f32(64, VOX + FACE)), (dense, weights, near, far),
        [pltpu.VMEM((128, VOX), jnp.float32)], flops=1 << 30, name="forward",
    )
    back = call(
        back_terms_kernel, f32(864, VOX), (weights, grads), flops=1 << 30, name="back_terms"
    )
    came, = after((came,), ours, back)
    pieces = call(split_sum_kernel, (f32(PART, 128),) * 4, (keep, came), name="sum_pair")
    others = [swap(pieces[q], m) for q, m in ((3, X1 | Z1), (2, Z1), (1, X1))]
    first, = after((first,), *pieces)
    first = over_ch(first, 1)
    inner = inner_part((2, 3))
    others = after(others, inner)
    total = call(sum_kernel, f32(PART, 128), (pieces[0], *others), name="sum_four")
    came = swap(total, X3)
    inner, = after((inner,), total)
    inner = inner_part((4, 5, 6), inner)
    came, = after((came,), inner)
    total = call(sum_kernel, f32(PART, 128), (total, came), name="sum_two")
    others = [swap(total, m) for m in (Z3, Z6, Z3 ^ Z6)]
    ours, first = after((ours, first), total)
    own, second = call(
        middle_kernel, (f32(32, VOX), f32(32, VOX + 4 * FACE)), (ours, first, near, far),
        name="middle",
    )
    second = over_ch(second, 3)
    inner = inner_part((7,), inner)
    others = after(others, inner, own)
    total = call(sum_kernel, f32(PART, 128), (total, *others), name="sum_four")
    others = [swap(total, m) for m in (X1, Z1, X1 | Z1)]
    output, grad_features = call(
        edge_kernel, (bf16(32, VOX), bf16(32, VOX)),
        (back, rules, weights, near, far, inner, own, first, second),
        [pltpu.VMEM((128, 2 * FACE), jnp.bfloat16), pltpu.VMEM((864, 2 * FACE), jnp.float32)],
        flops=2 << 30, name="edge",
    )
    others = after(others, output)
    even = call(join_kernel, f32(4 * PART, 128), (total, *others), name="join")
    odd = swap(even, 1)
    weight_grad = call(
        place_kernel, f32(864, 128), (even, odd), name="place",
    )
    return output, grad_features, weight_grad.reshape(27, 32, 128)


def solution(mesh):
    placed = (P("ch", "blk"), P(None, "ch", None), P("ch", "blk"), P(None, "blk"))
    return jax.shard_map(
        per_device,
        mesh=mesh,
        in_specs=placed,
        out_specs=(P("ch", "blk"), P("ch", "blk"), P(None, "ch", None)),
        check_vma=False,
    )
```

```python
import functools

import jax
import jax.numpy as jnp
from jax import lax
from jax.experimental import pallas as pl
from jax.experimental.pallas import tpu as pltpu
from jax.sharding import PartitionSpec as P

VOX = 1024
FACE = 128
LANES = 128
PART = 112
INNER = tuple(range(2, 8))
EDGE = (0, 1, 3)
X1, X3, Z1, Z3, Z6 = 2, 6, 8, 24, 48
ORDER = (0, 1, 3, 2)
VMEM = pl.BlockSpec(memory_space=pltpu.VMEM)


def source_tiles(group, dz):
    if group == 0:
        return {-1: (8,), 0: (0,), 1: INNER}[dz]
    if group == 1:
        return {-1: INNER, 0: (1,), 1: (9,)}[dz]
    return {-1: (0,) + INNER, 0: INNER, 1: (1,) + INNER}[dz]


def picked(row, group, tiles, load):
    span = row[:, LANES * group : LANES * (group + 1)]
    index = jnp.broadcast_to(span, (32, LANES))
    lane = index & (LANES - 1)
    tile = index >> 7
    total = jnp.zeros((32, LANES), jnp.float32)
    for t in tiles:
        values = jnp.take_along_axis(load(t), lane, axis=1, mode="promise_in_bounds")
        total = jnp.where(tile == t, values, total)
    return total


def own_part():
    place = lax.axis_index("blk")
    over_x = (place >> 1) ^ (place >> 2)
    over_z = (place >> 3) ^ (place >> 4) ^ (place >> 5)
    return (place & 1) | ((over_x & 1) << 1) | ((over_z & 1) << 2)


def tile_span(t):
    return slice(LANES * t, LANES * (t + 1))


def faces_kernel(x_ref, g_ref, near_ref, far_ref):
    odd = (lax.axis_index("blk") & 1) == 1
    for rows, ref in ((slice(0, 32), x_ref), (slice(32, 64), g_ref)):
        lowest = ref[:, :FACE].astype(jnp.float32)
        highest = ref[:, FACE : 2 * FACE].astype(jnp.float32)
        near_ref[rows, :] = jnp.where(odd, lowest, highest).astype(jnp.bfloat16)
        far_ref[rows, :] = jnp.where(odd, highest, lowest).astype(jnp.bfloat16)


def by_side(near, far):
    odd = (lax.axis_index("blk") & 1) == 1
    near = near.astype(jnp.float32)
    far = far.astype(jnp.float32)
    return jnp.where(odd, near, far), jnp.where(odd, far, near)


def gather_kernel(x_ref, rule_ref, dense_ref, table):
    table[...] = x_ref[...].astype(jnp.float32)
    for k in range(27):
        row = rule_ref[k : k + 1, :]
        for group in range(8):
            tiles = source_tiles(group, k % 3 - 1)
            if tiles[0] >= 8:
                continue
            got = picked(row, group, tiles, lambda t: table[:, tile_span(t)])
            dense_ref[32 * k : 32 * k + 32, tile_span(group)] = got.astype(jnp.bfloat16)


def faces_kernel(x_ref, g_ref, near_ref, far_ref):
    odd = (lax.axis_index("blk") & 1) == 1
    for rows, ref in ((slice(0, 32), x_ref), (slice(32, 64), g_ref)):
        lowest = ref[:, :FACE].astype(jnp.float32)
        highest = ref[:, FACE : 2 * FACE].astype(jnp.float32)
        near_ref[rows, :] = jnp.where(odd, lowest, highest).astype(jnp.bfloat16)
        far_ref[rows, :] = jnp.where(odd, highest, lowest).astype(jnp.bfloat16)


def by_side(near, far):
    odd = (lax.axis_index("blk") & 1) == 1
    near = near.astype(jnp.float32)
    far = far.astype(jnp.float32)
    return jnp.where(odd, near, far), jnp.where(odd, far, near)


def gather_kernel(x_ref, rule_ref, dense_ref, table):
    table[...] = x_ref[...].astype(jnp.float32)

    def step(j, carry):
        for d in range(3):
            k = 3 * j + d
            row = rule_ref[pl.ds(k, 1), :]
            for group in range(8):
                tiles = source_tiles(group, d - 1)
                if tiles[0] >= 8:
                    continue
                got = picked(row, group, tiles, lambda t: table[:, tile_span(t)])
                rows = pl.ds(pl.multiple_of(32 * k, 32), 32)
                dense_ref[rows, tile_span(group)] = got.astype(jnp.bfloat16)
        return carry

    lax.fori_loop(0, 9, step, 0)


def weight_kernel(
    dense_in, rule_ref, near_ref, far_ref, pair_ref, other_ref,
    dense_ref, grad_ref, keep_ref, send_ref, faces, terms,
):
    chan = lax.axis_index("ch")
    spot = own_part()
    for i, m in enumerate(ORDER):
        part = (pair_ref if i < 2 else other_ref)[32 * (i % 2) : 32 * (i % 2) + 32, :]
        grad_ref[pl.ds(pl.multiple_of(32 * (chan ^ m), 32), 32), :] = part
    faces[:, :FACE], faces[:, FACE:] = by_side(near_ref[:32, :], far_ref[:32, :])

    for j in range(9):
        for group, d in ((0, 0), (1, 2)):
            k = 3 * j + d
            row = rule_ref[k : k + 1, :]
            got = picked(row, group, (8 + group,), lambda t: faces[:, tile_span(t - 8)])
            dense_ref[32 * k : 32 * k + 32, tile_span(group)] = got.astype(jnp.bfloat16)
    terms[:864, :] = lax.dot_general(
        dense_ref[...], grad_ref[...], (((1,), (1,)), ((), ())),
        preferred_element_type=jnp.float32,
    ) * (1.0 / 256.0)
    terms[864:, :] = jnp.zeros((32, LANES), jnp.float32)
    for q in range(4):
        for odd, target in ((0, keep_ref), (1, send_ref)):
            start = pl.multiple_of(PART * (spot ^ (2 * q + odd)), 8)
            target[PART * q : PART * (q + 1), :] = terms[pl.ds(start, PART), :]


def forward_kernel(dense_ref, weight_ref, near_ref, far_ref, keep_ref, send_ref, sums):
    chan = lax.axis_index("ch")
    sums[...] = lax.dot_general(
        weight_ref[...], dense_ref[...], (((0,), (0,)), ((), ())),
        preferred_element_type=jnp.float32,
    )
    for target, parts in ((keep_ref, (0, 3)), (send_ref, (1, 2))):
        for i, m in enumerate(parts):
            rows = pl.ds(pl.multiple_of(32 * (chan ^ m), 32), 32)
            target[32 * i : 32 * i + 32, :VOX] = sums[rows, :]
    lower, upper = by_side(near_ref[32:, :], far_ref[32:, :])
    send_ref[:32, VOX:] = lower
    send_ref[32:, VOX:] = upper


def middle_kernel(keep_ref, came_ref, near_ref, far_ref, own_ref, send_ref):
    own_ref[...] = keep_ref[:32, :] + came_ref[:32, :VOX]
    send_ref[:, :VOX] = keep_ref[32:, :] + came_ref[32:, :VOX]
    lower, upper = by_side(near_ref[32:, :], far_ref[32:, :])
    send_ref[:, VOX : VOX + FACE] = lower
    send_ref[:, VOX + FACE : VOX + 2 * FACE] = upper
    send_ref[:, VOX + 2 * FACE : VOX + 3 * FACE] = came_ref[:32, VOX:]
    send_ref[:, VOX + 3 * FACE :] = came_ref[32:, VOX:]


def back_terms_kernel(weight_ref, grad_ref, terms_ref):
    terms_ref[...] = jnp.dot(
        weight_ref[...], grad_ref[...], preferred_element_type=jnp.float32
    )


def back_sum(groups, rule_ref, load):
    totals = {}
    for k in range(27):
        row = rule_ref[k : k + 1, :]
        rows = slice(32 * (26 - k), 32 * (26 - k) + 32)
        for group in groups:
            got = picked(row, group, source_tiles(group, k % 3 - 1), lambda t: load(rows, t))
            totals[group] = got if k == 0 else totals[group] + got
    return totals


def back_inner_kernel(groups, terms, rule_ref, *refs):
    totals = back_sum(groups, rule_ref, lambda rows, t: terms[rows, tile_span(t)])
    for group in groups:
        refs[-1][:, tile_span(group)] = totals[group]


def edge_kernel(
    terms, rule_ref, weight_ref, near_ref, far_ref, inner, own_ref, first_ref, second_ref,
    out_ref, grad_ref, faces, products,
):
    chan = lax.axis_index("ch")
    out_ref[...] = (own_ref[...] + second_ref[:, :VOX]).astype(jnp.bfloat16)
    lower, upper = by_side(near_ref[32:, :], far_ref[32:, :])
    pairs = (
        (lower, upper),
        (first_ref[:32, VOX:], first_ref[32:, VOX:]),
        (second_ref[:, VOX : VOX + FACE], second_ref[:, VOX + FACE : VOX + 2 * FACE]),
        (second_ref[:, VOX + 2 * FACE : VOX + 3 * FACE], second_ref[:, VOX + 3 * FACE :]),
    )
    for m, (lower, upper) in zip(ORDER, pairs):
        rows = pl.ds(pl.multiple_of(32 * (chan ^ m), 32), 32)
        faces[rows, :FACE] = lower.astype(jnp.bfloat16)
        faces[rows, FACE:] = upper.astype(jnp.bfloat16)
    products[...] = jnp.dot(
        weight_ref[...], faces[...], preferred_element_type=jnp.float32
    )
    totals = back_sum(
        EDGE, rule_ref,
        lambda rows, t: products[rows, tile_span(t - 8)] if t >= 8 else terms[rows, tile_span(t)],
    )
    for group in range(8):
        values = totals[group] if group in EDGE else inner[:, tile_span(group)]
        grad_ref[:, tile_span(group)] = values.astype(jnp.bfloat16)


def split_sum_kernel(keep_ref, came_ref, *outs):
    for q, out in enumerate(outs):
        rows = slice(PART * q, PART * (q + 1))
        out[...] = keep_ref[rows, :] + came_ref[rows, :]


def sum_kernel(*refs):
    values = [ref[...] for ref in refs[:-1]]
    while len(values) > 1:
        values = [values[i] + values[i + 1] for i in range(0, len(values), 2)]
    refs[-1][...] = values[0]


def join_kernel(*refs):
    size = refs[0].shape[0]
    for q, ref in enumerate(refs[:-1]):
        refs[-1][size * q : size * (q + 1), :] = ref[...]


def place_kernel(even_ref, odd_ref, out_ref):
    spot = own_part()
    short = 864 - 7 * PART
    for q in range(4):
        for odd, ref in enumerate((even_ref, odd_ref)):
            part = spot ^ (2 * q + odd)
            start = pl.multiple_of(PART * part, 8)
            out_ref[pl.ds(start, short), :] = ref[PART * q : PART * q + short, :]

            @pl.when(part < 7)
            def _():
                rows = pl.ds(pl.multiple_of(start + short, 8), PART - short)
                out_ref[rows, :] = ref[PART * q + short : PART * (q + 1), :]


def call(kernel, outs, args, scratch=(), aliases=None, flops=0, name=None):
    moved = sum(a.size * a.dtype.itemsize for a in list(args) + jax.tree.leaves(outs))
    return pl.pallas_call(
        kernel,
        out_shape=outs,
        in_specs=[VMEM] * len(args),
        out_specs=jax.tree.map(lambda _: VMEM, outs),
        scratch_shapes=list(scratch),
        input_output_aliases=aliases or {},
        compiler_params=pltpu.CompilerParams(vmem_limit_bytes=40 << 20),
        cost_estimate=pl.CostEstimate(flops=flops, bytes_accessed=moved, transcendentals=0),
        name=name,
    )(*args)


def f32(*shape):
    return jax.ShapeDtypeStruct(shape, jnp.float32)


def bf16(*shape):
    return jax.ShapeDtypeStruct(shape, jnp.bfloat16)


def swap(value, mask):
    count = lax.axis_size("blk")
    return lax.ppermute(value, "blk", [(i, i ^ mask) for i in range(count)])


def swap_far(value):
    count = lax.axis_size("blk")
    pairs = [(i, (i + 1 if i % 2 else i - 1) % count) for i in range(count)]
    return lax.ppermute(value, "blk", pairs)


def after(values, *others):
    return lax.optimization_barrier((*values, *others))[: len(values)]


def per_device(features, weight, grad_out, rulebook):
    weights = weight.reshape(864, 128)

    def over_ch(value, mask):
        return lax.ppermute(value, "ch", [(i, i ^ mask) for i in range(4)])

    x, g, rules = features, grad_out, rulebook
    cut = pl.BlockSpec((32, 2 * FACE), lambda i: (0, 0))
    face = pl.BlockSpec((64, FACE), lambda i: (0, 0))
    near, far = pl.pallas_call(
        faces_kernel, out_shape=(bf16(64, FACE),) * 2, grid=(1,),
        in_specs=[cut, cut], out_specs=(face, face),
        compiler_params=pltpu.CompilerParams(vmem_limit_bytes=56 << 20),
        cost_estimate=pl.CostEstimate(flops=1 << 30, bytes_accessed=1 << 16, transcendentals=0),
        name="faces",
    )(x, g)
    pair = call(join_kernel, bf16(64, VOX), (g, over_ch(g, 1)), name="join")
    near = swap(near, 1)
    far = swap_far(far)
    other = over_ch(pair, 3)
    dense = call(
        gather_kernel, bf16(864, VOX), (x, rules),
        [pltpu.VMEM((32, VOX), jnp.float32)], flops=3 << 30, name="gather",
    )
    dense, grads, keep, send = call(
        weight_kernel,
        (bf16(864, VOX), bf16(128, VOX), f32(4 * PART, 128), f32(4 * PART, 128)),
        (dense, rules, near, far, pair, other),
        [pltpu.VMEM((32, 2 * FACE), jnp.float32), pltpu.VMEM((8 * PART, 128), jnp.float32)],
        aliases={0: 0}, flops=1 << 30, name="weight_terms",
    )

    def inner_part(groups, inner=None):
        args = (back, rules) if inner is None else (back, rules, inner)
        return call(
            functools.partial(back_inner_kernel, groups), f32(32, VOX), args,
            aliases=None if inner is None else {2: 0}, flops=max(2, len(groups)) << 30,
            name="back_inner",
        )

    came = swap(send, 1)
    ours, first = call(
        forward_kernel, (f32(64, VOX), f32(64, VOX + FACE)), (dense, weights, near, far),
        [pltpu.VMEM((128, VOX), jnp.float32)], flops=1 << 30, name="forward",
    )
    back = call(
        back_terms_kernel, f32(864, VOX), (weights, grads), flops=1 << 30, name="back_terms"
    )
    came, = after((came,), ours, back)
    pieces = call(split_sum_kernel, (f32(PART, 128),) * 4, (keep, came), name="sum_pair")
    others = [swap(pieces[q], m) for q, m in ((3, X1 | Z1), (2, Z1), (1, X1))]
    first, = after((first,), *pieces)
    first = over_ch(first, 1)
    inner = inner_part((2,))
    others = after(others, inner)
    total = call(sum_kernel, f32(PART, 128), (pieces[0], *others), name="sum_four")
    came = swap(total, X3)
    inner, = after((inner,), total)
    inner = inner_part((4, 5, 6), inner)
    came, = after((came,), inner)
    total = call(sum_kernel, f32(PART, 128), (total, came), name="sum_two")
    others = [swap(total, m) for m in (Z3, Z6, Z3 ^ Z6)]
    ours, first = after((ours, first), total)
    own, second = call(
        middle_kernel, (f32(32, VOX), f32(32, VOX + 4 * FACE)), (ours, first, near, far),
        name="middle",
    )
    second = over_ch(second, 3)
    inner = inner_part((7,), inner)
    others = after(others, inner, own)
    total = call(sum_kernel, f32(PART, 128), (total, *others), name="sum_four")
    others = [swap(total, m) for m in (X1, Z1, X1 | Z1)]
    output, grad_features = call(
        edge_kernel, (bf16(32, VOX), bf16(32, VOX)),
        (back, rules, weights, near, far, inner, own, first, second),
        [pltpu.VMEM((128, 2 * FACE), jnp.bfloat16), pltpu.VMEM((864, 2 * FACE), jnp.float32)],
        flops=2 << 30, name="edge",
    )
    others = after(others, output)
    even = call(join_kernel, f32(4 * PART, 128), (total, *others), name="join")
    odd = swap(even, 1)
    weight_grad = call(
        place_kernel, f32(864, 128), (even, odd), name="place",
    )
    return output, grad_features, weight_grad.reshape(27, 32, 128)


def solution(mesh):
    placed = (P("ch", "blk"), P(None, "ch", None), P("ch", "blk"), P(None, "blk"))
    return jax.shard_map(
        per_device,
        mesh=mesh,
        in_specs=placed,
        out_specs=(P("ch", "blk"), P("ch", "blk"), P(None, "ch", None)),
        check_vma=False,
    )
```

```python
import functools

import jax
import jax.numpy as jnp
from jax import lax
from jax.experimental import pallas as pl
from jax.experimental.pallas import tpu as pltpu
from jax.sharding import PartitionSpec as P

VOX = 1024
FACE = 128
LANES = 128
PART = 112
INNER = tuple(range(2, 8))
EDGE = (0, 1, 3)
X1, X3, Z1, Z3, Z6 = 2, 6, 8, 24, 48
ORDER = (0, 1, 3, 2)
VMEM = pl.BlockSpec(memory_space=pltpu.VMEM)


def source_tiles(group, dz):
    if group == 0:
        return {-1: (8,), 0: (0,), 1: INNER}[dz]
    if group == 1:
        return {-1: INNER, 0: (1,), 1: (9,)}[dz]
    return {-1: (0,) + INNER, 0: INNER, 1: (1,) + INNER}[dz]


def picked(row, group, tiles, load):
    span = row[:, LANES * group : LANES * (group + 1)]
    index = jnp.broadcast_to(span, (32, LANES))
    lane = index & (LANES - 1)
    tile = index >> 7
    total = jnp.zeros((32, LANES), jnp.float32)
    for t in tiles:
        values = jnp.take_along_axis(load(t), lane, axis=1, mode="promise_in_bounds")
        total = jnp.where(tile == t, values, total)
    return total


def own_part():
    place = lax.axis_index("blk")
    over_x = (place >> 1) ^ (place >> 2)
    over_z = (place >> 3) ^ (place >> 4) ^ (place >> 5)
    return (place & 1) | ((over_x & 1) << 1) | ((over_z & 1) << 2)


def tile_span(t):
    return slice(LANES * t, LANES * (t + 1))


def faces_kernel(x_ref, g_ref, near_ref, far_ref):
    odd = (lax.axis_index("blk") & 1) == 1
    for rows, ref in ((slice(0, 32), x_ref), (slice(32, 64), g_ref)):
        lowest = ref[:, :FACE].astype(jnp.float32)
        highest = ref[:, FACE : 2 * FACE].astype(jnp.float32)
        near_ref[rows, :] = jnp.where(odd, lowest, highest).astype(jnp.bfloat16)
        far_ref[rows, :] = jnp.where(odd, highest, lowest).astype(jnp.bfloat16)


def by_side(near, far):
    odd = (lax.axis_index("blk") & 1) == 1
    near = near.astype(jnp.float32)
    far = far.astype(jnp.float32)
    return jnp.where(odd, near, far), jnp.where(odd, far, near)


def gather_kernel(x_ref, rule_ref, dense_ref, table):
    table[...] = x_ref[...].astype(jnp.float32)
    for k in range(27):
        row = rule_ref[k : k + 1, :]
        for group in range(8):
            tiles = source_tiles(group, k % 3 - 1)
            if tiles[0] >= 8:
                continue
            got = picked(row, group, tiles, lambda t: table[:, tile_span(t)])
            dense_ref[32 * k : 32 * k + 32, tile_span(group)] = got.astype(jnp.bfloat16)


def faces_kernel(x_ref, g_ref, near_ref, far_ref):
    odd = (lax.axis_index("blk") & 1) == 1
    for rows, ref in ((slice(0, 32), x_ref), (slice(32, 64), g_ref)):
        lowest = ref[:, :FACE].astype(jnp.float32)
        highest = ref[:, FACE : 2 * FACE].astype(jnp.float32)
        near_ref[rows, :] = jnp.where(odd, lowest, highest).astype(jnp.bfloat16)
        far_ref[rows, :] = jnp.where(odd, highest, lowest).astype(jnp.bfloat16)


def by_side(near, far):
    odd = (lax.axis_index("blk") & 1) == 1
    near = near.astype(jnp.float32)
    far = far.astype(jnp.float32)
    return jnp.where(odd, near, far), jnp.where(odd, far, near)


def gather_kernel(x_ref, rule_ref, dense_ref, table):
    table[...] = x_ref[...].astype(jnp.float32)

    def step(j, carry):
        for d in range(3):
            k = 3 * j + d
            row = rule_ref[pl.ds(k, 1), :]
            for group in range(8):
                tiles = source_tiles(group, d - 1)
                if tiles[0] >= 8:
                    continue
                got = picked(row, group, tiles, lambda t: table[:, tile_span(t)])
                rows = pl.ds(pl.multiple_of(32 * k, 32), 32)
                dense_ref[rows, tile_span(group)] = got.astype(jnp.bfloat16)
        return carry

    lax.fori_loop(0, 9, step, 0)


def weight_kernel(
    dense_in, rule_ref, near_ref, far_ref, pair_ref, other_ref,
    dense_ref, grad_ref, keep_ref, send_ref, faces, terms,
):
    chan = lax.axis_index("ch")
    spot = own_part()
    for i, m in enumerate(ORDER):
        part = (pair_ref if i < 2 else other_ref)[32 * (i % 2) : 32 * (i % 2) + 32, :]
        grad_ref[pl.ds(pl.multiple_of(32 * (chan ^ m), 32), 32), :] = part
    faces[:, :FACE], faces[:, FACE:] = by_side(near_ref[:32, :], far_ref[:32, :])

    for j in range(9):
        for group, d in ((0, 0), (1, 2)):
            k = 3 * j + d
            row = rule_ref[k : k + 1, :]
            got = picked(row, group, (8 + group,), lambda t: faces[:, tile_span(t - 8)])
            dense_ref[32 * k : 32 * k + 32, tile_span(group)] = got.astype(jnp.bfloat16)
    terms[:864, :] = lax.dot_general(
        dense_ref[...], grad_ref[...], (((1,), (1,)), ((), ())),
        preferred_element_type=jnp.float32,
    ) * (1.0 / 256.0)
    terms[864:, :] = jnp.zeros((32, LANES), jnp.float32)
    for q in range(4):
        for odd, target in ((0, keep_ref), (1, send_ref)):
            start = pl.multiple_of(PART * (spot ^ (2 * q + odd)), 8)
            target[PART * q : PART * (q + 1), :] = terms[pl.ds(start, PART), :]


def forward_kernel(dense_ref, weight_ref, near_ref, far_ref, keep_ref, send_ref, sums):
    chan = lax.axis_index("ch")
    sums[...] = lax.dot_general(
        weight_ref[...], dense_ref[...], (((0,), (0,)), ((), ())),
        preferred_element_type=jnp.float32,
    )
    for target, parts in ((keep_ref, (0, 3)), (send_ref, (1, 2))):
        for i, m in enumerate(parts):
            rows = pl.ds(pl.multiple_of(32 * (chan ^ m), 32), 32)
            target[32 * i : 32 * i + 32, :VOX] = sums[rows, :]
    lower, upper = by_side(near_ref[32:, :], far_ref[32:, :])
    send_ref[:32, VOX:] = lower
    send_ref[32:, VOX:] = upper


def middle_kernel(keep_ref, came_ref, near_ref, far_ref, own_ref, send_ref):
    own_ref[...] = keep_ref[:32, :] + came_ref[:32, :VOX]
    send_ref[:, :VOX] = keep_ref[32:, :] + came_ref[32:, :VOX]
    lower, upper = by_side(near_ref[32:, :], far_ref[32:, :])
    send_ref[:, VOX : VOX + FACE] = lower
    send_ref[:, VOX + FACE : VOX + 2 * FACE] = upper
    send_ref[:, VOX + 2 * FACE : VOX + 3 * FACE] = came_ref[:32, VOX:]
    send_ref[:, VOX + 3 * FACE :] = came_ref[32:, VOX:]


def back_terms_kernel(weight_ref, grad_ref, terms_ref):
    terms_ref[...] = jnp.dot(
        weight_ref[...], grad_ref[...], preferred_element_type=jnp.float32
    )


def back_sum(groups, rule_ref, load):
    totals = {}
    for k in range(27):
        row = rule_ref[k : k + 1, :]
        rows = slice(32 * (26 - k), 32 * (26 - k) + 32)
        for group in groups:
            got = picked(row, group, source_tiles(group, k % 3 - 1), lambda t: load(rows, t))
            totals[group] = got if k == 0 else totals[group] + got
    return totals


def back_inner_kernel(groups, terms, rule_ref, *refs):
    totals = back_sum(groups, rule_ref, lambda rows, t: terms[rows, tile_span(t)])
    for group in groups:
        refs[-1][:, tile_span(group)] = totals[group]


def edge_kernel(
    terms, rule_ref, weight_ref, near_ref, far_ref, inner, own_ref, first_ref, second_ref,
    out_ref, grad_ref, faces, products,
):
    chan = lax.axis_index("ch")
    out_ref[...] = (own_ref[...] + second_ref[:, :VOX]).astype(jnp.bfloat16)
    lower, upper = by_side(near_ref[32:, :], far_ref[32:, :])
    pairs = (
        (lower, upper),
        (first_ref[:32, VOX:], first_ref[32:, VOX:]),
        (second_ref[:, VOX : VOX + FACE], second_ref[:, VOX + FACE : VOX + 2 * FACE]),
        (second_ref[:, VOX + 2 * FACE : VOX + 3 * FACE], second_ref[:, VOX + 3 * FACE :]),
    )
    for m, (lower, upper) in zip(ORDER, pairs):
        rows = pl.ds(pl.multiple_of(32 * (chan ^ m), 32), 32)
        faces[rows, :FACE] = lower.astype(jnp.bfloat16)
        faces[rows, FACE:] = upper.astype(jnp.bfloat16)
    products[...] = jnp.dot(
        weight_ref[...], faces[...], preferred_element_type=jnp.float32
    )
    totals = back_sum(
        EDGE, rule_ref,
        lambda rows, t: products[rows, tile_span(t - 8)] if t >= 8 else terms[rows, tile_span(t)],
    )
    for group in range(8):
        values = totals[group] if group in EDGE else inner[:, tile_span(group)]
        grad_ref[:, tile_span(group)] = values.astype(jnp.bfloat16)


def split_sum_kernel(keep_ref, came_ref, *outs):
    for q, out in enumerate(outs):
        rows = slice(PART * q, PART * (q + 1))
        out[...] = keep_ref[rows, :] + came_ref[rows, :]


def sum_kernel(*refs):
    values = [ref[...] for ref in refs[:-1]]
    while len(values) > 1:
        values = [values[i] + values[i + 1] for i in range(0, len(values), 2)]
    refs[-1][...] = values[0]


def join_kernel(*refs):
    size = refs[0].shape[0]
    for q, ref in enumerate(refs[:-1]):
        refs[-1][size * q : size * (q + 1), :] = ref[...]


def place_kernel(even_ref, odd_ref, out_ref):
    spot = own_part()
    short = 864 - 7 * PART
    for q in range(4):
        for odd, ref in enumerate((even_ref, odd_ref)):
            part = spot ^ (2 * q + odd)
            start = pl.multiple_of(PART * part, 8)
            out_ref[pl.ds(start, short), :] = ref[PART * q : PART * q + short, :]

            @pl.when(part < 7)
            def _():
                rows = pl.ds(pl.multiple_of(start + short, 8), PART - short)
                out_ref[rows, :] = ref[PART * q + short : PART * (q + 1), :]


def call(kernel, outs, args, scratch=(), aliases=None, flops=0, name=None):
    moved = sum(a.size * a.dtype.itemsize for a in list(args) + jax.tree.leaves(outs))
    return pl.pallas_call(
        kernel,
        out_shape=outs,
        in_specs=[VMEM] * len(args),
        out_specs=jax.tree.map(lambda _: VMEM, outs),
        scratch_shapes=list(scratch),
        input_output_aliases=aliases or {},
        compiler_params=pltpu.CompilerParams(vmem_limit_bytes=40 << 20),
        cost_estimate=pl.CostEstimate(flops=flops, bytes_accessed=moved, transcendentals=0),
        name=name,
    )(*args)


def f32(*shape):
    return jax.ShapeDtypeStruct(shape, jnp.float32)


def bf16(*shape):
    return jax.ShapeDtypeStruct(shape, jnp.bfloat16)


def swap(value, mask):
    count = lax.axis_size("blk")
    return lax.ppermute(value, "blk", [(i, i ^ mask) for i in range(count)])


def swap_far(value):
    count = lax.axis_size("blk")
    pairs = [(i, (i + 1 if i % 2 else i - 1) % count) for i in range(count)]
    return lax.ppermute(value, "blk", pairs)


def after(values, *others):
    return lax.optimization_barrier((*values, *others))[: len(values)]


def per_device(features, weight, grad_out, rulebook):
    weights = weight.reshape(864, 128)

    def over_ch(value, mask):
        return lax.ppermute(value, "ch", [(i, i ^ mask) for i in range(4)])

    x, g, rules = features, grad_out, rulebook
    cut = pl.BlockSpec((32, 2 * FACE), lambda i: (0, 0))
    face = pl.BlockSpec((64, FACE), lambda i: (0, 0))
    near, far = pl.pallas_call(
        faces_kernel, out_shape=(bf16(64, FACE),) * 2, grid=(1,),
        in_specs=[cut, cut], out_specs=(face, face),
        compiler_params=pltpu.CompilerParams(vmem_limit_bytes=56 << 20),
        cost_estimate=pl.CostEstimate(flops=1 << 30, bytes_accessed=1 << 16, transcendentals=0),
        name="faces",
    )(x, g)
    pair = call(join_kernel, bf16(64, VOX), (g, over_ch(g, 1)), name="join")
    near = swap(near, 1)
    far = swap_far(far)
    other = over_ch(pair, 3)
    dense = call(
        gather_kernel, bf16(864, VOX), (x, rules),
        [pltpu.VMEM((32, VOX), jnp.float32)], flops=3 << 30, name="gather",
    )
    dense, grads, keep, send = call(
        weight_kernel,
        (bf16(864, VOX), bf16(128, VOX), f32(4 * PART, 128), f32(4 * PART, 128)),
        (dense, rules, near, far, pair, other),
        [pltpu.VMEM((32, 2 * FACE), jnp.float32), pltpu.VMEM((8 * PART, 128), jnp.float32)],
        aliases={0: 0}, flops=1 << 30, name="weight_terms",
    )

    def inner_part(groups, inner=None):
        args = (back, rules) if inner is None else (back, rules, inner)
        return call(
            functools.partial(back_inner_kernel, groups), f32(32, VOX), args,
            aliases=None if inner is None else {2: 0}, flops=max(2, len(groups)) << 30,
            name="back_inner",
        )

    came = swap(send, 1)
    ours, first = call(
        forward_kernel, (f32(64, VOX), f32(64, VOX + FACE)), (dense, weights, near, far),
        [pltpu.VMEM((128, VOX), jnp.float32)], flops=1 << 30, name="forward",
    )
    back = call(
        back_terms_kernel, f32(864, VOX), (weights, grads), flops=1 << 30, name="back_terms"
    )
    came, = after((came,), ours, back)
    pieces = call(split_sum_kernel, (f32(PART, 128),) * 4, (keep, came), name="sum_pair")
    others = [swap(pieces[q], m) for q, m in ((3, X1 | Z1), (2, Z1), (1, X1))]
    first, = after((first,), *pieces)
    first = over_ch(first, 1)
    inner = inner_part((2,))
    others = after(others, inner)
    total = call(sum_kernel, f32(PART, 128), (pieces[0], *others), name="sum_four")
    came = swap(total, X3)
    inner, = after((inner,), total)
    inner = inner_part((4, 5, 6), inner)
    came, = after((came,), inner)
    total = call(sum_kernel, f32(PART, 128), (total, came), name="sum_two")
    others = [swap(total, m) for m in (Z3, Z3 ^ Z6, Z6)]
    ours, first = after((ours, first), total)
    own, second = call(
        middle_kernel, (f32(32, VOX), f32(32, VOX + 4 * FACE)), (ours, first, near, far),
        name="middle",
    )
    second = over_ch(second, 3)
    inner = inner_part((7,), inner)
    others = after(others, inner, own)
    total = call(sum_kernel, f32(PART, 128), (total, *others), name="sum_four")
    others = [swap(total, m) for m in (X1, Z1, X1 | Z1)]
    output, grad_features = call(
        edge_kernel, (bf16(32, VOX), bf16(32, VOX)),
        (back, rules, weights, near, far, inner, own, first, second),
        [pltpu.VMEM((128, 2 * FACE), jnp.bfloat16), pltpu.VMEM((864, 2 * FACE), jnp.float32)],
        flops=2 << 30, name="edge",
    )
    others = after(others, output)
    even = call(join_kernel, f32(4 * PART, 128), (total, *others), name="join")
    odd = swap(even, 1)
    weight_grad = call(
        place_kernel, f32(864, 128), (even, odd), name="place",
    )
    return output, grad_features, weight_grad.reshape(27, 32, 128)


def solution(mesh):
    placed = (P("ch", "blk"), P(None, "ch", None), P("ch", "blk"), P(None, "blk"))
    return jax.shard_map(
        per_device,
        mesh=mesh,
        in_specs=placed,
        out_specs=(P("ch", "blk"), P("ch", "blk"), P(None, "ch", None)),
        check_vma=False,
    )
```

```python
import functools

import jax
import jax.numpy as jnp
from jax import lax
from jax.experimental import pallas as pl
from jax.experimental.pallas import tpu as pltpu
from jax.sharding import PartitionSpec as P

VOX = 1024
FACE = 128
LANES = 128
PART = 112
INNER = tuple(range(2, 8))
EDGE = (0, 1, 3)
X1, X3, Z1, Z3, Z6 = 2, 6, 8, 24, 48
ORDER = (0, 1, 3, 2)
VMEM = pl.BlockSpec(memory_space=pltpu.VMEM)


def source_tiles(group, dz):
    if group == 0:
        return {-1: (8,), 0: (0,), 1: INNER}[dz]
    if group == 1:
        return {-1: INNER, 0: (1,), 1: (9,)}[dz]
    return {-1: (0,) + INNER, 0: INNER, 1: (1,) + INNER}[dz]


def picked(row, group, tiles, load):
    span = row[:, LANES * group : LANES * (group + 1)]
    index = jnp.broadcast_to(span, (32, LANES))
    lane = index & (LANES - 1)
    tile = index >> 7
    total = jnp.zeros((32, LANES), jnp.float32)
    for t in tiles:
        values = jnp.take_along_axis(load(t), lane, axis=1, mode="promise_in_bounds")
        total = jnp.where(tile == t, values, total)
    return total


def own_part():
    place = lax.axis_index("blk")
    over_x = (place >> 1) ^ (place >> 2)
    over_z = (place >> 3) ^ (place >> 4) ^ (place >> 5)
    return (place & 1) | ((over_x & 1) << 1) | ((over_z & 1) << 2)


def tile_span(t):
    return slice(LANES * t, LANES * (t + 1))


def faces_kernel(x_ref, g_ref, near_ref, far_ref):
    odd = (lax.axis_index("blk") & 1) == 1
    for rows, ref in ((slice(0, 32), x_ref), (slice(32, 64), g_ref)):
        lowest = ref[:, :FACE].astype(jnp.float32)
        highest = ref[:, FACE : 2 * FACE].astype(jnp.float32)
        near_ref[rows, :] = jnp.where(odd, lowest, highest).astype(jnp.bfloat16)
        far_ref[rows, :] = jnp.where(odd, highest, lowest).astype(jnp.bfloat16)


def by_side(near, far):
    odd = (lax.axis_index("blk") & 1) == 1
    near = near.astype(jnp.float32)
    far = far.astype(jnp.float32)
    return jnp.where(odd, near, far), jnp.where(odd, far, near)


def gather_kernel(x_ref, rule_ref, dense_ref, table):
    table[...] = x_ref[...].astype(jnp.float32)
    for k in range(27):
        row = rule_ref[k : k + 1, :]
        for group in range(8):
            tiles = (group,) if k == 13 else source_tiles(group, k % 3 - 1)
            if tiles[0] >= 8:
                continue
            got = picked(row, group, tiles, lambda t: table[:, tile_span(t)])
            dense_ref[32 * k : 32 * k + 32, tile_span(group)] = got.astype(jnp.bfloat16)


def faces_kernel(x_ref, g_ref, near_ref, far_ref):
    odd = (lax.axis_index("blk") & 1) == 1
    for rows, ref in ((slice(0, 32), x_ref), (slice(32, 64), g_ref)):
        lowest = ref[:, :FACE].astype(jnp.float32)
        highest = ref[:, FACE : 2 * FACE].astype(jnp.float32)
        near_ref[rows, :] = jnp.where(odd, lowest, highest).astype(jnp.bfloat16)
        far_ref[rows, :] = jnp.where(odd, highest, lowest).astype(jnp.bfloat16)


def by_side(near, far):
    odd = (lax.axis_index("blk") & 1) == 1
    near = near.astype(jnp.float32)
    far = far.astype(jnp.float32)
    return jnp.where(odd, near, far), jnp.where(odd, far, near)


def gather_kernel(x_ref, rule_ref, dense_ref, table):
    table[...] = x_ref[...].astype(jnp.float32)

    def step(j, carry):
        for d in range(3):
            k = 3 * j + d
            row = rule_ref[pl.ds(k, 1), :]
            for group in range(8):
                tiles = source_tiles(group, d - 1)
                if tiles[0] >= 8:
                    continue
                got = picked(row, group, tiles, lambda t: table[:, tile_span(t)])
                rows = pl.ds(pl.multiple_of(32 * k, 32), 32)
                dense_ref[rows, tile_span(group)] = got.astype(jnp.bfloat16)
        return carry

    lax.fori_loop(0, 9, step, 0)


def weight_kernel(
    dense_in, rule_ref, near_ref, far_ref, pair_ref, other_ref,
    dense_ref, grad_ref, keep_ref, send_ref, faces, terms,
):
    chan = lax.axis_index("ch")
    spot = own_part()
    for i, m in enumerate(ORDER):
        part = (pair_ref if i < 2 else other_ref)[32 * (i % 2) : 32 * (i % 2) + 32, :]
        grad_ref[pl.ds(pl.multiple_of(32 * (chan ^ m), 32), 32), :] = part
    faces[:, :FACE], faces[:, FACE:] = by_side(near_ref[:32, :], far_ref[:32, :])

    for j in range(9):
        for group, d in ((0, 0), (1, 2)):
            k = 3 * j + d
            row = rule_ref[k : k + 1, :]
            got = picked(row, group, (8 + group,), lambda t: faces[:, tile_span(t - 8)])
            dense_ref[32 * k : 32 * k + 32, tile_span(group)] = got.astype(jnp.bfloat16)
    terms[:864, :] = lax.dot_general(
        dense_ref[...], grad_ref[...], (((1,), (1,)), ((), ())),
        preferred_element_type=jnp.float32,
    ) * (1.0 / 256.0)
    terms[864:, :] = jnp.zeros((32, LANES), jnp.float32)
    for q in range(4):
        for odd, target in ((0, keep_ref), (1, send_ref)):
            start = pl.multiple_of(PART * (spot ^ (2 * q + odd)), 8)
            target[PART * q : PART * (q + 1), :] = terms[pl.ds(start, PART), :]


def forward_kernel(dense_ref, weight_ref, near_ref, far_ref, keep_ref, send_ref, sums):
    chan = lax.axis_index("ch")
    sums[...] = lax.dot_general(
        weight_ref[...], dense_ref[...], (((0,), (0,)), ((), ())),
        preferred_element_type=jnp.float32,
    )
    for target, parts in ((keep_ref, (0, 3)), (send_ref, (1, 2))):
        for i, m in enumerate(parts):
            rows = pl.ds(pl.multiple_of(32 * (chan ^ m), 32), 32)
            target[32 * i : 32 * i + 32, :VOX] = sums[rows, :]
    lower, upper = by_side(near_ref[32:, :], far_ref[32:, :])
    send_ref[:32, VOX:] = lower
    send_ref[32:, VOX:] = upper


def middle_kernel(keep_ref, came_ref, near_ref, far_ref, own_ref, send_ref):
    own_ref[...] = keep_ref[:32, :] + came_ref[:32, :VOX]
    send_ref[:, :VOX] = keep_ref[32:, :] + came_ref[32:, :VOX]
    lower, upper = by_side(near_ref[32:, :], far_ref[32:, :])
    send_ref[:, VOX : VOX + FACE] = lower
    send_ref[:, VOX + FACE : VOX + 2 * FACE] = upper
    send_ref[:, VOX + 2 * FACE : VOX + 3 * FACE] = came_ref[:32, VOX:]
    send_ref[:, VOX + 3 * FACE :] = came_ref[32:, VOX:]


def back_terms_kernel(weight_ref, grad_ref, terms_ref):
    terms_ref[...] = jnp.dot(
        weight_ref[...], grad_ref[...], preferred_element_type=jnp.float32
    )


def back_sum(groups, rule_ref, load):
    totals = {}
    for k in range(27):
        row = rule_ref[k : k + 1, :]
        rows = slice(32 * (26 - k), 32 * (26 - k) + 32)
        for group in groups:
            tiles = (group,) if k == 13 else source_tiles(group, k % 3 - 1)
            got = picked(row, group, tiles, lambda t: load(rows, t))
            totals[group] = got if k == 0 else totals[group] + got
    return totals


def back_inner_kernel(groups, terms, rule_ref, *refs):
    totals = back_sum(groups, rule_ref, lambda rows, t: terms[rows, tile_span(t)])
    for group in groups:
        refs[-1][:, tile_span(group)] = totals[group]


def edge_kernel(
    terms, rule_ref, weight_ref, near_ref, far_ref, inner, own_ref, first_ref, second_ref,
    out_ref, grad_ref, faces, products,
):
    chan = lax.axis_index("ch")
    out_ref[...] = (own_ref[...] + second_ref[:, :VOX]).astype(jnp.bfloat16)
    lower, upper = by_side(near_ref[32:, :], far_ref[32:, :])
    pairs = (
        (lower, upper),
        (first_ref[:32, VOX:], first_ref[32:, VOX:]),
        (second_ref[:, VOX : VOX + FACE], second_ref[:, VOX + FACE : VOX + 2 * FACE]),
        (second_ref[:, VOX + 2 * FACE : VOX + 3 * FACE], second_ref[:, VOX + 3 * FACE :]),
    )
    for m, (lower, upper) in zip(ORDER, pairs):
        rows = pl.ds(pl.multiple_of(32 * (chan ^ m), 32), 32)
        faces[rows, :FACE] = lower.astype(jnp.bfloat16)
        faces[rows, FACE:] = upper.astype(jnp.bfloat16)
    products[...] = jnp.dot(
        weight_ref[...], faces[...], preferred_element_type=jnp.float32
    )
    totals = back_sum(
        EDGE, rule_ref,
        lambda rows, t: products[rows, tile_span(t - 8)] if t >= 8 else terms[rows, tile_span(t)],
    )
    for group in range(8):
        values = totals[group] if group in EDGE else inner[:, tile_span(group)]
        grad_ref[:, tile_span(group)] = values.astype(jnp.bfloat16)


def split_sum_kernel(keep_ref, came_ref, *outs):
    for q, out in enumerate(outs):
        rows = slice(PART * q, PART * (q + 1))
        out[...] = keep_ref[rows, :] + came_ref[rows, :]


def sum_kernel(*refs):
    values = [ref[...] for ref in refs[:-1]]
    while len(values) > 1:
        values = [values[i] + values[i + 1] for i in range(0, len(values), 2)]
    refs[-1][...] = values[0]


def join_kernel(*refs):
    size = refs[0].shape[0]
    for q, ref in enumerate(refs[:-1]):
        refs[-1][size * q : size * (q + 1), :] = ref[...]


def place_kernel(even_ref, odd_ref, out_ref):
    spot = own_part()
    short = 864 - 7 * PART
    for q in range(4):
        for odd, ref in enumerate((even_ref, odd_ref)):
            part = spot ^ (2 * q + odd)
            start = pl.multiple_of(PART * part, 8)
            out_ref[pl.ds(start, short), :] = ref[PART * q : PART * q + short, :]

            @pl.when(part < 7)
            def _():
                rows = pl.ds(pl.multiple_of(start + short, 8), PART - short)
                out_ref[rows, :] = ref[PART * q + short : PART * (q + 1), :]


def call(kernel, outs, args, scratch=(), aliases=None, flops=0, name=None):
    moved = sum(a.size * a.dtype.itemsize for a in list(args) + jax.tree.leaves(outs))
    return pl.pallas_call(
        kernel,
        out_shape=outs,
        in_specs=[VMEM] * len(args),
        out_specs=jax.tree.map(lambda _: VMEM, outs),
        scratch_shapes=list(scratch),
        input_output_aliases=aliases or {},
        compiler_params=pltpu.CompilerParams(vmem_limit_bytes=40 << 20),
        cost_estimate=pl.CostEstimate(flops=flops, bytes_accessed=moved, transcendentals=0),
        name=name,
    )(*args)


def f32(*shape):
    return jax.ShapeDtypeStruct(shape, jnp.float32)


def bf16(*shape):
    return jax.ShapeDtypeStruct(shape, jnp.bfloat16)


def swap(value, mask):
    count = lax.axis_size("blk")
    return lax.ppermute(value, "blk", [(i, i ^ mask) for i in range(count)])


def swap_far(value):
    count = lax.axis_size("blk")
    pairs = [(i, (i + 1 if i % 2 else i - 1) % count) for i in range(count)]
    return lax.ppermute(value, "blk", pairs)


def after(values, *others):
    return lax.optimization_barrier((*values, *others))[: len(values)]


def per_device(features, weight, grad_out, rulebook):
    weights = weight.reshape(864, 128)

    def over_ch(value, mask):
        return lax.ppermute(value, "ch", [(i, i ^ mask) for i in range(4)])

    x, g, rules = features, grad_out, rulebook
    cut = pl.BlockSpec((32, 2 * FACE), lambda i: (0, 0))
    face = pl.BlockSpec((64, FACE), lambda i: (0, 0))
    near, far = pl.pallas_call(
        faces_kernel, out_shape=(bf16(64, FACE),) * 2, grid=(1,),
        in_specs=[cut, cut], out_specs=(face, face),
        compiler_params=pltpu.CompilerParams(vmem_limit_bytes=56 << 20),
        cost_estimate=pl.CostEstimate(flops=1 << 30, bytes_accessed=1 << 16, transcendentals=0),
        name="faces",
    )(x, g)
    pair = call(join_kernel, bf16(64, VOX), (g, over_ch(g, 1)), name="join")
    near = swap(near, 1)
    far = swap_far(far)
    other = over_ch(pair, 3)
    dense = call(
        gather_kernel, bf16(864, VOX), (x, rules),
        [pltpu.VMEM((32, VOX), jnp.float32)], flops=3 << 30, name="gather",
    )
    dense, grads, keep, send = call(
        weight_kernel,
        (bf16(864, VOX), bf16(128, VOX), f32(4 * PART, 128), f32(4 * PART, 128)),
        (dense, rules, near, far, pair, other),
        [pltpu.VMEM((32, 2 * FACE), jnp.float32), pltpu.VMEM((8 * PART, 128), jnp.float32)],
        aliases={0: 0}, flops=1 << 30, name="weight_terms",
    )

    def inner_part(groups, inner=None):
        args = (back, rules) if inner is None else (back, rules, inner)
        return call(
            functools.partial(back_inner_kernel, groups), f32(32, VOX), args,
            aliases=None if inner is None else {2: 0}, flops=max(2, len(groups)) << 30,
            name="back_inner",
        )

    came = swap(send, 1)
    ours, first = call(
        forward_kernel, (f32(64, VOX), f32(64, VOX + FACE)), (dense, weights, near, far),
        [pltpu.VMEM((128, VOX), jnp.float32)], flops=1 << 30, name="forward",
    )
    back = call(
        back_terms_kernel, f32(864, VOX), (weights, grads), flops=1 << 30, name="back_terms"
    )
    came, = after((came,), ours, back)
    pieces = call(split_sum_kernel, (f32(PART, 128),) * 4, (keep, came), name="sum_pair")
    others = [swap(pieces[q], m) for q, m in ((3, X1 | Z1), (2, Z1), (1, X1))]
    first, = after((first,), *pieces)
    first = over_ch(first, 1)
    inner = inner_part((2,))
    others = after(others, inner)
    total = call(sum_kernel, f32(PART, 128), (pieces[0], *others), name="sum_four")
    came = swap(total, X3)
    inner, = after((inner,), total)
    inner = inner_part((4, 5, 6), inner)
    came, = after((came,), inner)
    total = call(sum_kernel, f32(PART, 128), (total, came), name="sum_two")
    others = [swap(total, m) for m in (Z3, Z6, Z3 ^ Z6)]
    ours, first = after((ours, first), total)
    own, second = call(
        middle_kernel, (f32(32, VOX), f32(32, VOX + 4 * FACE)), (ours, first, near, far),
        name="middle",
    )
    second = over_ch(second, 3)
    inner = inner_part((7,), inner)
    others = after(others, inner, own)
    total = call(sum_kernel, f32(PART, 128), (total, *others), name="sum_four")
    others = [swap(total, m) for m in (X1, Z1, X1 | Z1)]
    output, grad_features = call(
        edge_kernel, (bf16(32, VOX), bf16(32, VOX)),
        (back, rules, weights, near, far, inner, own, first, second),
        [pltpu.VMEM((128, 2 * FACE), jnp.bfloat16), pltpu.VMEM((864, 2 * FACE), jnp.float32)],
        flops=2 << 30, name="edge",
    )
    others = after(others, output)
    even = call(join_kernel, f32(4 * PART, 128), (total, *others), name="join")
    odd = swap(even, 1)
    weight_grad = call(
        place_kernel, f32(864, 128), (even, odd), name="place",
    )
    return output, grad_features, weight_grad.reshape(27, 32, 128)


def solution(mesh):
    placed = (P("ch", "blk"), P(None, "ch", None), P("ch", "blk"), P(None, "blk"))
    return jax.shard_map(
        per_device,
        mesh=mesh,
        in_specs=placed,
        out_specs=(P("ch", "blk"), P("ch", "blk"), P(None, "ch", None)),
        check_vma=False,
    )
```
